32 devices in a mesh: dp: 8 (over y, x, core), fsdp: 4 (over z).
Axes of the slice: x: 2, y: 2, z: 4, core: 2. Of those that a mesh axis runs over, the one named last changes fastest.
Arguments:
- inputs: bfloat16 [32, 512, 1024], P(('dp', 'fsdp')), may hold values from -6 to 6
- segment_ids: int32 [32, 512], P(('dp', 'fsdp')), may hold values from 0 to 6, as said below
- query_weight: bfloat16 [1024, 1024], P(('dp', 'fsdp')), may hold values from -0.1875 to 0.1875
- key_weight: bfloat16 [1024, 1024], P(('dp', 'fsdp')), may hold values from -0.1875 to 0.1875
- value_weight: bfloat16 [1024, 1024], P(('dp', 'fsdp')), may hold values from -0.1875 to 0.1875
- output_weight: bfloat16 [1024, 1024], P(('dp', 'fsdp')), may hold values from -1 to 1
- query_bias: bfloat16 [1024], P(('dp', 'fsdp')), may hold values from -3 to 3
- value_bias: bfloat16 [1024], P(('dp', 'fsdp')), may hold values from -3 to 3
- output_bias: bfloat16 [1024], P(('dp', 'fsdp')), may hold values from -3 to 3
- attn_gain: bfloat16 [1024], P(('dp', 'fsdp')), may hold values from 0.5 to 1.5
- attn_shift: bfloat16 [1024], P(('dp', 'fsdp')), may hold values from -2 to 2
- inner_weight: bfloat16 [1024, 4096], P(('dp', 'fsdp')), may hold values from -0.1875 to 0.1875
- inner_bias: bfloat16 [4096], P(('dp', 'fsdp')), may hold values from -3 to 3
- outer_weight: bfloat16 [4096, 1024], P(('dp', 'fsdp')), may hold values from -0.125 to 0.125
- outer_bias: bfloat16 [1024], P(('dp', 'fsdp')), may hold values from -3 to 3
- ffn_gain: bfloat16 [1024], P(('dp', 'fsdp')), may hold values from 0.5 to 1.5
- ffn_shift: bfloat16 [1024], P(('dp', 'fsdp')), may hold values from -2 to 2
- out_grad: bfloat16 [32, 512, 1024], P(('dp', 'fsdp')), may hold values from -6 to 6
Outputs:
- outputs: bfloat16 [32, 512, 1024], P(('dp', 'fsdp'))
- input_grad: float32 [32, 512, 1024], P(('dp', 'fsdp'))
- grad_query_weight: float32 [1024, 1024], P(('dp', 'fsdp'))
- grad_key_weight: float32 [1024, 1024], P(('dp', 'fsdp'))
- grad_value_weight: float32 [1024, 1024], P(('dp', 'fsdp'))
- grad_output_weight: float32 [1024, 1024], P(('dp', 'fsdp'))
- grad_query_bias: float32 [1024], P(('dp', 'fsdp'))
- grad_value_bias: float32 [1024], P(('dp', 'fsdp'))
- grad_output_bias: float32 [1024], P(('dp', 'fsdp'))
- grad_attn_gain: float32 [1024], P(('dp', 'fsdp'))
- grad_attn_shift: float32 [1024], P(('dp', 'fsdp'))
- grad_inner_weight: float32 [1024, 4096], P(('dp', 'fsdp'))
- grad_inner_bias: float32 [4096], P(('dp', 'fsdp'))
- grad_outer_weight: float32 [4096, 1024], P(('dp', 'fsdp'))
- grad_outer_bias: float32 [1024], P(('dp', 'fsdp'))
- grad_ffn_gain: float32 [1024], P(('dp', 'fsdp'))
- grad_ffn_shift: float32 [1024], P(('dp', 'fsdp'))
The draws below stay inside these ranges and needn't reach their ends.
Inputs may be any that keep to these rules, and one draw needn't show every extreme that they name: `segment_ids`: in each row the document numbers start at 1, never fall and rise by one at each new document, up to 6 documents; padding (0) is a tail of at most 128 positions.
All inputs are finite; a program needn't handle non-finite values.
Results may differ from the reference program's by a relative error of at most 0.014.
Values may be sent and summed in bfloat16 or wider, within the bound.
No kernel may reach another device: no remote copies, remote signals or barrier semaphores. Data moves between devices by JAX's collectives and lax.ppermute only.
A program may use at most 256 MiB of HBM per device.

```python
import math
from functools import partial
import jax
import jax.numpy as jnp
from jax import lax

D = 1024
H = 16
HD = 64
FF = 4096
SEQ = 512
DOCS = 6
ROWS = 32


def draw_segment_ids(key, part):
    key_docs, key_pad, key_cuts = jax.random.split(jax.random.fold_in(key, 17), 3)
    doc_count = jax.random.randint(key_docs, (ROWS,), 1, DOCS + 1)
    doc_count = doc_count.at[0].set(DOCS)
    pad_count = jax.random.randint(key_pad, (ROWS,), 0, SEQ // 4 + 1)
    pad_count = pad_count.at[0].set(0)
    pad_count = pad_count.at[ROWS - 1].set(SEQ // 4)
    row_keys = jax.random.split(key_cuts, ROWS)
    shuffled = jax.vmap(lambda row_key: jax.random.permutation(row_key, SEQ - 1))(row_keys) + 1
    cut_points = shuffled[:, :DOCS - 1]
    cut_live = jnp.arange(DOCS - 1)[None, :] < (doc_count - 1)[:, None]
    positions = jnp.arange(SEQ)
    cut_count = jnp.sum((cut_points[:, None, :] <= positions[None, :, None]) & cut_live[:, None, :], axis=2)
    segments = 1 + cut_count
    segments = jnp.where(positions[None, :] < SEQ - pad_count[:, None], segments, 0)
    return segments.astype(jnp.int32)


def block_scale(key, shape, pieces, smallest, high):
    factor_of, own = 1.0, jax.random.fold_in(key, 6)
    for position, shards_of in pieces:
        draws = jnp.exp(jax.random.uniform(jax.random.fold_in(own, position), (shards_of,), jnp.float32, smallest / len(pieces), high / len(pieces)))
        factor_of = factor_of * jnp.repeat(draws, shape[position] // shards_of).reshape([-1 if axis == position else 1 for axis in range(len(shape))])
    return factor_of


def normal_values(own_key, extent, width, most, pieces=(), dtype=jnp.bfloat16):
    result = jax.random.normal(own_key, extent, jnp.float32) * width
    if len(pieces) > 0:
        result = block_scale(own_key, extent, pieces, -0.22, 0.18) * result
    return jnp.clip(result, min=-most, max=most).astype(dtype)


def setup_inputs(seed: int = 0) -> dict:
    streams_of = jax.random.split(jax.random.key(seed), 19)
    inputs = normal_values(streams_of[0], (ROWS, SEQ, D), 1.0, 6.0, ((0, 32),))
    segment_ids = draw_segment_ids(jax.random.fold_in(streams_of[18], 71), 0)
    query_weight = normal_values(streams_of[2], (D, D), D ** -0.5, 0.1875, ((0, 32),))
    key_weight = normal_values(streams_of[3], (D, D), D ** -0.5, 0.1875, ((0, 32),))
    value_weight = normal_values(streams_of[4], (D, D), D ** -0.5, 0.1875, ((0, 32),))
    output_weight = normal_values(streams_of[5], (D, D), (D // 32) ** -0.5, 1.0, ((0, 32),))
    query_bias = normal_values(streams_of[6], (D,), 0.5, 3.0, ((0, 32),))
    value_bias = normal_values(streams_of[7], (D,), 0.5, 3.0, ((0, 32),))
    output_bias = normal_values(streams_of[8], (D,), 0.5, 3.0, ((0, 32),))
    attn_gain = jnp.clip(1.0 + 0.1 * jax.random.normal(streams_of[9], (D,), jnp.float32), 0.5, 1.5).astype(jnp.bfloat16)
    attn_shift = normal_values(streams_of[10], (D,), 0.3, 2.0, ((0, 32),))
    inner_weight = normal_values(streams_of[11], (D, FF), D ** -0.5, 0.1875, ((0, 32),))
    inner_bias = normal_values(streams_of[12], (FF,), 0.5, 3.0, ((0, 32),))
    outer_weight = normal_values(streams_of[13], (FF, D), (FF // 2) ** -0.5, 0.125, ((0, 32),))
    outer_bias = normal_values(streams_of[14], (D,), 0.5, 3.0, ((0, 32),))
    ffn_gain = jnp.clip(1.0 + 0.1 * jax.random.normal(streams_of[15], (D,), jnp.float32), 0.5, 1.5).astype(jnp.bfloat16)
    ffn_shift = normal_values(streams_of[16], (D,), 0.3, 2.0, ((0, 32),))
    out_grad = normal_values(streams_of[17], (ROWS, SEQ, D), 1.0, 6.0, ((0, 32),))
    return dict(inputs=inputs, segment_ids=segment_ids, query_weight=query_weight, key_weight=key_weight, value_weight=value_weight, output_weight=output_weight, query_bias=query_bias, value_bias=value_bias, output_bias=output_bias, attn_gain=attn_gain, attn_shift=attn_shift, inner_weight=inner_weight, inner_bias=inner_bias, outer_weight=outer_weight, outer_bias=outer_bias, ffn_gain=ffn_gain, ffn_shift=ffn_shift, out_grad=out_grad)


EPSILON = 1e-05

@jax.custom_vjp
def low(v):
    return lax.optimization_barrier(v.astype(jnp.bfloat16)).astype(jnp.float32)

@jax.custom_vjp
def low_back(v):
    return v

def low_keep(v):
    return (low(v), None)

def low_pass(kept, grad):
    return (grad,)

def back_keep(v):
    return (v, None)

def back_low(kept, grad):
    return (low(grad),)
low.defvjp(low_keep, low_pass)
low_back.defvjp(back_keep, back_low)

def project(hidden, matrix):
    return jnp.einsum('bld,de->ble', hidden, matrix, precision=lax.Precision.HIGHEST)

def layer_norm(rows_in, gain, shift):
    row_mean = lax.optimization_barrier(jnp.mean(rows_in, axis=-1, keepdims=True))
    centred = rows_in - row_mean
    spread = lax.optimization_barrier(jnp.mean(centred * centred, axis=-1, keepdims=True))
    return centred * lax.rsqrt(spread + EPSILON) * gain + shift

def layer(params, hidden, seg_rows):
    query_weight, key_weight, value_weight, output_weight, query_bias, value_bias, output_bias, attn_gain, attn_shift, inner_weight, inner_bias, outer_weight, outer_bias, ffn_gain, ffn_shift = params
    batch_rows, seq_len, model_width = hidden.shape
    highest = lax.Precision.HIGHEST
    queries = low(low_back(project(hidden, query_weight) + query_bias))
    key_rows = low(low_back(project(hidden, key_weight)))
    value_rows = low(low_back(project(hidden, value_weight) + value_bias))
    shape_heads = (batch_rows, seq_len, H, HD)
    scores = jnp.einsum('bqhd,bkhd->bhqk', queries.reshape(shape_heads), key_rows.reshape(shape_heads), precision=highest) * HD ** (-0.5)
    scores = low_back(scores)
    same_doc = seg_rows[:, None, :, None] == seg_rows[:, None, None, :]
    scores = jnp.where(same_doc, scores, -1e+30)
    weights_soft = low(jax.nn.softmax(scores, axis=-1))
    mixed = jnp.einsum('bhqk,bkhd->bqhd', weights_soft, value_rows.reshape(shape_heads), precision=highest).reshape(batch_rows, seq_len, model_width)
    mixed = low(low_back(mixed))
    attn_branch = low_back(project(mixed, output_weight) + output_bias)
    attn_normed = layer_norm(hidden + attn_branch, attn_gain, attn_shift)
    inner_pre = low_back(project(low(attn_normed), inner_weight) + inner_bias)
    inner_act = jax.nn.gelu(inner_pre, approximate=False)
    ffn_branch = low_back(project(low(inner_act), outer_weight) + outer_bias)
    return layer_norm(attn_normed + ffn_branch, ffn_gain, ffn_shift)

def reference(inputs, segment_ids, query_weight, key_weight, value_weight, output_weight, query_bias, value_bias, output_bias, attn_gain, attn_shift, inner_weight, inner_bias, outer_weight, outer_bias, ffn_gain, ffn_shift, out_grad):
    params = (query_weight.astype(jnp.float32), key_weight.astype(jnp.float32), value_weight.astype(jnp.float32), output_weight.astype(jnp.float32), query_bias.astype(jnp.float32), value_bias.astype(jnp.float32), output_bias.astype(jnp.float32), attn_gain.astype(jnp.float32), attn_shift.astype(jnp.float32), inner_weight.astype(jnp.float32), inner_bias.astype(jnp.float32), outer_weight.astype(jnp.float32), outer_bias.astype(jnp.float32), ffn_gain.astype(jnp.float32), ffn_shift.astype(jnp.float32))
    hidden_all = inputs.astype(jnp.float32)
    group_rows = math.gcd(ROWS, max(1, 4096 // SEQ))
    blocks = ROWS // group_rows

    def run(params_in, hidden_in):
        block_fn = jax.checkpoint(partial(layer, params_in))

        def scan_step(carry, item_pair):
            return (carry, block_fn(item_pair[0], item_pair[1]))
        _, layer_outs = lax.scan(scan_step, jnp.zeros((), jnp.float32), (hidden_in.reshape(blocks, group_rows, SEQ, D), segment_ids.reshape(blocks, group_rows, SEQ)))
        return layer_outs.reshape(ROWS, SEQ, D)
    outputs, pullback = jax.vjp(run, params, hidden_all)
    grads, input_grad = pullback(out_grad.astype(jnp.float32))
    return (outputs.astype(jnp.bfloat16), input_grad, grads[0], grads[1], grads[2], grads[3], grads[4], grads[5], grads[6], grads[7], grads[8], grads[9], grads[10], grads[11], grads[12], grads[13], grads[14])
```

```python
import functools

import jax
import jax.numpy as jnp
from jax import lax
from jax.experimental import pallas as pl
from jax.experimental.pallas import tpu as pltpu
from jax.sharding import PartitionSpec as P

H = 16
HD = 64


EPSILON = 1e-05


def scaled_norm(rows_in, gain):
    row_mean = jnp.mean(rows_in, axis=-1, keepdims=True)
    centred = rows_in - row_mean
    spread = jnp.mean(centred * centred, axis=-1, keepdims=True)
    return centred * lax.rsqrt(spread + EPSILON) * gain


def gelu_exact(value_in):
    return jax.nn.gelu(value_in, approximate=False)


def to_groups(matrix, row_count, seq_len):
    groups = H // 4
    shaped = matrix.reshape(row_count, seq_len, groups, 4, HD).transpose(0, 2, 1, 3, 4)
    return shaped.reshape(row_count * groups, seq_len, 4, HD)


def from_groups(stacked, row_count, seq_len):
    groups = stacked.shape[0] // row_count
    shaped = stacked.reshape(row_count, groups, seq_len, 4, HD).transpose(0, 2, 1, 3, 4)
    return shaped.reshape(row_count * seq_len, groups * 4 * HD)


def masked_scores(query_block, key_block, seg_row):
    score_scale = HD ** (-0.5)
    scores = (
        jnp.einsum("qhd,khd->hqk", query_block, key_block, preferred_element_type=jnp.float32)
        * score_scale
    )
    same_doc = seg_row[:, None] == seg_row[None, :]
    return jnp.where(same_doc[None], scores, -1e30)


def attend_forward(item_set):
    query_block, key_block, value_block, seg_row = item_set
    scores = masked_scores(query_block, key_block, seg_row)
    row_max = jnp.max(scores, axis=-1, keepdims=True)
    raised = jnp.exp(scores - row_max)
    row_total = jnp.sum(raised, axis=-1, keepdims=True)
    prob_low = (raised / row_total).astype(jnp.bfloat16)
    mixed_block = jnp.einsum(
        "hqk,khd->qhd", prob_low, value_block, preferred_element_type=jnp.float32
    )
    return (mixed_block, (row_max + jnp.log(row_total))[..., 0])


def attend_backward(item_set):
    query_block, key_block, value_block, seg_row, mixed_grad, log_total = item_set
    score_scale = HD ** (-0.5)
    scores = masked_scores(query_block, key_block, seg_row)
    probabilities = jnp.exp(scores - log_total[..., None])
    prob_low = probabilities.astype(jnp.bfloat16)
    value_grad = jnp.einsum(
        "hqk,qhd->khd", prob_low, mixed_grad, preferred_element_type=jnp.float32
    )
    prob_grad = jnp.einsum(
        "qhd,khd->hqk", mixed_grad, value_block, preferred_element_type=jnp.float32
    )
    inner_sum = jnp.sum(probabilities * prob_grad, axis=-1, keepdims=True)
    score_grad = (probabilities * (prob_grad - inner_sum)).astype(jnp.bfloat16)
    query_grad = (
        jnp.einsum("hqk,khd->qhd", score_grad, key_block, preferred_element_type=jnp.float32)
        * score_scale
    )
    key_grad = (
        jnp.einsum("hqk,qhd->khd", score_grad, query_block, preferred_element_type=jnp.float32)
        * score_scale
    )
    return (query_grad, key_grad, value_grad)


def matmul(left, right):
    return jnp.dot(left, right, preferred_element_type=jnp.float32)


def column_sum(matrix):
    return jnp.sum(matrix.astype(jnp.float32), axis=0)


AXES = ("dp", "fsdp")
BF = jnp.bfloat16
F32 = jnp.float32


class Slice:
    def __init__(self, dp, inner):
        self.inner, self.chips, self.count = inner, dp // 2, dp * inner

    def swap(self, value, mask):
        pairs = [(i, i ^ mask) for i in range(self.count)]
        return lax.ppermute(value, AXES, pairs)

    def across_core(self, value):
        return self.swap(value, self.inner)

    def across_chip(self, value, hop):
        return self.swap(value, hop * 2 * self.inner)

    def place(self):
        me = lax.axis_index(AXES)
        z = me % self.inner
        core = (me // self.inner) % 2
        return me, jnp.stack([me // (2 * self.inner), core, z]).astype(jnp.int32)


def gather_pieces(net, shard):
    along_z = jnp.stack([shard] + [net.swap(shard, s) for s in range(1, net.inner)])
    pieces = [(along_z, 0, 0, 0)]
    if net.chips == 4:
        half = net.inner // 2
        first, second = net.across_chip(along_z, 1), net.across_chip(along_z, 2)
        low = net.across_chip(first[:half], 2)
        high = net.across_chip(second[half:], 1)
        pieces += [(first, 1, 0, 0), (second, 2, 0, 0), (low, 3, 0, 0), (high, 3, 0, half)]
    else:
        pieces += [(net.across_chip(along_z, j), j, 0, 0) for j in range(1, net.chips)]
    return pieces + [(net.across_core(p), j, 1, s) for p, j, _, s in pieces]


def assemble(net, pieces, ids, me, parts, tile):
    rows = pieces[0][0].shape[1]
    total = net.count * rows
    if rows % 16:
        hops = []
        for _, j, c, s in pieces:
            hops.append((j * 2 + c) * net.inner + s)
        order = {}
        start = 0
        for (p, j, c, s), hop in zip(pieces, hops):
            for i in range(p.shape[0]):
                order[hop + i] = start + i
            start += p.shape[0]
        stacked = jnp.concatenate([p for p, _, _, _ in pieces], axis=0)
        stacked = jnp.stack([stacked[order[i]] for i in range(net.count)])
        whole = jnp.take(stacked, jnp.arange(net.count) ^ me, axis=0)
        whole = whole.reshape(total, -1)
        return [whole[:, a : a + w] for a, w in parts]
    first = [a // tile for a, _ in parts]
    count = [w // tile for _, w in parts]
    steps = sum(count)
    base = [sum(count[:i]) for i in range(len(parts))]
    start = first[0]
    meta = [(p.shape[0], j, c, s) for p, j, c, s in pieces]

    def body(ids_ref, *refs):
        sources, sinks = refs[: len(meta)], refs[len(meta) :]
        step = pl.program_id(0)
        for sink, lo, n in zip(sinks, base, count):

            @pl.when((step >= lo) & (step < lo + n))
            def _():
                for source, (depth, j, c, s) in zip(sources, meta):
                    block = ((ids_ref[0] ^ j) * 2 + (ids_ref[1] ^ c)) * net.inner
                    for i in range(depth):
                        row = (block + (ids_ref[2] ^ (s + i))) * rows
                        sink[pl.ds(pl.multiple_of(row, rows), rows), :] = source[i]

    return pl.pallas_call(
        body,
        out_shape=[jax.ShapeDtypeStruct((total, w), BF) for _, w in parts],
        grid_spec=pltpu.PrefetchScalarGridSpec(
            num_scalar_prefetch=1,
            grid=(steps,),
            in_specs=[
                pl.BlockSpec((depth, rows, tile), lambda n, ids: (0, 0, start + n))
                for depth, _, _, _ in meta
            ],
            out_specs=[
                pl.BlockSpec(
                    (total, tile),
                    lambda n, ids, lo=lo, c=c: (0, jnp.clip(n - lo, 0, c - 1)),
                )
                for lo, c in zip(base, count)
            ],
        ),
        name="assemble",
    )(ids, *[p for p, _, _, _ in pieces])


def column_blocks(net, left, ids, order, core):
    width = left.shape[1] // (net.chips * 2)
    picked = []
    for j in order:
        at = ((ids[0] ^ j) * 2 + (ids[1] ^ core)) * width
        picked.append(lax.dynamic_slice_in_dim(left, at, width, axis=1))
    return picked[0] if len(picked) == 1 else jnp.concatenate(picked, axis=1)


def outer_dot(left, right):
    return jnp.einsum("tm,tn->mn", left, right, preferred_element_type=F32)


def hop_orders(net, backwards):
    bits = [1 << b for b in range(net.chips.bit_length() - 1)]
    return bits[::-1] if backwards else bits


def reduce_rows(net, left, right, ids, backwards):
    bits = hop_orders(net, backwards)
    held = list(range(net.chips))
    order = [0]
    for b in bits[::-1]:
        order = order + [j ^ b for j in order]
    width = left.shape[1] // (net.chips * 2)
    sent = outer_dot(column_blocks(net, left, ids, order, 1), right).astype(BF)
    got = net.across_core(sent)
    half = len(order) // 2
    if half == 0:
        keep = outer_dot(column_blocks(net, left, ids, order, 0), right) + got.astype(F32)
    else:
        away = (
            outer_dot(column_blocks(net, left, ids, order[half:], 0), right)
            + got[half * width :].astype(F32)
        ).astype(BF)
        arrived = net.across_chip(away, bits[0])
        keep = (
            outer_dot(column_blocks(net, left, ids, order[:half], 0), right)
            + got[: half * width].astype(F32)
        ).astype(BF)
        keep = keep.astype(F32) + arrived.astype(F32)
        for b in bits[1:]:
            half //= 2
            away = keep[half * width :].astype(BF)
            arrived = net.across_chip(away, b)
            keep = keep[: half * width].astype(BF).astype(F32) + arrived.astype(F32)
    blocks = keep.reshape(net.inner, width // net.inner, -1)
    total = lax.dynamic_index_in_dim(blocks, ids[2], axis=0, keepdims=False)
    for s in range(1, net.inner):
        piece = lax.dynamic_index_in_dim(blocks, ids[2] ^ s, axis=0, keepdims=False)
        total = total + net.swap(piece.astype(BF), s).astype(F32)
    return total


def reduce_vectors(net, vectors):
    packed = jnp.concatenate([v.reshape(net.count, -1) for v in vectors], axis=1)
    summed = jnp.sum(lax.all_to_all(packed, AXES, 0, 0, tiled=True), axis=0)
    out, at = [], 0
    for v in vectors:
        n = v.shape[0] // net.count
        out.append(summed[at : at + n])
        at += n
    return out


def shards(
    net,
    inputs,
    segment_ids,
    query_weight,
    key_weight,
    value_weight,
    output_weight,
    query_bias,
    value_bias,
    output_bias,
    attn_gain,
    attn_shift,
    inner_weight,
    inner_bias,
    outer_weight,
    outer_bias,
    ffn_gain,
    ffn_shift,
    out_grad,
):
    row_count, seq_len, model_width = inputs.shape
    tokens_here = row_count * seq_len
    flattened = inputs.reshape(tokens_here, model_width)
    me, ids = net.place()
    own_rows = query_weight.shape[0]
    small = [query_bias, value_bias, output_bias, attn_gain, attn_shift, outer_bias, ffn_gain, ffn_shift]
    small = jnp.concatenate([jnp.stack(small, axis=1), inner_bias.reshape(own_rows, -1)], axis=1)
    spare = 128 - small.shape[1]
    small = jnp.pad(small, ((0, 0), (0, spare)))
    first = gather_pieces(
        net, jnp.concatenate([query_weight, key_weight, value_weight, small], axis=1)
    )
    second = gather_pieces(net, jnp.concatenate([output_weight, inner_weight], axis=1))
    third = gather_pieces(net, outer_weight)
    width = query_weight.shape[1]
    wide = inner_weight.shape[1]
    query_full, key_full, value_full = assemble(
        net, first, ids, me, [(0, width), (width, width), (2 * width, width)], width
    )
    (small_full,) = assemble(net, first, ids, me, [(3 * width, 128)], 128)
    lanes = small_full[:, :8].astype(jnp.float32).T
    (
        query_bias_full,
        value_bias_full,
        output_bias_full,
        attn_gain_full,
        attn_shift_full,
        outer_bias_full,
        ffn_gain_full,
        ffn_shift_full,
    ) = [lanes[i] for i in range(8)]
    inner_bias_full = small_full[:, 8 : 8 + wide // width].astype(jnp.float32).reshape(-1)
    output_full, inner_full = assemble(
        net, second, ids, me, [(0, width), (width, wide)], width
    )
    (outer_full,) = assemble(net, third, ids, me, [(0, width)], min(width, 512))
    inner_back, outer_back, ffn_gain_back = inner_full, outer_full, ffn_gain_full
    query_back, key_back, value_back, output_back, attn_gain_back = (
        query_full,
        key_full,
        value_full,
        output_full,
        attn_gain_full,
    )
    queries = (matmul(flattened, query_full) + query_bias_full.astype(jnp.float32)).astype(
        jnp.bfloat16
    )
    key_rows = matmul(flattened, key_full).astype(jnp.bfloat16)
    value_rows = (matmul(flattened, value_full) + value_bias_full.astype(jnp.float32)).astype(
        jnp.bfloat16
    )
    query_groups = to_groups(queries, row_count, seq_len)
    key_groups = to_groups(key_rows, row_count, seq_len)
    value_groups = to_groups(value_rows, row_count, seq_len)
    seg_repeat = jnp.repeat(segment_ids, H // 4, axis=0)
    group_mixed, log_totals = lax.map(
        attend_forward, (query_groups, key_groups, value_groups, seg_repeat)
    )
    mixed_low = from_groups(group_mixed, row_count, seq_len).astype(jnp.bfloat16)
    attn_branch = matmul(mixed_low, output_full) + output_bias_full.astype(jnp.float32)
    attn_sum = flattened.astype(jnp.float32) + attn_branch
    attn_normed = scaled_norm(
        attn_sum, attn_gain_full.astype(jnp.float32)
    ) + attn_shift_full.astype(jnp.float32)
    normed_low = attn_normed.astype(jnp.bfloat16)
    inner_pre = matmul(normed_low, inner_full) + inner_bias_full.astype(jnp.float32)
    act_low = gelu_exact(inner_pre).astype(jnp.bfloat16)
    ffn_branch = matmul(act_low, outer_full) + outer_bias_full.astype(jnp.float32)
    ffn_sum = attn_normed + ffn_branch
    outputs = (
        scaled_norm(ffn_sum, ffn_gain_full.astype(jnp.float32)) + ffn_shift_full.astype(jnp.float32)
    ).astype(jnp.bfloat16)
    grad_out = out_grad.reshape(tokens_here, model_width).astype(jnp.float32)
    _, ffn_norm_pull = jax.vjp(scaled_norm, ffn_sum, ffn_gain_back.astype(jnp.float32))
    grad_ffn_sum, grad_ffn_gain = ffn_norm_pull(grad_out)
    grad_ffn_shift = jnp.sum(grad_out, axis=0)
    branch_grad = grad_ffn_sum.astype(jnp.bfloat16)
    grad_outer_bias = column_sum(branch_grad)
    shard_outer = reduce_rows(net, act_low, branch_grad, ids, False)
    grad_act = jnp.einsum("nd,fd->nf", branch_grad, outer_back, preferred_element_type=jnp.float32)
    _, gelu_pull = jax.vjp(gelu_exact, inner_pre)
    inner_grad = gelu_pull(grad_act)[0].astype(jnp.bfloat16)
    grad_inner_bias = column_sum(inner_grad)
    shard_inner = reduce_rows(net, normed_low, inner_grad, ids, True)
    grad_normed = grad_ffn_sum + jnp.einsum(
        "nf,df->nd", inner_grad, inner_back, preferred_element_type=jnp.float32
    )
    _, attn_norm_pull = jax.vjp(scaled_norm, attn_sum, attn_gain_back.astype(jnp.float32))
    grad_attn_sum, grad_attn_gain = attn_norm_pull(grad_normed)
    grad_attn_shift = jnp.sum(grad_normed, axis=0)
    attn_grad = grad_attn_sum.astype(jnp.bfloat16)
    grad_output_bias = column_sum(attn_grad)
    shard_output = reduce_rows(net, mixed_low, attn_grad, ids, False)
    mixed_grad = jnp.einsum(
        "ne,de->nd", attn_grad, output_back, preferred_element_type=jnp.float32
    ).astype(jnp.bfloat16)
    group_qgrad, group_kgrad, group_vgrad = lax.map(
        attend_backward,
        (
            query_groups,
            key_groups,
            value_groups,
            seg_repeat,
            to_groups(mixed_grad, row_count, seq_len),
            log_totals,
        ),
    )
    query_grad = from_groups(group_qgrad, row_count, seq_len).astype(jnp.bfloat16)
    key_grad = from_groups(group_kgrad, row_count, seq_len).astype(jnp.bfloat16)
    value_grad = from_groups(group_vgrad, row_count, seq_len).astype(jnp.bfloat16)
    grad_query_bias = column_sum(query_grad)
    grad_value_bias = column_sum(value_grad)
    middle = key_grad.shape[1] // 2
    shard_low = reduce_rows(
        net, flattened, jnp.concatenate([query_grad, key_grad[:, :middle]], axis=1), ids, False
    )
    shard_high = reduce_rows(
        net, flattened, jnp.concatenate([key_grad[:, middle:], value_grad], axis=1), ids, True
    )
    shard_query = shard_low[:, :model_width]
    shard_key = jnp.concatenate([shard_low[:, model_width:], shard_high[:, :middle]], axis=1)
    shard_value = shard_high[:, middle:]
    input_grad = (
        grad_attn_sum
        + jnp.einsum("ne,de->nd", query_grad, query_back, preferred_element_type=jnp.float32)
        + jnp.einsum("ne,de->nd", key_grad, key_back, preferred_element_type=jnp.float32)
        + jnp.einsum("ne,de->nd", value_grad, value_back, preferred_element_type=jnp.float32)
    )
    (
        shard_query_bias,
        shard_value_bias,
        shard_output_bias,
        shard_attn_gain,
        shard_attn_shift,
        shard_inner_bias,
        shard_outer_bias,
        shard_ffn_gain,
        shard_ffn_shift,
    ) = reduce_vectors(
        net,
        [
            grad_query_bias,
            grad_value_bias,
            grad_output_bias,
            grad_attn_gain,
            grad_attn_shift,
            grad_inner_bias,
            grad_outer_bias,
            grad_ffn_gain,
            grad_ffn_shift,
        ],
    )
    return (
        outputs.reshape(row_count, seq_len, model_width),
        input_grad.reshape(row_count, seq_len, model_width),
        shard_query,
        shard_key,
        shard_value,
        shard_output,
        shard_query_bias,
        shard_value_bias,
        shard_output_bias,
        shard_attn_gain,
        shard_attn_shift,
        shard_inner,
        shard_inner_bias,
        shard_outer,
        shard_outer_bias,
        shard_ffn_gain,
        shard_ffn_shift,
    )


def solution(mesh):
    placed = (
        P(("dp", "fsdp"), None, None),
        P(("dp", "fsdp"), None),
        P(("dp", "fsdp"), None),
        P(("dp", "fsdp"), None),
        P(("dp", "fsdp"), None),
        P(("dp", "fsdp"), None),
        P(("dp", "fsdp")),
        P(("dp", "fsdp")),
        P(("dp", "fsdp")),
        P(("dp", "fsdp")),
        P(("dp", "fsdp")),
        P(("dp", "fsdp"), None),
        P(("dp", "fsdp")),
        P(("dp", "fsdp"), None),
        P(("dp", "fsdp")),
        P(("dp", "fsdp")),
        P(("dp", "fsdp")),
        P(("dp", "fsdp"), None, None),
    )
    return jax.shard_map(
        functools.partial(shards, Slice(mesh.shape["dp"], mesh.shape["fsdp"])),
        mesh=mesh,
        in_specs=placed,
        out_specs=(
            P(("dp", "fsdp"), None, None),
            P(("dp", "fsdp"), None, None),
            P(("dp", "fsdp"), None),
            P(("dp", "fsdp"), None),
            P(("dp", "fsdp"), None),
            P(("dp", "fsdp"), None),
            P(("dp", "fsdp")),
            P(("dp", "fsdp")),
            P(("dp", "fsdp")),
            P(("dp", "fsdp")),
            P(("dp", "fsdp")),
            P(("dp", "fsdp"), None),
            P(("dp", "fsdp")),
            P(("dp", "fsdp"), None),
            P(("dp", "fsdp")),
            P(("dp", "fsdp")),
            P(("dp", "fsdp")),
        ),
        check_vma=False,
    )
```

```python
import functools

import jax
import jax.numpy as jnp
from jax import lax
from jax.experimental import pallas as pl
from jax.experimental.pallas import tpu as pltpu
from jax.sharding import PartitionSpec as P

H = 16
HD = 64
AXES = ("dp", "fsdp")
BF = jnp.bfloat16
F32 = jnp.float32
EPSILON = 1e-05
NT = (((1,), (1,)), ((), ()))
TN = (((0,), (0,)), ((), ()))
MASKED = -1e30
LIGHT = pl.CostEstimate(flops=1, bytes_accessed=1, transcendentals=0)
ANY = pl.BlockSpec(memory_space=pl.ANY)


def whole(shape):
    return pl.BlockSpec(shape, lambda *_: (0,) * len(shape))


def struct(shape, dtype):
    return jax.ShapeDtypeStruct(shape, dtype)


def dot(left, right):
    return jnp.dot(left, right, preferred_element_type=F32)


def dot_tn(left, right):
    return lax.dot_general(left, right, TN, preferred_element_type=F32)


def dot_nt(left, right):
    return lax.dot_general(left, right, NT, preferred_element_type=F32)


def tie(value, *after):
    return lax.optimization_barrier((value, *after))[0]


def normalise(rows):
    centred = rows - jnp.mean(rows, axis=-1, keepdims=True)
    spread = jnp.mean(centred * centred, axis=-1, keepdims=True)
    inverse = lax.rsqrt(spread + EPSILON)
    return centred * inverse, inverse


def normalise_back(cotangent, normed, inverse):
    slope = jnp.mean(cotangent * normed, axis=-1, keepdims=True)
    return inverse * (cotangent - jnp.mean(cotangent, axis=-1, keepdims=True) - normed * slope)


def total_rows(matrix):
    return jnp.sum(matrix, axis=0, keepdims=True)


def lane_half(block, which):
    lane = lax.broadcasted_iota(jnp.int32, block.shape, 1)
    return jnp.where((lane >= HD) == (which == 1), block, jnp.zeros_like(block))


def set_mask(seg_ref, mask_ref):
    seg_row = seg_ref[...].astype(F32)
    seg_col = jnp.broadcast_to(seg_row, (128, seg_row.shape[1])).T
    for at in range(0, seg_row.shape[1], 128):
        same = seg_col == seg_row[:, at : at + 128]
        mask_ref[:, at : at + 128] = jnp.where(same, 0.0, MASKED)


def attend_forward_body(seg_ref, q_ref, k_ref, v_ref, mixed_ref, total_ref, mask_ref):
    @pl.when(pl.program_id(1) == 0)
    def _():
        set_mask(seg_ref, mask_ref)

    query = q_ref[...] * jnp.bfloat16(HD**-0.5)
    key = k_ref[...]
    value_t = v_ref[...].T
    halves = []
    for h in range(2):
        scores = lax.dot_general(lane_half(key, h), query, NT, preferred_element_type=F32)
        scores = scores + mask_ref[...]
        high = jnp.max(scores, axis=0, keepdims=True)
        raised = jnp.exp(scores - high)
        total = jnp.sum(raised, axis=0, keepdims=True)
        low = (raised * (1.0 / total)).astype(BF)
        rows = value_t[h * HD : (h + 1) * HD]
        halves.append(jnp.dot(rows, low, preferred_element_type=F32))
        total_ref[0, h : h + 1, :] = high + jnp.log(total)
    mixed_ref[...] = jnp.concatenate(halves, axis=0).T.astype(BF)


def attend_backward_body(
    seg_ref, q_ref, k_ref, v_ref, g_ref, total_ref, *rest
):
    dq_ref, dk_ref, dv_ref, dq_sum_ref, dv_sum_ref, mask_ref = rest[-6:]

    @pl.when(pl.program_id(1) == 0)
    def _():
        set_mask(seg_ref, mask_ref)

    scale = HD**-0.5
    query = q_ref[...] * jnp.bfloat16(scale)
    key, value, grad = k_ref[...], v_ref[...], g_ref[...]
    key_t = key.T
    lane = lax.broadcasted_iota(jnp.int32, key.shape, 1)
    dq_t, dk, dv = [], None, None
    for h in range(2):
        scores = lax.dot_general(lane_half(key, h), query, NT, preferred_element_type=F32)
        probs = jnp.exp(scores + mask_ref[...] - total_ref[0, h : h + 1, :])
        prob_grad = lax.dot_general(lane_half(value, h), grad, NT, preferred_element_type=F32)
        inner_sum = jnp.sum(probs * prob_grad, axis=0, keepdims=True)
        score_grad = (probs * (prob_grad - inner_sum)).astype(BF)
        dv_h = jnp.dot(probs.astype(BF), grad, preferred_element_type=F32)
        dk_h = jnp.dot(score_grad, query, preferred_element_type=F32)
        dv = dv_h if h == 0 else jnp.where(lane < HD, dv, dv_h)
        dk = dk_h if h == 0 else jnp.where(lane < HD, dk, dk_h)
        rows = key_t[h * HD : (h + 1) * HD]
        dq_t.append(jnp.dot(rows, score_grad, preferred_element_type=F32))
    dq = (jnp.concatenate(dq_t, axis=0).T * scale).astype(BF)
    dv = dv.astype(BF)
    dq_ref[...] = dq
    dk_ref[...] = dk.astype(BF)
    dv_ref[...] = dv
    wide = (8, dq.shape[1])
    dq_sum_ref[0] = jnp.broadcast_to(jnp.sum(dq.astype(F32), axis=0, keepdims=True), wide)
    dv_sum_ref[0] = jnp.broadcast_to(jnp.sum(dv.astype(F32), axis=0, keepdims=True), wide)


def attention_specs(seq_len, deps):
    block = pl.BlockSpec((seq_len, 2 * HD), lambda r, n: (r, n))
    seg = pl.BlockSpec((None, 1, seq_len), lambda r, n: (r, 0, 0))
    total = pl.BlockSpec((None, 1, 8, seq_len), lambda r, n: (r, n, 0, 0))
    sums = pl.BlockSpec((1, 8, 2 * HD), lambda r, n: (r, 0, n))
    return block, seg, total, sums, [pl.BlockSpec(memory_space=pl.ANY)] * deps


def attend_forward(seg, queries, keys, values):
    rows, seq_len = seg.shape
    block, seg_spec, total, _, _ = attention_specs(seq_len, 0)
    tokens, width = queries.shape
    pairs = width // (2 * HD)
    return pl.pallas_call(
        attend_forward_body,
        out_shape=[
            jax.ShapeDtypeStruct((tokens, width), BF),
            jax.ShapeDtypeStruct((rows, pairs, 8, seq_len), F32),
        ],
        grid=(rows, pairs),
        in_specs=[seg_spec, block, block, block],
        out_specs=[block, total],
        scratch_shapes=[pltpu.VMEM((seq_len, seq_len), F32)],
        name="attend_forward",
        cost_estimate=LIGHT,
    )(seg.reshape(rows, 1, seq_len), queries, keys, values)


def attend_backward(seg, queries, keys, values, mixed_grad, totals, deps):
    rows, seq_len = seg.shape
    block, seg_spec, total, sums, extra = attention_specs(seq_len, len(deps))
    tokens, width = queries.shape
    pairs = width // (2 * HD)
    outs = pl.pallas_call(
        attend_backward_body,
        out_shape=[jax.ShapeDtypeStruct((tokens, width), BF)] * 3
        + [jax.ShapeDtypeStruct((rows, 8, width), F32)] * 2,
        grid=(rows, pairs),
        in_specs=[seg_spec, block, block, block, block, total] + extra,
        out_specs=[block, block, block, sums, sums],
        scratch_shapes=[pltpu.VMEM((seq_len, seq_len), F32)],
        name="attend_backward",
        cost_estimate=LIGHT,
    )(seg.reshape(rows, 1, seq_len), queries, keys, values, mixed_grad, totals, *deps)
    dq, dk, dv, dq_sum, dv_sum = outs
    return dq, dk, dv, jnp.sum(dq_sum[:, 0], axis=0), jnp.sum(dv_sum[:, 0], axis=0)


class Slice:
    def __init__(self, dp, inner):
        self.inner, self.chips, self.count = inner, dp // 2, dp * inner

    def swap(self, value, mask):
        pairs = [(i, i ^ mask) for i in range(self.count)]
        return lax.ppermute(value, AXES, pairs)

    def across_core(self, value):
        return self.swap(value, self.inner)

    def across_chip(self, value, hop):
        return self.swap(value, hop * 2 * self.inner)

    def place(self):
        me = lax.axis_index(AXES)
        z = me % self.inner
        core = (me // self.inner) % 2
        return me, jnp.stack([me // (2 * self.inner), core, z]).astype(jnp.int32)


def first_shard(matrices, vectors):
    rows = matrices[0].shape[0]
    columns = sum(p.shape[1] for p in matrices)

    def body(*refs):
        out_ref, turn_ref = refs[-2:]
        at = 0
        for ref in refs[: len(matrices)]:
            out_ref[:, at : at + ref.shape[1]] = ref[...]
            at += ref.shape[1]
        turn_ref[...] = jnp.zeros_like(turn_ref)
        row = 0
        for ref in refs[len(matrices) : -2]:
            for start in range(0, ref.shape[1], rows):
                turn_ref[row : row + 1, 0:rows] = ref[:, start : start + rows].astype(F32)
                row += 1
        out_ref[:, at:] = turn_ref[...].T[0:rows].astype(BF)

    return pl.pallas_call(
        body,
        out_shape=struct((rows, columns + 128), BF),
        scratch_shapes=[pltpu.VMEM((128, 128), F32)],
        name="first_shard",
        cost_estimate=LIGHT,
    )(*matrices, *[v.reshape(1, -1) for v in vectors])


def in_z_order(net, parts, ids):
    rows, columns = parts[0].shape
    if rows % 16:
        stacked = jnp.stack(parts)
        return jnp.take(stacked, jnp.arange(net.inner) ^ ids[2], axis=0).reshape(-1, columns)
    tile = next(columns // n for n in (2, 3, 1) if columns % (n * 128) == 0)

    def body(ids_ref, *refs):
        for s, part in enumerate(refs[:-1]):
            row = (ids_ref[2] ^ s) * rows
            refs[-1][pl.ds(pl.multiple_of(row, rows), rows), :] = part[...]

    return pl.pallas_call(
        body,
        out_shape=struct((net.inner * rows, columns), BF),
        grid_spec=pltpu.PrefetchScalarGridSpec(
            num_scalar_prefetch=1,
            grid=(columns // tile,),
            in_specs=[pl.BlockSpec((rows, tile), lambda n, ids: (0, n))] * net.inner,
            out_specs=pl.BlockSpec((net.inner * rows, tile), lambda n, ids: (0, n)),
        ),
        name="in_z_order",
        cost_estimate=LIGHT,
    )(ids, *parts)


class Gather:
    def __init__(self, net, shard, ids, relay, *late):
        self.net, self.ids = net, ids
        self.relayed = relay and net.chips == 4
        self.along = [shard]
        reach = net.inner // 2
        while reach:
            if late and len(self.along) > 1:
                self.along[1:] = [tie(part, *late) for part in self.along[1:]]
            self.along = [
                part
                for near in self.along
                for part in (near, net.swap(near, reach))
            ]
            reach //= 2
        order = [0]
        reach = net.inner // 2
        while reach:
            order = [s ^ far for s in order for far in (0, reach)]
            reach //= 2
        self.along = [self.along[order.index(s)] for s in range(net.inner)]

    def ordered(self, *after):
        parts = list(lax.optimization_barrier((*self.along, *after))[: self.net.inner])
        self.block = in_z_order(self.net, parts, self.ids)
        self.rows = self.block.shape[0]
        return self.block

    def plane(self, *after):
        net = self.net
        self.pieces = [(self.block, 0, 0, 0)]
        hops = range(1, 3 if self.relayed else net.chips)
        sent = tie(self.block, *after)
        self.pieces += [(net.across_chip(sent, j), j, 0, 0) for j in hops]

    def relay(self, *after):
        net = self.net
        if self.relayed:
            half = self.rows // 2
            first, second = self.pieces[1][0], self.pieces[2][0]
            low = net.across_chip(tie(first, second, *after)[:half], 2)
            high = net.across_chip(tie(second, first, *after)[half:], 1)
            self.pieces += [(low, 3, 0, 0), (high, 3, 0, half)]
        return [p for p, _, _, _ in self.pieces]

    def cores(self, *after):
        across = [(self.net.across_core(tie(p, *after)), j, 1, s) for p, j, _, s in self.pieces]
        return Rows(self.net, self.rows, self.pieces + across)


class Rows:
    def __init__(self, net, block, pieces):
        self.block = block
        self.count = net.chips * 2
        self.arrays = [p for p, _, _, _ in pieces]
        self.meta = [(p.shape[0], j, c, s) for p, j, c, s in pieces]

    def after(self, *others):
        again = Rows.__new__(Rows)
        again.block, again.count, again.meta = self.block, self.count, self.meta
        tied = lax.optimization_barrier((*self.arrays, *others))
        again.arrays = list(tied[: len(self.arrays)])
        return again

    def start(self, ids_ref, refs, column, target, at, width, sems):
        for ref, (rows, j, c, s) in zip(refs, self.meta):
            block = (ids_ref[0] ^ j) * 2 + (ids_ref[1] ^ c)
            row = pl.multiple_of(block * self.block + s, 16)
            pltpu.make_async_copy(
                ref.at[:, pl.ds(column, width)],
                target.at[pl.ds(row, rows), pl.ds(at, width)],
                sems.at[block],
            ).start()

    def wait(self, block, target, at, width, sems):
        row = block * self.block
        if not isinstance(row, int):
            row = pl.multiple_of(row, 16)
        there = target.at[pl.ds(row, self.block), pl.ds(at, width)]
        pltpu.make_async_copy(there, there, sems.at[block]).wait()

    def wait_all(self, target, at, width, sems):
        for block in range(self.count):
            self.wait(block, target, at, width, sems)


def kernel(body, name, ids, grid, operands, outs, scratch):
    return pl.pallas_call(
        body,
        out_shape=[o for o, _ in outs],
        grid_spec=pltpu.PrefetchScalarGridSpec(
            num_scalar_prefetch=1,
            grid=grid,
            in_specs=[s for _, s in operands],
            out_specs=[s for _, s in outs],
            scratch_shapes=scratch,
        ),
        name=name,
        cost_estimate=LIGHT,
    )(ids, *[o for o, _ in operands])


def project(ids, tokens, weights):
    count, width = tokens.shape
    tile = 512
    per = width // tile
    n_pieces = len(weights.arrays)

    def body(ids_ref, x_ref, *refs):
        pieces = refs[:n_pieces]
        outs = refs[n_pieces : n_pieces + 3]
        vec_ref, w_ref, s_ref, sems = refs[n_pieces + 3 :]
        step = pl.program_id(0)

        @pl.when(step == 0)
        def _():
            weights.start(ids_ref, pieces, 4 * width, s_ref, 0, 128, sems.at[3])
            for i in range(3):
                weights.start(ids_ref, pieces, i * width, w_ref, i * width, width, sems.at[i])
            weights.wait_all(s_ref, 0, 128, sems.at[3])
            vec_ref[...] = s_ref[...].astype(F32).T[0 : vec_ref.shape[0]]

        for i, row in enumerate((0, None, 1)):

            @pl.when(step == i * per)
            def _():
                weights.wait_all(w_ref, i * width, width, sems.at[i])

            @pl.when((step >= i * per) & (step < (i + 1) * per))
            def _():
                columns = pl.ds(pl.multiple_of(step * tile, tile), tile)
                out = dot(x_ref[...], w_ref[:, columns])
                if row is not None:
                    inside = pl.ds(pl.multiple_of((step - i * per) * tile, tile), tile)
                    out = out + vec_ref[row : row + 1, inside]
                outs[i][...] = out.astype(BF)

    def out_spec(i):
        return pl.BlockSpec((count, tile), lambda n, ids: (0, jnp.clip(n - i * per, 0, per - 1)))

    return kernel(
        body,
        "project",
        ids,
        (3 * per,),
        [(tokens, whole(tokens.shape))] + [(p, ANY) for p in weights.arrays],
        [(struct(tokens.shape, BF), out_spec(i)) for i in range(3)]
        + [(struct((16, width), F32), whole((16, width)))],
        [
            pltpu.VMEM((width, 3 * width), BF),
            pltpu.VMEM((width, 128), BF),
            pltpu.SemaphoreType.DMA((4, weights.count)),
        ],
    )


def close_attention(ids, mixed, tokens, weights, vectors):
    count, width = tokens.shape
    rows = 256
    n_pieces = len(weights.arrays)

    def body(ids_ref, m_ref, x_ref, vec_ref, *refs):
        pieces = refs[:n_pieces]
        normed_ref, inverse_ref, low_ref, w_ref, sems = refs[n_pieces:]

        @pl.when(pl.program_id(0) == 0)
        def _():
            weights.start(ids_ref, pieces, 3 * width, w_ref, 0, width, sems)
            weights.wait_all(w_ref, 0, width, sems)

        total = x_ref[...].astype(F32) + (dot(m_ref[...], w_ref[...]) + vec_ref[2:3])
        normed, inverse = normalise(total)
        normed_ref[...] = normed
        inverse_ref[...] = jnp.broadcast_to(inverse, inverse_ref.shape)
        low_ref[...] = (normed * vec_ref[3:4] + vec_ref[4:5]).astype(BF)

    block = pl.BlockSpec((rows, width), lambda n, ids: (n, 0))
    return kernel(
        body,
        "close_attention",
        ids,
        (count // rows,),
        [(mixed, block), (tokens, block), (vectors, whole(vectors.shape))]
        + [(p, ANY) for p in weights.arrays],
        [
            (struct((count, width), F32), block),
            (struct((count, 128), F32), pl.BlockSpec((rows, 128), lambda n, ids: (n, 0))),
            (struct((count, width), BF), block),
        ],
        [pltpu.VMEM((width, width), BF), pltpu.SemaphoreType.DMA((weights.count,))],
    )


def ffn_in(ids, low, weights, bias):
    count, width = low.shape
    wide = bias.shape[1]
    tile = 1024
    n_pieces = len(weights.arrays)

    def body(ids_ref, x_ref, bias_ref, *refs):
        pieces = refs[:n_pieces]
        act_ref, slope_ref, w_ref, sems = refs[n_pieces:]
        step = pl.program_id(0)

        @pl.when(step == 0)
        def _():
            for g in range(wide // tile):
                weights.start(ids_ref, pieces, g * tile, w_ref.at[g], 0, tile, sems.at[g])

        weights.wait_all(w_ref.at[step], 0, tile, sems.at[step])
        for at in range(0, tile, 512):
            columns = slice(at, at + 512)
            pre = dot(x_ref[...], w_ref[step, :, columns]) + bias_ref[:, columns]
            below = 0.5 + 0.5 * lax.erf(pre * (0.5**0.5))
            density = jnp.exp(pre * pre * -0.5) * 0.3989422804014327
            act_ref[:, columns] = (pre * below).astype(BF)
            slope_ref[:, columns] = below + pre * density

    block = pl.BlockSpec((count, tile), lambda n, ids: (0, n))
    return kernel(
        body,
        "ffn_in",
        ids,
        (wide // tile,),
        [(low, whole(low.shape)), (bias, pl.BlockSpec((1, tile), lambda n, ids: (0, n)))]
        + [(p, ANY) for p in weights.arrays],
        [(struct((count, wide), BF), block), (struct((count, wide), F32), block)],
        [
            pltpu.VMEM((wide // tile, width, tile), BF),
            pltpu.SemaphoreType.DMA((wide // tile, weights.count)),
        ],
    )


def ffn_out(ids, act, normed, out_grad, weights, vectors):
    count, wide = act.shape
    width = normed.shape[1]
    n_pieces = len(weights.arrays)

    def body(ids_ref, act_ref, n_ref, g_ref, vec_ref, *refs):
        pieces = refs[:n_pieces]
        out_ref, sum_ref, low_ref, sums_ref, acc_ref, w_ref, sems = refs[n_pieces:]
        tile = 256
        for i in range(width // tile):
            weights.start(ids_ref, pieces, i * tile, w_ref, i * tile, tile, sems.at[i])
        for i in range(width // tile):
            part = slice(i * tile, (i + 1) * tile)
            start = n_ref[:, part] * vec_ref[3:4, part] + vec_ref[4:5, part] + vec_ref[5:6, part]
            weights.wait_all(w_ref, i * tile, tile, sems.at[i])
            acc_ref[:, part] = start + dot(act_ref[...], w_ref[:, part])
        n2, inverse = normalise(acc_ref[...])
        out_ref[...] = (n2 * vec_ref[6:7] + vec_ref[7:8]).astype(BF)
        grad = g_ref[...].astype(F32)
        back = normalise_back(grad * vec_ref[6:7], n2, inverse)
        low = back.astype(BF)
        sum_ref[...] = back
        low_ref[...] = low
        sums_ref[0:1, :] = total_rows(grad * n2)
        sums_ref[1:2, :] = total_rows(grad)
        sums_ref[2:3, :] = total_rows(low.astype(F32))

    size = (count, width)
    return kernel(
        body,
        "ffn_out",
        ids,
        (1,),
        [
            (act, whole(act.shape)),
            (normed, whole(size)),
            (out_grad, whole(size)),
            (vectors, whole(vectors.shape)),
        ]
        + [(p, ANY) for p in weights.arrays],
        [
            (struct(size, BF), whole(size)),
            (struct(size, F32), whole(size)),
            (struct(size, BF), whole(size)),
            (struct((8, width), F32), whole((8, width))),
        ],
        [
            pltpu.VMEM(size, F32),
            pltpu.VMEM((wide, width), BF),
            pltpu.SemaphoreType.DMA((width // 256, weights.count)),
        ],
    )


def ffn_back(ids, grad, slope, weights, deps):
    count, wide = slope.shape
    width = grad.shape[1]
    block = min(wide, 1024)
    per = block // weights.block
    n_pieces = len(weights.arrays)

    def body(ids_ref, grad_ref, slope_ref, *refs):
        pieces = refs[:n_pieces]
        out_ref, sums_ref, w_ref, sems = refs[-4:]
        step = pl.program_id(0)

        @pl.when(step == 0)
        def _():
            weights.start(ids_ref, pieces, 0, w_ref, 0, width, sems)

        for i in range(per):
            weights.wait(step * per + i, w_ref, 0, width, sems)
        rows = pl.ds(pl.multiple_of(step * block, 16), block)
        back = (dot_nt(grad_ref[...], w_ref[rows, :]) * slope_ref[...]).astype(BF)
        out_ref[...] = back
        sums_ref[...] = jnp.broadcast_to(total_rows(back.astype(F32)), sums_ref.shape)

    tile = pl.BlockSpec((count, block), lambda n, ids: (0, n))
    return kernel(
        body,
        "ffn_back",
        ids,
        (wide // block,),
        [(grad, whole(grad.shape)), (slope, tile)]
        + [(p, ANY) for p in weights.arrays]
        + [(d, ANY) for d in deps],
        [
            (struct((count, wide), BF), tile),
            (struct((8, wide), F32), pl.BlockSpec((8, block), lambda n, ids: (0, n))),
        ],
        [pltpu.VMEM((wide, width), BF), pltpu.SemaphoreType.DMA((weights.count,))],
    )


def attention_norm_back(ids, inner_grad, ffn_grad, normed, inverse, inner, weights, vectors, deps):
    count, wide = inner_grad.shape
    width = normed.shape[1]
    tile = 256
    steps = width // tile
    per = tile // inner.block
    n_pieces = len(weights.arrays)

    def body(ids_ref, grad_ref, ffn_ref, n_ref, inverse_ref, vec_ref, *refs):
        pieces = refs[:n_pieces]
        inner_pieces = refs[n_pieces : 2 * n_pieces]
        low_ref, sum_ref, mixed_ref, sums_ref, acc_ref, w_ref, w_sems, o_ref, o_sems = refs[-9:]
        step = pl.program_id(0)

        @pl.when(step == 0)
        def _():
            inner.start(ids_ref, inner_pieces, 0, w_ref, 0, wide, w_sems)
            weights.start(ids_ref, pieces, 3 * width, o_ref, 0, width, o_sems)

        for i in range(per):
            inner.wait(step * per + i, w_ref, 0, wide, w_sems)
        place = pl.ds(pl.multiple_of(step * tile, tile), tile)
        acc_ref[:, place] = ffn_ref[...] + dot_nt(grad_ref[...], w_ref[place, :])

        @pl.when(step == steps - 1)
        def _():
            grad = acc_ref[...]
            normed_rows = n_ref[...]
            back = normalise_back(grad * vec_ref[3:4], normed_rows, inverse_ref[:, 0:1])
            low = back.astype(BF)
            low_ref[...] = low
            sum_ref[...] = back
            sums_ref[0:1, :] = total_rows(grad * normed_rows)
            sums_ref[1:2, :] = total_rows(grad)
            sums_ref[2:3, :] = total_rows(low.astype(F32))
            weights.wait_all(o_ref, 0, width, o_sems)
            mixed_ref[...] = dot_nt(low, o_ref[...]).astype(BF)

    size = (count, width)
    return kernel(
        body,
        "attention_norm_back",
        ids,
        (steps,),
        [
            (inner_grad, whole(inner_grad.shape)),
            (ffn_grad, pl.BlockSpec((count, tile), lambda n, ids: (0, n))),
            (normed, whole(size)),
            (inverse, whole(inverse.shape)),
            (vectors, whole(vectors.shape)),
        ]
        + [(p, ANY) for p in weights.arrays + inner.arrays]
        + [(d, ANY) for d in deps],
        [
            (struct(size, BF), whole(size)),
            (struct(size, F32), whole(size)),
            (struct(size, BF), whole(size)),
            (struct((8, width), F32), whole((8, width))),
        ],
        [
            pltpu.VMEM(size, F32),
            pltpu.VMEM((width, wide), BF),
            pltpu.SemaphoreType.DMA((weights.count,)),
            pltpu.VMEM((width, width), BF),
            pltpu.SemaphoreType.DMA((weights.count,)),
        ],
    )


def inputs_back(ids, base, grads, weights, deps):
    count, width = base.shape
    tile = 256
    per = tile // weights.block
    n_pieces = len(weights.arrays)

    def body(ids_ref, base_ref, q_ref, k_ref, v_ref, *refs):
        pieces = refs[:n_pieces]
        out_ref, w_ref, sems = refs[-3:]
        step = pl.program_id(0)

        @pl.when(step == 0)
        def _():
            weights.start(ids_ref, pieces, 0, w_ref, 0, 3 * width, sems)

        for i in range(per):
            weights.wait(step * per + i, w_ref, 0, 3 * width, sems)
        place = pl.ds(pl.multiple_of(step * tile, tile), tile)
        out = base_ref[...]
        for i, ref in enumerate((q_ref, k_ref, v_ref)):
            out = out + dot_nt(ref[...], w_ref[place, i * width : (i + 1) * width])
        out_ref[...] = out

    block = pl.BlockSpec((count, tile), lambda n, ids: (0, n))
    return kernel(
        body,
        "inputs_back",
        ids,
        (width // tile,),
        [(base, block)]
        + [(g, whole(g.shape)) for g in grads]
        + [(p, ANY) for p in weights.arrays]
        + [(d, ANY) for d in deps],
        [(struct(base.shape, F32), block)],
        [pltpu.VMEM((width, 3 * width), BF), pltpu.SemaphoreType.DMA((weights.count,))],
    )[0]


def split_hops(kept, bit):
    stay = [j for j in kept if not j & bit]
    return stay, [j | bit for j in stay]


class RowSum:
    def __init__(self, net, pairs, ids, tile):
        self.net, self.ids, self.tile = net, ids, tile
        self.rights = [right for _, right in pairs]
        self.left = []
        for left, _ in pairs:
            if not any(left is known for known in self.left):
                self.left.append(left)
        self.uses = [[left is known for known in self.left].index(True) for left, _ in pairs]
        self.width = self.left[0].shape[1] // (net.chips * 2)
        self.columns = sum(r.shape[1] for r in self.rights)
        bits = [1 << b for b in range(net.chips.bit_length() - 1)]
        self.bits = (bits, bits[::-1])
        self.kept = [list(range(net.chips))] * 2

    def lefts(self, core):
        net, width = self.net, self.width
        if width % 128 == 0:
            spec = [
                pl.BlockSpec(
                    (self.left[0].shape[0], width),
                    lambda n, ids, j=j: (0, (ids[0] ^ j) * 2 + (ids[1] ^ core)),
                )
                for j in range(net.chips)
            ]
            return [left for left in self.left for _ in spec], spec * len(self.left)
        chosen = []
        for left in self.left:
            picked = []
            for j in range(net.chips):
                at = ((self.ids[0] ^ j) * 2 + (self.ids[1] ^ core)) * width
                picked.append(lax.dynamic_slice_in_dim(left, at, width, axis=1))
            chosen.append(jnp.concatenate(picked, axis=1))
        return chosen, [whole(picked.shape) for picked in chosen]

    def right_specs(self):
        specs, lo = [], 0
        for right in self.rights:
            count = right.shape[1] // self.tile
            specs.append(
                pl.BlockSpec(
                    (right.shape[0], self.tile),
                    lambda n, ids, lo=lo, c=count: (0, jnp.clip(n - lo, 0, c - 1)),
                )
            )
            lo += count
        return specs

    def product(self, left_refs, right_refs, step, then):
        each = len(left_refs) // len(self.left)
        lo = 0
        for ref, right, use in zip(right_refs, self.rights, self.uses):
            count = right.shape[1] // self.tile

            @pl.when((step >= lo) & (step < lo + count))
            def _():
                left = [part[...] for part in left_refs[use * each : (use + 1) * each]]
                if each > 1 and self.width < 512:
                    left = [jnp.concatenate(left, axis=1)]
                for i, part in enumerate(left):
                    then(i * part.shape[1], dot_tn(part, ref[...]))

            lo += count

    def other_core(self, *deps):
        lefts, left_specs = self.lefts(1)
        rows = self.net.chips * self.width

        def body(ids_ref, *refs):
            out_ref = refs[-1]

            def store(at, value):
                out_ref[at : at + value.shape[0], :] = value.astype(BF)

            self.product(
                refs[: len(lefts)],
                refs[len(lefts) : len(lefts) + len(self.rights)],
                pl.program_id(0),
                store,
            )

        (self.sent,) = kernel(
            body,
            "rows_of_other_core",
            self.ids,
            (self.columns // self.tile,),
            list(zip(lefts + self.rights, left_specs + self.right_specs()))
            + [(d, ANY) for d in deps],
            [
                (
                    struct((rows, self.columns), BF),
                    pl.BlockSpec((rows, self.tile), lambda n, ids: (0, n)),
                )
            ],
            [],
        )
        self.got = self.net.across_core(self.sent)
        return self.sent

    def own_core(self, *deps):
        lefts, left_specs = self.lefts(0)
        rows, tile = self.net.chips * self.width, self.tile
        steps = self.columns // tile
        half = steps // 2
        sides = [split_hops(self.kept[s], self.bits[s][0]) for s in range(2)]

        def body(ids_ref, *refs):
            got_ref = refs[len(lefts) + len(self.rights)]
            out_refs = refs[-4:]
            step = pl.program_id(0)

            def store(at, value):
                value = (value + got_ref[at : at + value.shape[0], :].astype(F32)).astype(BF)
                for side in range(2):

                    @pl.when((step >= side * half) & (step < (side + 1) * half))
                    def _():
                        for which, hops in enumerate(sides[side]):
                            for i, j in enumerate(hops):
                                row = j * self.width - at
                                if 0 <= row < value.shape[0]:
                                    out_refs[side * 2 + which][
                                        i * self.width : (i + 1) * self.width, :
                                    ] = value[row : row + self.width]

            self.product(
                refs[: len(lefts)],
                refs[len(lefts) : len(lefts) + len(self.rights)],
                step,
                store,
            )

        outs = []
        for side in range(2):
            spec = pl.BlockSpec(
                (rows // 2, tile),
                lambda n, ids, side=side: (0, jnp.clip(n - side * half, 0, half - 1)),
            )
            outs += [(struct((rows // 2, self.columns // 2), BF), spec)] * 2
        out = kernel(
            body,
            "rows_of_own_core",
            self.ids,
            (steps,),
            list(zip(lefts + self.rights, left_specs + self.right_specs()))
            + [(self.got, pl.BlockSpec((rows, tile), lambda n, ids: (0, n)))]
            + [(d, ANY) for d in deps],
            outs,
            [],
        )
        self.held = [out[0], out[2]]
        self.away = [out[1], out[3]]
        self.send()
        return out[0]

    def send(self):
        for s in range(2):
            self.kept[s] = split_hops(self.kept[s], self.bits[s][0])[0]
        self.arrived = [self.net.across_chip(self.away[s], self.bits[s][0]) for s in range(2)]
        self.bits = (self.bits[0][1:], self.bits[1][1:])

    def fold(self, *deps):
        rows, columns = self.held[0].shape
        tile = columns // 2
        sides = [split_hops(self.kept[s], self.bits[s][0]) for s in range(2)]

        def body(ids_ref, *refs):
            out_refs = refs[-4:]
            for s in range(2):
                for which, hops in enumerate(sides[s]):
                    for i, j in enumerate(hops):
                        at = self.kept[s].index(j) * self.width
                        part = slice(at, at + self.width)
                        value = refs[2 * s][part, :].astype(F32) + refs[2 * s + 1][part, :].astype(F32)
                        out_refs[2 * s + which][i * self.width : (i + 1) * self.width, :] = (
                            value.astype(BF)
                        )

        block = pl.BlockSpec((rows, tile), lambda n, ids: (0, n))
        half = pl.BlockSpec((rows // 2, tile), lambda n, ids: (0, n))
        out = kernel(
            body,
            "fold",
            self.ids,
            (columns // tile,),
            [(a, block) for s in range(2) for a in (self.held[s], self.arrived[s])]
            + [(d, ANY) for d in deps],
            [(struct((rows // 2, columns), BF), half)] * 4,
            [],
        )
        self.held = [out[0], out[2]]
        self.away = [out[1], out[3]]
        self.send()
        return self.fold() if self.bits[0] else out[0]

    def fold_z(self, *deps):
        net, count = self.net, self.net.inner
        columns = self.held[0].shape[1]
        rows = self.width // count
        stay, leave = split_hops(list(range(count)), 1)
        size = (rows * len(stay), 2 * columns)
        if rows % 16:
            held = tie(jnp.concatenate(self.held, axis=1), *deps).astype(F32)
            held = held + jnp.concatenate(self.arrived, axis=1).astype(F32)
            held = held.reshape(count, rows, -1).astype(BF)
            keep, away = (
                jnp.take(held, jnp.array(hops) ^ self.ids[2], axis=0).reshape(size)
                for hops in (stay, leave)
            )
        else:

            def body(ids_ref, *refs):
                for out_ref, hops in zip(refs[-2:], (stay, leave)):
                    for i, s in enumerate(hops):
                        at = pl.ds(pl.multiple_of((ids_ref[2] ^ s) * rows, 16), rows)
                        for side in range(2):
                            value = refs[2 * side][at, :].astype(F32)
                            value = value + refs[2 * side + 1][at, :].astype(F32)
                            place = slice(side * columns, (side + 1) * columns)
                            out_ref[i * rows : (i + 1) * rows, place] = value.astype(BF)

            keep, away = kernel(
                body,
                "fold_z",
                self.ids,
                (1,),
                [
                    (a, whole(a.shape))
                    for s in range(2)
                    for a in (self.held[s], self.arrived[s])
                ]
                + [(d, ANY) for d in deps],
                [(struct(size, BF), whole(size))] * 2,
                [],
            )
        self.total, self.came, self.reach = keep, net.swap(away, 1), 1
        return keep

    def fold_far(self, *deps):
        while self.reach * 2 < self.net.inner:
            self.reach *= 2
            total = tie(self.total, *deps).astype(F32) + self.came.astype(F32)
            rows = self.width // self.net.inner
            count = total.shape[0] // rows
            stay = [i for i in range(count) if not i & 1]
            blocks = total.reshape(count, rows, -1)
            away = jnp.concatenate([blocks[i + 1] for i in stay], axis=0).astype(BF)
            self.total = jnp.concatenate([blocks[i] for i in stay], axis=0)
            self.came = self.net.swap(away, self.reach)
        return self.came

    def finish(self, *deps):
        return tie(self.total, *deps).astype(F32) + self.came.astype(F32)


def shards(
    net,
    inputs,
    segment_ids,
    query_weight,
    key_weight,
    value_weight,
    output_weight,
    query_bias,
    value_bias,
    output_bias,
    attn_gain,
    attn_shift,
    inner_weight,
    inner_bias,
    outer_weight,
    outer_bias,
    ffn_gain,
    ffn_shift,
    out_grad,
):
    row_count, seq_len, width = inputs.shape
    tokens = inputs.reshape(row_count * seq_len, width)
    _, ids = net.place()
    small = [
        query_bias,
        value_bias,
        output_bias,
        attn_gain,
        attn_shift,
        outer_bias,
        ffn_gain,
        ffn_shift,
        inner_bias,
    ]
    mine = query_bias.shape[0]
    shard = first_shard([query_weight, key_weight, value_weight, output_weight], small)
    gather_a = Gather(net, shard, ids, True)
    gather_a.ordered()
    gather_a.plane()
    gather_b = Gather(net, tie(inner_weight, gather_a.block), ids, True)
    arrived = gather_a.relay(*gather_b.along)
    weights_a = gather_a.cores()
    gather_b.ordered(*arrived)
    gather_b.plane(*weights_a.arrays)
    queries, keys, values, vectors = project(ids, tokens, weights_a)
    gather_c = Gather(
        net, tie(outer_weight, gather_b.block, *weights_a.arrays), ids, True, queries
    )
    spread = inner_bias.shape[0] // mine
    inner_bias_full = vectors[8 : 8 + spread].reshape(spread, net.count, mine)
    inner_bias_full = inner_bias_full.swapaxes(0, 1).reshape(1, -1)
    mixed, totals = attend_forward(segment_ids, queries, keys, values)
    arrived = gather_b.relay(mixed, *gather_c.along)
    weights_b = gather_b.cores()
    gather_c.ordered(*arrived)
    gather_c.plane()
    normed, inverse, normed_low = close_attention(ids, mixed, tokens, weights_a, vectors)
    act, slope = ffn_in(ids, normed_low, weights_b, inner_bias_full)
    gather_c.relay(act)
    weights_c = gather_c.cores()
    grad_out = out_grad.reshape(tokens.shape)
    outputs, ffn_grad, branch_grad, ffn_sums = ffn_out(
        ids, act, normed, grad_out, weights_c, vectors
    )
    outer_sum = RowSum(net, [(act, branch_grad)], ids, 512)
    last = outer_sum.other_core()
    inner_grad, inner_sums = ffn_back(ids, branch_grad, slope, weights_c, [last])
    last = outer_sum.own_core(inner_grad)
    inner_sum = RowSum(net, [(normed_low, inner_grad)], ids, 1024)
    last = inner_sum.other_core(last)
    attn_grad, attn_sum_grad, mixed_grad, attn_sums = attention_norm_back(
        ids, inner_grad, ffn_grad, normed, inverse, weights_b, weights_a, vectors, [last]
    )
    last = outer_sum.fold(attn_grad)
    last = inner_sum.own_core(last)
    query_grad, key_grad, value_grad, grad_query_bias, grad_value_bias = attend_backward(
        segment_ids, queries, keys, values, mixed_grad, totals, [last]
    )
    inputs_sum = RowSum(
        net,
        [(mixed, attn_grad)] + [(tokens, g) for g in (query_grad, key_grad, value_grad)],
        ids,
        1024,
    )
    last = inputs_sum.other_core(*outer_sum.arrived, *inner_sum.arrived)
    last = inner_sum.fold(last)
    last = outer_sum.fold_z(last)
    last = inputs_sum.own_core(last)
    outer_sum.fold_far(last)
    last = inner_sum.fold_z(last)
    input_grad = inputs_back(
        ids, attn_sum_grad, (query_grad, key_grad, value_grad), weights_a, [last, outer_sum.came]
    )
    shard_outer = outer_sum.finish(input_grad)
    last = inputs_sum.fold(input_grad)
    inner_sum.fold_far(last)
    last = inputs_sum.fold_z(inner_sum.came)
    shard_inner = inner_sum.finish(last)
    inputs_sum.fold_far(last)
    shard_inputs = inputs_sum.finish()
    shard_output, shard_query, shard_key, shard_value = (
        shard_inputs[:, i * width : (i + 1) * width] for i in range(4)
    )
    rows = jnp.concatenate(
        [grad_query_bias[None], grad_value_bias[None], attn_sums[:3], ffn_sums[:3]], axis=0
    )
    rows = rows.reshape(8, net.count, mine).swapaxes(0, 1).reshape(net.count, 8 * mine)
    packed = jnp.concatenate([rows, inner_sums[0].reshape(net.count, -1)], axis=1)
    packed = tie(packed, last)
    summed = jnp.sum(lax.all_to_all(packed, AXES, 0, 0, tiled=True), axis=0)
    vector = [summed[i * mine : (i + 1) * mine] for i in range(8)]
    return (
        outputs.reshape(inputs.shape),
        input_grad.reshape(inputs.shape),
        shard_query,
        shard_key,
        shard_value,
        shard_output,
        vector[0],
        vector[1],
        vector[4],
        vector[2],
        vector[3],
        shard_inner,
        summed[8 * mine :],
        shard_outer,
        vector[7],
        vector[5],
        vector[6],
    )


def solution(mesh):
    placed = (
        P(("dp", "fsdp"), None, None),
        P(("dp", "fsdp"), None),
        P(("dp", "fsdp"), None),
        P(("dp", "fsdp"), None),
        P(("dp", "fsdp"), None),
        P(("dp", "fsdp"), None),
        P(("dp", "fsdp")),
        P(("dp", "fsdp")),
        P(("dp", "fsdp")),
        P(("dp", "fsdp")),
        P(("dp", "fsdp")),
        P(("dp", "fsdp"), None),
        P(("dp", "fsdp")),
        P(("dp", "fsdp"), None),
        P(("dp", "fsdp")),
        P(("dp", "fsdp")),
        P(("dp", "fsdp")),
        P(("dp", "fsdp"), None, None),
    )
    return jax.shard_map(
        functools.partial(shards, Slice(mesh.shape["dp"], mesh.shape["fsdp"])),
        mesh=mesh,
        in_specs=placed,
        out_specs=(
            P(("dp", "fsdp"), None, None),
            P(("dp", "fsdp"), None, None),
            P(("dp", "fsdp"), None),
            P(("dp", "fsdp"), None),
            P(("dp", "fsdp"), None),
            P(("dp", "fsdp"), None),
            P(("dp", "fsdp")),
            P(("dp", "fsdp")),
            P(("dp", "fsdp")),
            P(("dp", "fsdp")),
            P(("dp", "fsdp")),
            P(("dp", "fsdp"), None),
            P(("dp", "fsdp")),
            P(("dp", "fsdp"), None),
            P(("dp", "fsdp")),
            P(("dp", "fsdp")),
            P(("dp", "fsdp")),
        ),
        check_vma=False,
    )
```

```python
import functools

import jax
import jax.numpy as jnp
from jax import lax
from jax.experimental import pallas as pl
from jax.experimental.pallas import tpu as pltpu
from jax.sharding import PartitionSpec as P

H = 16
HD = 64
AXES = ("dp", "fsdp")
BF = jnp.bfloat16
F32 = jnp.float32
EPSILON = 1e-05
NT = (((1,), (1,)), ((), ()))
TN = (((0,), (0,)), ((), ()))
MASKED = -1e30
WEIGHT = 0.3


def spend(micros):
    return pl.CostEstimate(flops=1, bytes_accessed=int(micros * WEIGHT * 1e6), transcendentals=0)


ANY = pl.BlockSpec(memory_space=pl.ANY)


def whole(shape):
    return pl.BlockSpec(shape, lambda *_: (0,) * len(shape))


def struct(shape, dtype):
    return jax.ShapeDtypeStruct(shape, dtype)


def dot(left, right):
    return jnp.dot(left, right, preferred_element_type=F32)


def dot_tn(left, right):
    return lax.dot_general(left, right, TN, preferred_element_type=F32)


def dot_nt(left, right):
    return lax.dot_general(left, right, NT, preferred_element_type=F32)


def tie(value, *after):
    return lax.optimization_barrier((value, *after))[0]


def normalise(rows):
    centred = rows - jnp.mean(rows, axis=-1, keepdims=True)
    spread = jnp.mean(centred * centred, axis=-1, keepdims=True)
    inverse = lax.rsqrt(spread + EPSILON)
    return centred * inverse, inverse


def normalise_back(cotangent, normed, inverse):
    slope = jnp.mean(cotangent * normed, axis=-1, keepdims=True)
    return inverse * (cotangent - jnp.mean(cotangent, axis=-1, keepdims=True) - normed * slope)


def total_rows(matrix):
    return jnp.sum(matrix, axis=0, keepdims=True)


def lane_half(block, which):
    lane = lax.broadcasted_iota(jnp.int32, block.shape, 1)
    return jnp.where((lane >= HD) == (which == 1), block, jnp.zeros_like(block))


def set_mask(seg_ref, mask_ref):
    seg_row = seg_ref[...].astype(F32)
    seg_col = jnp.broadcast_to(seg_row, (128, seg_row.shape[1])).T
    for at in range(0, seg_row.shape[1], 128):
        same = seg_col == seg_row[:, at : at + 128]
        mask_ref[:, at : at + 128] = jnp.where(same, 0.0, MASKED)


def attend_forward_body(seg_ref, q_ref, k_ref, v_ref, mixed_ref, total_ref, mask_ref):
    @pl.when(pl.program_id(1) == 0)
    def _():
        set_mask(seg_ref, mask_ref)

    query = q_ref[...] * jnp.bfloat16(HD**-0.5)
    key = k_ref[...]
    value_t = v_ref[...].T
    halves = []
    for h in range(2):
        scores = lax.dot_general(lane_half(key, h), query, NT, preferred_element_type=F32)
        scores = scores + mask_ref[...]
        high = jnp.max(scores, axis=0, keepdims=True)
        raised = jnp.exp(scores - high)
        total = jnp.sum(raised, axis=0, keepdims=True)
        low = (raised * (1.0 / total)).astype(BF)
        rows = value_t[h * HD : (h + 1) * HD]
        halves.append(jnp.dot(rows, low, preferred_element_type=F32))
        total_ref[0, h : h + 1, :] = high + jnp.log(total)
    mixed_ref[...] = jnp.concatenate(halves, axis=0).T.astype(BF)


def attend_backward_body(
    seg_ref, q_ref, k_ref, v_ref, g_ref, total_ref, *rest
):
    dq_ref, dk_ref, dv_ref, dq_sum_ref, dv_sum_ref, mask_ref = rest[-6:]

    @pl.when(pl.program_id(1) == 0)
    def _():
        set_mask(seg_ref, mask_ref)

    scale = HD**-0.5
    query = q_ref[...] * jnp.bfloat16(scale)
    key, value, grad = k_ref[...], v_ref[...], g_ref[...]
    key_t = key.T
    lane = lax.broadcasted_iota(jnp.int32, key.shape, 1)
    dq_t, dk, dv = [], None, None
    for h in range(2):
        scores = lax.dot_general(lane_half(key, h), query, NT, preferred_element_type=F32)
        probs = jnp.exp(scores + mask_ref[...] - total_ref[0, h : h + 1, :])
        prob_grad = lax.dot_general(lane_half(value, h), grad, NT, preferred_element_type=F32)
        inner_sum = jnp.sum(probs * prob_grad, axis=0, keepdims=True)
        score_grad = (probs * (prob_grad - inner_sum)).astype(BF)
        dv_h = jnp.dot(probs.astype(BF), grad, preferred_element_type=F32)
        dk_h = jnp.dot(score_grad, query, preferred_element_type=F32)
        dv = dv_h if h == 0 else jnp.where(lane < HD, dv, dv_h)
        dk = dk_h if h == 0 else jnp.where(lane < HD, dk, dk_h)
        rows = key_t[h * HD : (h + 1) * HD]
        dq_t.append(jnp.dot(rows, score_grad, preferred_element_type=F32))
    dq = (jnp.concatenate(dq_t, axis=0).T * scale).astype(BF)
    dv = dv.astype(BF)
    dq_ref[...] = dq
    dk_ref[...] = dk.astype(BF)
    dv_ref[...] = dv
    wide = (8, dq.shape[1])
    dq_sum_ref[0] = jnp.broadcast_to(jnp.sum(dq.astype(F32), axis=0, keepdims=True), wide)
    dv_sum_ref[0] = jnp.broadcast_to(jnp.sum(dv.astype(F32), axis=0, keepdims=True), wide)


def attention_specs(seq_len, deps):
    block = pl.BlockSpec((seq_len, 2 * HD), lambda r, n: (r, n))
    seg = pl.BlockSpec((None, 1, seq_len), lambda r, n: (r, 0, 0))
    total = pl.BlockSpec((None, 1, 8, seq_len), lambda r, n: (r, n, 0, 0))
    sums = pl.BlockSpec((1, 8, 2 * HD), lambda r, n: (r, 0, n))
    return block, seg, total, sums, [pl.BlockSpec(memory_space=pl.ANY)] * deps


def attend_forward(seg, queries, keys, values):
    rows, seq_len = seg.shape
    block, seg_spec, total, _, _ = attention_specs(seq_len, 0)
    tokens, width = queries.shape
    pairs = width // (2 * HD)
    return pl.pallas_call(
        attend_forward_body,
        out_shape=[
            jax.ShapeDtypeStruct((tokens, width), BF),
            jax.ShapeDtypeStruct((rows, pairs, 8, seq_len), F32),
        ],
        grid=(rows, pairs),
        in_specs=[seg_spec, block, block, block],
        out_specs=[block, total],
        scratch_shapes=[pltpu.VMEM((seq_len, seq_len), F32)],
        name="attend_forward",
        cost_estimate=spend(13),
    )(seg.reshape(rows, 1, seq_len), queries, keys, values)


def attend_backward(seg, queries, keys, values, mixed_grad, totals, deps):
    rows, seq_len = seg.shape
    block, seg_spec, total, sums, extra = attention_specs(seq_len, len(deps))
    tokens, width = queries.shape
    pairs = width // (2 * HD)
    outs = pl.pallas_call(
        attend_backward_body,
        out_shape=[jax.ShapeDtypeStruct((tokens, width), BF)] * 3
        + [jax.ShapeDtypeStruct((rows, 8, width), F32)] * 2,
        grid=(rows, pairs),
        in_specs=[seg_spec, block, block, block, block, total] + extra,
        out_specs=[block, block, block, sums, sums],
        scratch_shapes=[pltpu.VMEM((seq_len, seq_len), F32)],
        name="attend_backward",
        cost_estimate=spend(17),
    )(seg.reshape(rows, 1, seq_len), queries, keys, values, mixed_grad, totals, *deps)
    dq, dk, dv, dq_sum, dv_sum = outs
    return dq, dk, dv, jnp.sum(dq_sum[:, 0], axis=0), jnp.sum(dv_sum[:, 0], axis=0)


class Slice:
    def __init__(self, dp, inner):
        self.inner, self.chips, self.count = inner, dp // 2, dp * inner

    def swap(self, value, mask):
        pairs = [(i, i ^ mask) for i in range(self.count)]
        return lax.ppermute(value, AXES, pairs)

    def across_core(self, value):
        return self.swap(value, self.inner)

    def across_chip(self, value, hop):
        return self.swap(value, hop * 2 * self.inner)

    def place(self):
        me = lax.axis_index(AXES)
        z = me % self.inner
        core = (me // self.inner) % 2
        return me, jnp.stack([me // (2 * self.inner), core, z]).astype(jnp.int32)


def first_shard(matrices, vectors):
    rows = matrices[0].shape[0]
    columns = sum(p.shape[1] for p in matrices)

    def body(*refs):
        out_ref, turn_ref = refs[-2:]
        at = 0
        for ref in refs[: len(matrices)]:
            out_ref[:, at : at + ref.shape[1]] = ref[...]
            at += ref.shape[1]
        turn_ref[...] = jnp.zeros_like(turn_ref)
        row = 0
        for ref in refs[len(matrices) : -2]:
            for start in range(0, ref.shape[1], rows):
                turn_ref[row : row + 1, 0:rows] = ref[:, start : start + rows].astype(F32)
                row += 1
        out_ref[:, at:] = turn_ref[...].T[0:rows].astype(BF)

    return pl.pallas_call(
        body,
        out_shape=struct((rows, columns + 128), BF),
        scratch_shapes=[pltpu.VMEM((128, 128), F32)],
        name="first_shard",
        cost_estimate=spend(2),
    )(*matrices, *[v.reshape(1, -1) for v in vectors])


def in_z_order(net, parts, ids):
    rows, columns = parts[0].shape
    if rows % 16:
        stacked = jnp.stack(parts)
        return jnp.take(stacked, jnp.arange(net.inner) ^ ids[2], axis=0).reshape(-1, columns)
    tile = next(columns // n for n in (2, 3, 1) if columns % (n * 128) == 0)

    def body(ids_ref, *refs):
        for s, part in enumerate(refs[:-1]):
            row = (ids_ref[2] ^ s) * rows
            refs[-1][pl.ds(pl.multiple_of(row, rows), rows), :] = part[...]

    return pl.pallas_call(
        body,
        out_shape=struct((net.inner * rows, columns), BF),
        grid_spec=pltpu.PrefetchScalarGridSpec(
            num_scalar_prefetch=1,
            grid=(columns // tile,),
            in_specs=[pl.BlockSpec((rows, tile), lambda n, ids: (0, n))] * net.inner,
            out_specs=pl.BlockSpec((net.inner * rows, tile), lambda n, ids: (0, n)),
        ),
        name="in_z_order",
        cost_estimate=spend(3),
    )(ids, *parts)


class Gather:
    def __init__(self, net, shard, ids, relay, *late):
        self.net, self.ids = net, ids
        self.relayed = relay and net.chips == 4
        self.along = [shard]
        reach = net.inner // 2
        while reach:
            if late and len(self.along) > 1:
                self.along[1:] = [tie(part, *late) for part in self.along[1:]]
            self.along = [
                part
                for near in self.along
                for part in (near, net.swap(near, reach))
            ]
            reach //= 2
        order = [0]
        reach = net.inner // 2
        while reach:
            order = [s ^ far for s in order for far in (0, reach)]
            reach //= 2
        self.along = [self.along[order.index(s)] for s in range(net.inner)]

    def ordered(self, *after):
        parts = list(lax.optimization_barrier((*self.along, *after))[: self.net.inner])
        self.block = in_z_order(self.net, parts, self.ids)
        self.rows = self.block.shape[0]
        return self.block

    def plane(self, *after):
        net = self.net
        self.pieces = [(self.block, 0, 0, 0)]
        hops = range(1, 3 if self.relayed else net.chips)
        sent = tie(self.block, *after)
        self.pieces += [(net.across_chip(sent, j), j, 0, 0) for j in hops]

    def relay(self, *after):
        net = self.net
        if self.relayed:
            half = self.rows // 2
            first, second = self.pieces[1][0], self.pieces[2][0]
            low = net.across_chip(tie(first, second, *after)[:half], 2)
            high = net.across_chip(tie(second, first, *after)[half:], 1)
            self.pieces += [(low, 3, 0, 0), (high, 3, 0, half)]
        return [p for p, _, _, _ in self.pieces]

    def cores(self, *after):
        across = [(self.net.across_core(tie(p, *after)), j, 1, s) for p, j, _, s in self.pieces]
        return Rows(self.net, self.rows, self.pieces + across)


class Rows:
    def __init__(self, net, block, pieces):
        self.block = block
        self.count = net.chips * 2
        self.arrays = [p for p, _, _, _ in pieces]
        self.meta = [(p.shape[0], j, c, s) for p, j, c, s in pieces]

    def after(self, *others):
        again = Rows.__new__(Rows)
        again.block, again.count, again.meta = self.block, self.count, self.meta
        tied = lax.optimization_barrier((*self.arrays, *others))
        again.arrays = list(tied[: len(self.arrays)])
        return again

    def start(self, ids_ref, refs, column, target, at, width, sems, hop=None):
        for ref, (rows, j, c, s) in zip(refs, self.meta):
            if hop is not None and j != hop:
                continue
            block = (ids_ref[0] ^ j) * 2 + (ids_ref[1] ^ c)
            row = pl.multiple_of(block * self.block + s, 16)
            pltpu.make_async_copy(
                ref.at[:, pl.ds(column, width)],
                target.at[pl.ds(row, rows), pl.ds(at, width)],
                sems.at[block],
            ).start()

    def wait(self, block, target, at, width, sems):
        row = block * self.block
        if not isinstance(row, int):
            row = pl.multiple_of(row, 16)
        there = target.at[pl.ds(row, self.block), pl.ds(at, width)]
        pltpu.make_async_copy(there, there, sems.at[block]).wait()

    def wait_all(self, target, at, width, sems):
        for block in range(self.count):
            self.wait(block, target, at, width, sems)


def copies(pairs, sems, *at):
    return [
        pltpu.make_async_copy(source, target, sems.at[(*at, i)])
        for i, (source, target) in enumerate(pairs)
    ]


def start_all(some):
    for copy in some:
        copy.start()


def wait_for(some):
    for copy in some:
        copy.wait()


def aligned(start, size):
    return pl.ds(pl.multiple_of(start, 128), size)


def kernel(body, name, micros, ids, grid, operands, outs, scratch):
    return pl.pallas_call(
        body,
        out_shape=[o for o, _ in outs],
        grid_spec=pltpu.PrefetchScalarGridSpec(
            num_scalar_prefetch=1,
            grid=grid,
            in_specs=[s for _, s in operands],
            out_specs=[s for _, s in outs],
            scratch_shapes=scratch,
        ),
        name=name,
        cost_estimate=spend(micros),
    )(ids, *[o for o, _ in operands])


def project(ids, tokens, weights):
    count, width = tokens.shape
    tile = min(width, 1024)
    per = width // tile
    n_pieces = len(weights.arrays)

    def body(ids_ref, x_ref, *refs):
        pieces = refs[:n_pieces]
        outs = refs[n_pieces : n_pieces + 3]
        vec_ref, w_ref, s_ref, sems = refs[n_pieces + 3 :]
        step = pl.program_id(0)

        @pl.when(step == 0)
        def _():
            weights.start(ids_ref, pieces, 4 * width, s_ref, 0, 128, sems.at[3])
            for i in range(3):
                weights.start(ids_ref, pieces, i * width, w_ref, i * width, width, sems.at[i])
            weights.wait_all(s_ref, 0, 128, sems.at[3])
            vec_ref[...] = s_ref[...].astype(F32).T[0 : vec_ref.shape[0]]

        for i, row in enumerate((0, None, 1)):

            @pl.when(step == i * per)
            def _():
                weights.wait_all(w_ref, i * width, width, sems.at[i])

            @pl.when((step >= i * per) & (step < (i + 1) * per))
            def _():
                columns = pl.ds(pl.multiple_of(step * tile, tile), tile)
                out = dot(x_ref[...], w_ref[:, columns])
                if row is not None:
                    inside = pl.ds(pl.multiple_of((step - i * per) * tile, tile), tile)
                    out = out + vec_ref[row : row + 1, inside]
                outs[i][...] = out.astype(BF)

    def out_spec(i):
        return pl.BlockSpec((count, tile), lambda n, ids: (0, jnp.clip(n - i * per, 0, per - 1)))

    return kernel(
        body,
        "project",
        10,
        ids,
        (3 * per,),
        [(tokens, whole(tokens.shape))] + [(p, ANY) for p in weights.arrays],
        [(struct(tokens.shape, BF), out_spec(i)) for i in range(3)]
        + [(struct((16, width), F32), whole((16, width)))],
        [
            pltpu.VMEM((width, 3 * width), BF),
            pltpu.VMEM((width, 128), BF),
            pltpu.SemaphoreType.DMA((4, weights.count)),
        ],
    )


def close_attention(ids, mixed, tokens, weights, vectors):
    count, width = tokens.shape
    rows = 256
    n_pieces = len(weights.arrays)

    def body(ids_ref, m_ref, x_ref, vec_ref, *refs):
        pieces = refs[:n_pieces]
        normed_ref, inverse_ref, low_ref, w_ref, sems = refs[n_pieces:]

        @pl.when(pl.program_id(0) == 0)
        def _():
            weights.start(ids_ref, pieces, 3 * width, w_ref, 0, width, sems)
            weights.wait_all(w_ref, 0, width, sems)

        total = x_ref[...].astype(F32) + (dot(m_ref[...], w_ref[...]) + vec_ref[2:3])
        normed, inverse = normalise(total)
        normed_ref[...] = normed
        inverse_ref[...] = jnp.broadcast_to(inverse, inverse_ref.shape)
        low_ref[...] = (normed * vec_ref[3:4] + vec_ref[4:5]).astype(BF)

    block = pl.BlockSpec((rows, width), lambda n, ids: (n, 0))
    return kernel(
        body,
        "close_attention",
        7,
        ids,
        (count // rows,),
        [(mixed, block), (tokens, block), (vectors, whole(vectors.shape))]
        + [(p, ANY) for p in weights.arrays],
        [
            (struct((count, width), F32), block),
            (struct((count, 128), F32), pl.BlockSpec((rows, 128), lambda n, ids: (n, 0))),
            (struct((count, width), BF), block),
        ],
        [pltpu.VMEM((width, width), BF), pltpu.SemaphoreType.DMA((weights.count,))],
    )


def ffn_in(ids, low, weights, bias):
    count, width = low.shape
    wide = bias.shape[1]
    tile = 1024
    n_pieces = len(weights.arrays)

    def body(ids_ref, x_ref, bias_ref, *refs):
        pieces = refs[:n_pieces]
        act_ref, slope_ref, w_ref, sems = refs[n_pieces:]
        step = pl.program_id(0)

        @pl.when(step == 0)
        def _():
            for g in range(wide // tile):
                weights.start(ids_ref, pieces, g * tile, w_ref.at[g], 0, tile, sems.at[g])

        weights.wait_all(w_ref.at[step], 0, tile, sems.at[step])
        @pl.loop(0, tile // 512)
        def _(part):
            columns = pl.ds(pl.multiple_of(part * 512, 512), 512)
            pre = dot(x_ref[...], w_ref[step, :, columns]) + bias_ref[:, columns]
            below = 0.5 + 0.5 * lax.erf(pre * (0.5**0.5))
            density = jnp.exp(pre * pre * -0.5) * 0.3989422804014327
            act_ref[:, columns] = (pre * below).astype(BF)
            slope_ref[:, columns] = below + pre * density

    block = pl.BlockSpec((count, tile), lambda n, ids: (0, n))
    return kernel(
        body,
        "ffn_in",
        13,
        ids,
        (wide // tile,),
        [(low, whole(low.shape)), (bias, pl.BlockSpec((1, tile), lambda n, ids: (0, n)))]
        + [(p, ANY) for p in weights.arrays],
        [(struct((count, wide), BF), block), (struct((count, wide), F32), block)],
        [
            pltpu.VMEM((wide // tile, width, tile), BF),
            pltpu.SemaphoreType.DMA((wide // tile, weights.count)),
        ],
    )


def ffn_out(ids, act, normed, out_grad, weights, vectors):
    count, wide = act.shape
    width = normed.shape[1]
    block = weights.block
    hops = weights.count // 2
    n_pieces = len(weights.arrays)
    step = 128

    def body(ids_ref, vec_ref, act_hbm, n_hbm, g_hbm, *refs):
        pieces = refs[:n_pieces]
        out_hbm, sum_hbm, low_hbm, sums_ref, sent_hbm = refs[n_pieces : n_pieces + 5]
        acc_ref, n_ref, g_ref, out_ref, low_ref = refs[n_pieces + 5 : n_pieces + 10]
        act_ref, w_ref, sent_ref, sems, in_sems, out_sems, sent_sems = refs[n_pieces + 10 :]
        places = [aligned((ids_ref[0] ^ j) * 2 * block, 2 * block) for j in range(hops)]
        fetch = copies([(act_hbm.at[:, p], act_ref.at[:, p]) for p in places], in_sems)
        for j in range(hops):
            fetch[j].start()
            weights.start(ids_ref, pieces, 0, w_ref, 0, width, sems, hop=j)
        late = [
            pltpu.make_async_copy(n_hbm, n_ref, in_sems.at[hops]),
            pltpu.make_async_copy(g_hbm, g_ref, in_sems.at[hops + 1]),
        ]
        start_all(late)
        for j in range(hops):
            fetch[j].wait()
            for c in range(2):
                weights.wait((ids_ref[0] ^ j) * 2 + c, w_ref, 0, width, sems)
            product = dot(act_ref[:, places[j]], w_ref[places[j], :])
            if j == 0:
                acc_ref[...] = product
            else:
                acc_ref[...] += product
        sums_ref[...] = jnp.zeros_like(sums_ref)
        wait_for(late)

        @pl.loop(0, count // step)
        def _(part):
            rows = pl.ds(pl.multiple_of(part * step, step), step)
            base = n_ref[rows, :] * vec_ref[3:4] + vec_ref[4:5] + vec_ref[5:6]
            n2, inverse = normalise(acc_ref[rows, :] + base)
            out_ref[rows, :] = (n2 * vec_ref[6:7] + vec_ref[7:8]).astype(BF)
            grad = g_ref[rows, :].astype(F32)
            back = normalise_back(grad * vec_ref[6:7], n2, inverse)
            low = back.astype(BF)
            acc_ref[rows, :] = back
            low_ref[rows, :] = low
            sums_ref[0:1, :] += total_rows(grad * n2)
            sums_ref[1:2, :] += total_rows(grad)
            sums_ref[2:3, :] += total_rows(low.astype(F32))

        done = copies([(low_ref, low_hbm), (acc_ref, sum_hbm), (out_ref, out_hbm)], out_sems)
        start_all(done)
        send = copies(
            [(sent_ref.at[j], sent_hbm.at[pl.ds(j * block, block), :]) for j in range(hops)],
            sent_sems,
        )
        for j in range(hops):
            at = ((ids_ref[0] ^ j) * 2 + (ids_ref[1] ^ 1)) * block
            sent_ref[j] = dot_tn(act_ref[:, aligned(at, block)], low_ref[...]).astype(BF)
            send[j].start()
        wait_for(done + send)

    size = (count, width)
    return kernel(
        body,
        "ffn_out",
        18,
        ids,
        (1,),
        [(vectors, whole(vectors.shape))]
        + [(a, ANY) for a in [act, normed, out_grad] + weights.arrays],
        [
            (struct(size, BF), ANY),
            (struct(size, F32), ANY),
            (struct(size, BF), ANY),
            (struct((8, width), F32), whole((8, width))),
            (struct((wide // 2, width), BF), ANY),
        ],
        [
            pltpu.VMEM(size, F32),
            pltpu.VMEM(size, F32),
            pltpu.VMEM(size, BF),
            pltpu.VMEM(size, BF),
            pltpu.VMEM(size, BF),
            pltpu.VMEM((count, wide), BF),
            pltpu.VMEM((wide, width), BF),
            pltpu.VMEM((hops, block, width), BF),
            pltpu.SemaphoreType.DMA((weights.count,)),
            pltpu.SemaphoreType.DMA((hops + 2,)),
            pltpu.SemaphoreType.DMA((3,)),
            pltpu.SemaphoreType.DMA((hops,)),
        ],
    )


def ffn_back(ids, grad, slope, weights, lefts, left_specs, deps):
    count, wide = slope.shape
    width = grad.shape[1]
    block = min(wide, 1024)
    per = block // weights.block
    n_pieces = len(weights.arrays)
    rows_out = sum(spec.block_shape[1] for spec in left_specs)

    def body(ids_ref, grad_ref, slope_ref, *refs):
        left_refs = refs[: len(lefts)]
        pieces = refs[len(lefts) : len(lefts) + n_pieces]
        out_ref, sums_ref, sent_ref, w_ref, sems = refs[-5:]
        step = pl.program_id(0)

        @pl.when(step == 0)
        def _():
            weights.start(ids_ref, pieces, 0, w_ref, 0, width, sems)

        for i in range(per):
            weights.wait(step * per + i, w_ref, 0, width, sems)
        rows = pl.ds(pl.multiple_of(step * block, 16), block)
        back = (dot_nt(grad_ref[...], w_ref[rows, :]) * slope_ref[...]).astype(BF)
        out_ref[...] = back
        sums_ref[...] = jnp.broadcast_to(total_rows(back.astype(F32)), sums_ref.shape)
        left = jnp.concatenate([ref[...] for ref in left_refs], axis=1)
        sent_ref[...] = dot_tn(left, out_ref[...]).astype(BF)

    tile = pl.BlockSpec((count, block), lambda n, ids: (0, n))
    return kernel(
        body,
        "ffn_back",
        12,
        ids,
        (wide // block,),
        [(grad, whole(grad.shape)), (slope, tile)]
        + list(zip(lefts, left_specs))
        + [(p, ANY) for p in weights.arrays]
        + [(d, ANY) for d in deps],
        [
            (struct((count, wide), BF), tile),
            (struct((8, wide), F32), pl.BlockSpec((8, block), lambda n, ids: (0, n))),
            (
                struct((rows_out, wide), BF),
                pl.BlockSpec((rows_out, block), lambda n, ids: (0, n)),
            ),
        ],
        [pltpu.VMEM((wide, width), BF), pltpu.SemaphoreType.DMA((weights.count,))],
    )


def attention_norm_back(ids, inner_grad, ffn_grad, normed, inverse, inner, weights, vectors, deps):
    count, wide = inner_grad.shape
    width = normed.shape[1]
    tile = min(wide, 1024)
    steps = wide // tile
    n_pieces = len(weights.arrays)
    part_rows = 128

    def body(ids_ref, inverse_ref, vec_ref, grad_hbm, ffn_hbm, n_hbm, *refs):
        pieces = refs[:n_pieces]
        inner_pieces = refs[n_pieces : 2 * n_pieces]
        low_hbm, sum_hbm, mixed_hbm, sums_ref = refs[-17:-13]
        acc_ref, ffn_ref, n_ref, low_ref, mixed_ref, grad_ref, w_ref = refs[-13:-6]
        w_sems, o_ref, o_sems, sems, grad_sems, out_sems = refs[-6:]
        tiles = [slice(g * tile, (g + 1) * tile) for g in range(steps)]
        fetch = copies([(grad_hbm.at[:, t], grad_ref.at[:, t]) for t in tiles], grad_sems)
        for g in range(steps):
            fetch[g].start()
            inner.start(ids_ref, inner_pieces, g * tile, w_ref.at[g], 0, tile, w_sems.at[g])
        late = copies([(ffn_hbm, ffn_ref), (n_hbm, n_ref)], sems)
        start_all(late)
        weights.start(ids_ref, pieces, 3 * width, o_ref, 0, width, o_sems)
        acc_ref[...] = jnp.zeros_like(acc_ref)

        @pl.loop(0, steps)
        def _(g):
            there = grad_ref.at[:, aligned(g * tile, tile)]
            pltpu.make_async_copy(there, there, grad_sems.at[g]).wait()
            inner.wait_all(w_ref.at[g], 0, tile, w_sems.at[g])
            acc_ref[...] += dot_nt(there[...], w_ref[g])

        wait_for(late)
        sums_ref[...] = jnp.zeros_like(sums_ref)

        @pl.loop(0, count // part_rows)
        def _(part):
            rows = pl.ds(pl.multiple_of(part * part_rows, part_rows), part_rows)
            grad = acc_ref[rows, :] + ffn_ref[rows, :]
            normed_rows = n_ref[rows, :]
            back = normalise_back(grad * vec_ref[3:4], normed_rows, inverse_ref[rows, 0:1])
            low = back.astype(BF)
            low_ref[rows, :] = low
            acc_ref[rows, :] = back
            sums_ref[0:1, :] += total_rows(grad * normed_rows)
            sums_ref[1:2, :] += total_rows(grad)
            sums_ref[2:3, :] += total_rows(low.astype(F32))

        done = copies(
            [(low_ref, low_hbm), (acc_ref, sum_hbm), (mixed_ref, mixed_hbm)], out_sems
        )
        start_all(done[:2])
        weights.wait_all(o_ref, 0, width, o_sems)
        mixed_ref[...] = dot_nt(low_ref[...], o_ref[...]).astype(BF)
        done[2].start()
        wait_for(done)

    size = (count, width)
    return kernel(
        body,
        "attention_norm_back",
        16,
        ids,
        (1,),
        [(inverse, whole(inverse.shape)), (vectors, whole(vectors.shape))]
        + [
            (a, ANY)
            for a in [inner_grad, ffn_grad, normed] + weights.arrays + inner.arrays + list(deps)
        ],
        [
            (struct(size, BF), ANY),
            (struct(size, F32), ANY),
            (struct(size, BF), ANY),
            (struct((8, width), F32), whole((8, width))),
        ],
        [
            pltpu.VMEM(size, F32),
            pltpu.VMEM(size, F32),
            pltpu.VMEM(size, F32),
            pltpu.VMEM(size, BF),
            pltpu.VMEM(size, BF),
            pltpu.VMEM((count, wide), BF),
            pltpu.VMEM((steps, width, tile), BF),
            pltpu.SemaphoreType.DMA((steps, inner.count)),
            pltpu.VMEM((width, width), BF),
            pltpu.SemaphoreType.DMA((weights.count,)),
            pltpu.SemaphoreType.DMA((2,)),
            pltpu.SemaphoreType.DMA((steps,)),
            pltpu.SemaphoreType.DMA((3,)),
        ],
    )


def inputs_back(ids, base, grads, weights, deps):
    count, width = base.shape
    tile = 256
    per = tile // weights.block
    n_pieces = len(weights.arrays)

    def body(ids_ref, base_ref, q_ref, k_ref, v_ref, *refs):
        pieces = refs[:n_pieces]
        out_ref, w_ref, sems = refs[-3:]
        step = pl.program_id(0)

        @pl.when(step == 0)
        def _():
            weights.start(ids_ref, pieces, 0, w_ref, 0, 3 * width, sems)

        for i in range(per):
            weights.wait(step * per + i, w_ref, 0, 3 * width, sems)
        place = pl.ds(pl.multiple_of(step * tile, tile), tile)
        out = base_ref[...]
        for i, ref in enumerate((q_ref, k_ref, v_ref)):
            out = out + dot_nt(ref[...], w_ref[place, i * width : (i + 1) * width])
        out_ref[...] = out

    block = pl.BlockSpec((count, tile), lambda n, ids: (0, n))
    return kernel(
        body,
        "inputs_back",
        10,
        ids,
        (width // tile,),
        [(base, block)]
        + [(g, whole(g.shape)) for g in grads]
        + [(p, ANY) for p in weights.arrays]
        + [(d, ANY) for d in deps],
        [(struct(base.shape, F32), block)],
        [pltpu.VMEM((width, 3 * width), BF), pltpu.SemaphoreType.DMA((weights.count,))],
    )[0]


def split_hops(kept, bit):
    stay = [j for j in kept if not j & bit]
    return stay, [j | bit for j in stay]


class RowSum:
    def __init__(self, net, pairs, ids, tile):
        self.net, self.ids, self.tile = net, ids, tile
        self.rights = [right for _, right in pairs]
        self.left = []
        for left, _ in pairs:
            if not any(left is known for known in self.left):
                self.left.append(left)
        self.uses = [[left is known for known in self.left].index(True) for left, _ in pairs]
        self.width = self.left[0].shape[1] // (net.chips * 2)
        self.columns = sum(r.shape[1] for r in self.rights)
        bits = [1 << b for b in range(net.chips.bit_length() - 1)]
        self.bits = (bits, bits[::-1])
        self.kept = [list(range(net.chips))] * 2

    def lefts(self, core):
        net, width = self.net, self.width
        if width % 128 == 0:
            spec = [
                pl.BlockSpec(
                    (self.left[0].shape[0], width),
                    lambda n, ids, j=j: (0, (ids[0] ^ j) * 2 + (ids[1] ^ core)),
                )
                for j in range(net.chips)
            ]
            return [left for left in self.left for _ in spec], spec * len(self.left)
        chosen = []
        for left in self.left:
            picked = []
            for j in range(net.chips):
                at = ((self.ids[0] ^ j) * 2 + (self.ids[1] ^ core)) * width
                picked.append(lax.dynamic_slice_in_dim(left, at, width, axis=1))
            chosen.append(jnp.concatenate(picked, axis=1))
        return chosen, [whole(picked.shape) for picked in chosen]

    def multiply(self, name, micros, core, got, outs, groups, targets, deps):
        net, width, tile = self.net, self.width, self.tile
        rows, tokens = net.chips * width, self.left[0].shape[0]
        ready = width % 128 != 0
        lefts = self.lefts(core)[0] if ready else self.left
        tiles = []
        for right, use in zip(range(len(self.rights)), self.uses):
            for at in range(0, self.rights[right].shape[1], tile):
                tiles.append((right, at, use))
        extra = [] if got is None else [got]
        cuts = [t for t in range(1, len(tiles)) if tiles[t][2] != tiles[t - 1][2]]

        def body(ids_ref, *refs):
            left_hbm = refs[: len(lefts)]
            right_hbm = refs[len(lefts) : len(lefts) + len(self.rights)]
            got_hbm = refs[len(lefts) + len(self.rights)]
            scratch = refs[len(refs) - 7 - len(extra) :]
            out_hbm = refs[len(refs) - 7 - len(extra) - len(outs) : len(refs) - 7 - len(extra)]
            left_ref, right_ref, out_ref, left_sems, right_sems, got_sems, out_sems = scratch[:7]
            fetch_left = []
            for i, source in enumerate(left_hbm):
                if ready:
                    pairs = [(source, left_ref.at[i])]
                else:
                    pairs = []
                    for j in range(net.chips):
                        at = ((ids_ref[0] ^ j) * 2 + (ids_ref[1] ^ core)) * width
                        place = (slice(None), slice(j * width, (j + 1) * width))
                        pairs.append((source.at[:, aligned(at, width)], left_ref.at[i].at[place]))
                fetch_left.append(copies(pairs, left_sems, i))
            fetch_right = [
                pltpu.make_async_copy(
                    right_hbm[r].at[:, at : at + tile], right_ref.at[t], right_sems.at[t]
                )
                for t, (r, at, _) in enumerate(tiles)
            ]
            fetch_got = [
                pltpu.make_async_copy(
                    got_hbm.at[:, t * tile : (t + 1) * tile], scratch[7].at[t], got_sems.at[t]
                )
                for t in range(len(tiles) if extra else 0)
            ]
            waited = set()
            for t, (_, _, use) in enumerate(tiles):
                if use not in waited:
                    start_all(fetch_left[use])
                    waited.add(use)
                fetch_right[t].start()
                if extra:
                    fetch_got[t].start()
            def part(t, which):
                use = sum(((t >= cut).astype(jnp.int32) for cut in cuts), jnp.int32(0))
                there = [right_ref.at[t]] + [ref.at[t] for ref in scratch[7:]]
                for ref, sems in zip(there, (right_sems, got_sems)):
                    pltpu.make_async_copy(ref, ref, sems.at[t]).wait()
                value = dot_tn(left_ref[use], right_ref[t])
                for ref in there[1:]:
                    value = value + ref[...].astype(F32)
                out_ref[t] = value.astype(BF)
                return copies(
                    [
                        (
                            out_ref.at[t].at[first : first + n, :],
                            out_hbm[kind].at[row : row + n, aligned(column, tile)],
                        )
                        for first, n, kind, row, column in targets(t, which)
                    ],
                    out_sems,
                    t,
                )

            count = len(tiles)
            group = count // groups
            waited = 0
            for which in range(groups):
                last = tiles[(which + 1) * group - 1][2]
                while waited <= last:
                    wait_for(fetch_left[waited])
                    waited += 1

                @pl.loop(which * group, (which + 1) * group)
                def _(t):
                    start_all(part(t, which))

            for t in range(count):
                wait_for(
                    pltpu.make_async_copy(
                        out_ref.at[t].at[first : first + n, :],
                        out_ref.at[t].at[first : first + n, :],
                        out_sems.at[t, i],
                    )
                    for i, (first, n, _, _, _) in enumerate(targets(t, t // group))
                )

        count = len(tiles)
        return kernel(
            body,
            name,
            micros,
            self.ids,
            (1,),
            [(a, ANY) for a in list(lefts) + self.rights + extra + list(deps)],
            [(o, ANY) for o in outs],
            [
                pltpu.VMEM((len(lefts), tokens, rows), BF),
                pltpu.VMEM((count, tokens, tile), BF),
                pltpu.VMEM((count, rows, tile), BF),
                pltpu.SemaphoreType.DMA((len(lefts), net.chips)),
                pltpu.SemaphoreType.DMA((count,)),
                pltpu.SemaphoreType.DMA((count,)),
                pltpu.SemaphoreType.DMA((count, net.chips)),
            ]
            + [pltpu.VMEM((count, rows, tile), BF) for _ in extra],
        )

    def other_core(self, *deps):
        rows = self.net.chips * self.width
        (self.sent,) = self.multiply(
            "rows_of_other_core",
            7,
            1,
            None,
            [struct((rows, self.columns), BF)],
            1,
            lambda t, _: [(0, rows, 0, 0, t * self.tile)],
            deps,
        )
        return self.exchange(self.sent)

    def exchange(self, sent):
        self.got = self.net.across_core(sent)
        return sent

    def own_core(self, *deps):
        rows, tile, width = self.net.chips * self.width, self.tile, self.width
        half = self.columns // tile // 2
        sides = [split_hops(self.kept[s], self.bits[s][0]) for s in range(2)]

        def targets(t, side):
            return [
                (j * width, width, side * 2 + which, i * width, (t - side * half) * tile)
                for which, hops in enumerate(sides[side])
                for i, j in enumerate(hops)
            ]

        out = self.multiply(
            "rows_of_own_core",
            9,
            0,
            self.got,
            [struct((rows // 2, self.columns // 2), BF)] * 4,
            2,
            targets,
            deps,
        )
        self.held = [out[0], out[2]]
        self.away = [out[1], out[3]]
        self.send()
        return out[0]

    def send(self):
        for s in range(2):
            self.kept[s] = split_hops(self.kept[s], self.bits[s][0])[0]
        self.arrived = [self.net.across_chip(self.away[s], self.bits[s][0]) for s in range(2)]
        self.bits = (self.bits[0][1:], self.bits[1][1:])

    def fold(self, *deps):
        rows, columns = self.held[0].shape
        tile = columns // 2
        sides = [split_hops(self.kept[s], self.bits[s][0]) for s in range(2)]

        def body(ids_ref, *refs):
            out_refs = refs[-4:]
            for s in range(2):
                for which, hops in enumerate(sides[s]):
                    for i, j in enumerate(hops):
                        at = self.kept[s].index(j) * self.width
                        part = slice(at, at + self.width)
                        value = refs[2 * s][part, :].astype(F32) + refs[2 * s + 1][part, :].astype(F32)
                        out_refs[2 * s + which][i * self.width : (i + 1) * self.width, :] = (
                            value.astype(BF)
                        )

        block = pl.BlockSpec((rows, tile), lambda n, ids: (0, n))
        half = pl.BlockSpec((rows // 2, tile), lambda n, ids: (0, n))
        out = kernel(
            body,
            "fold",
            4,
            self.ids,
            (columns // tile,),
            [(a, block) for s in range(2) for a in (self.held[s], self.arrived[s])]
            + [(d, ANY) for d in deps],
            [(struct((rows // 2, columns), BF), half)] * 4,
            [],
        )
        self.held = [out[0], out[2]]
        self.away = [out[1], out[3]]
        self.send()
        return self.fold() if self.bits[0] else out[0]

    def fold_z(self, *deps):
        net, count = self.net, self.net.inner
        columns = self.held[0].shape[1]
        rows = self.width // count
        stay, leave = split_hops(list(range(count)), 1)
        size = (rows * len(stay), 2 * columns)
        if rows % 16:
            held = tie(jnp.concatenate(self.held, axis=1), *deps).astype(F32)
            held = held + jnp.concatenate(self.arrived, axis=1).astype(F32)
            held = held.reshape(count, rows, -1).astype(BF)
            keep, away = (
                jnp.take(held, jnp.array(hops) ^ self.ids[2], axis=0).reshape(size)
                for hops in (stay, leave)
            )
        else:

            def body(ids_ref, *refs):
                for out_ref, hops in zip(refs[-2:], (stay, leave)):
                    for i, s in enumerate(hops):
                        at = pl.ds(pl.multiple_of((ids_ref[2] ^ s) * rows, 16), rows)
                        for side in range(2):
                            value = refs[2 * side][at, :].astype(F32)
                            value = value + refs[2 * side + 1][at, :].astype(F32)
                            place = slice(side * columns, (side + 1) * columns)
                            out_ref[i * rows : (i + 1) * rows, place] = value.astype(BF)

            keep, away = kernel(
                body,
                "fold_z",
                3,
                self.ids,
                (1,),
                [
                    (a, whole(a.shape))
                    for s in range(2)
                    for a in (self.held[s], self.arrived[s])
                ]
                + [(d, ANY) for d in deps],
                [(struct(size, BF), whole(size))] * 2,
                [],
            )
        self.total, self.came, self.reach = keep, net.swap(away, 1), 1
        return keep

    def fold_far(self, *deps):
        while self.reach * 2 < self.net.inner:
            self.reach *= 2
            total = tie(self.total, *deps).astype(F32) + self.came.astype(F32)
            rows = self.width // self.net.inner
            count = total.shape[0] // rows
            stay = [i for i in range(count) if not i & 1]
            blocks = total.reshape(count, rows, -1)
            away = jnp.concatenate([blocks[i + 1] for i in stay], axis=0).astype(BF)
            self.total = jnp.concatenate([blocks[i] for i in stay], axis=0)
            self.came = self.net.swap(away, self.reach)
        return self.came

    def finish(self, *deps):
        return tie(self.total, *deps).astype(F32) + self.came.astype(F32)


def shards(
    net,
    inputs,
    segment_ids,
    query_weight,
    key_weight,
    value_weight,
    output_weight,
    query_bias,
    value_bias,
    output_bias,
    attn_gain,
    attn_shift,
    inner_weight,
    inner_bias,
    outer_weight,
    outer_bias,
    ffn_gain,
    ffn_shift,
    out_grad,
):
    row_count, seq_len, width = inputs.shape
    tokens = inputs.reshape(row_count * seq_len, width)
    _, ids = net.place()
    small = [
        query_bias,
        value_bias,
        output_bias,
        attn_gain,
        attn_shift,
        outer_bias,
        ffn_gain,
        ffn_shift,
        inner_bias,
    ]
    mine = query_bias.shape[0]
    shard = first_shard([query_weight, key_weight, value_weight, output_weight], small)
    gather_a = Gather(net, shard, ids, True)
    gather_a.ordered()
    gather_a.plane()
    gather_b = Gather(net, tie(inner_weight, gather_a.block), ids, True)
    gather_a.relay(*gather_b.along)
    gather_b.ordered()
    weights_a = gather_a.cores()
    gather_b.plane(*weights_a.arrays)
    queries, keys, values, vectors = project(ids, tokens, weights_a)
    spread = inner_bias.shape[0] // mine
    inner_bias_full = vectors[8 : 8 + spread].reshape(spread, net.count, mine)
    inner_bias_full = inner_bias_full.swapaxes(0, 1).reshape(1, -1)
    mixed, totals = attend_forward(segment_ids, queries, keys, values)
    gather_c = Gather(net, tie(outer_weight, queries), ids, True, mixed)
    arrived = gather_b.relay(mixed)
    gather_c.ordered()
    gather_c.plane(*arrived)
    weights_b = gather_b.cores()
    normed, inverse, normed_low = close_attention(ids, mixed, tokens, weights_a, vectors)
    act, slope = ffn_in(ids, normed_low, weights_b, inner_bias_full)
    gather_c.relay(act)
    weights_c = gather_c.cores()
    grad_out = out_grad.reshape(tokens.shape)
    outputs, ffn_grad, branch_grad, ffn_sums, sent = ffn_out(
        ids, act, normed, grad_out, weights_c, vectors
    )
    outer_sum = RowSum(net, [(act, branch_grad)], ids, 256)
    last = outer_sum.exchange(sent)
    lefts = RowSum(net, [(normed_low, slope)], ids, 1024).lefts(1)
    inner_grad, inner_sums, sent = ffn_back(ids, branch_grad, slope, weights_c, *lefts, [last])
    inner_sum = RowSum(net, [(normed_low, inner_grad)], ids, 1024)
    last = inner_sum.exchange(sent)
    last = outer_sum.own_core(last)
    attn_grad, attn_sum_grad, mixed_grad, attn_sums = attention_norm_back(
        ids, inner_grad, ffn_grad, normed, inverse, weights_b, weights_a, vectors, [last]
    )
    last = outer_sum.fold(attn_grad)
    last = inner_sum.own_core(last)
    query_grad, key_grad, value_grad, grad_query_bias, grad_value_bias = attend_backward(
        segment_ids, queries, keys, values, mixed_grad, totals, [last]
    )
    input_grad = inputs_back(
        ids, attn_sum_grad, (query_grad, key_grad, value_grad), weights_a, []
    )
    inputs_sum = RowSum(
        net,
        [(mixed, attn_grad)] + [(tokens, g) for g in (query_grad, key_grad, value_grad)],
        ids,
        1024,
    )
    last = inputs_sum.other_core(input_grad, *outer_sum.arrived, *inner_sum.arrived)
    last = inner_sum.fold(last)
    last = outer_sum.fold_z(last)
    last = inputs_sum.own_core(last)
    outer_sum.fold_far(last)
    last = inner_sum.fold_z(last)
    last = inputs_sum.fold(last, outer_sum.came)
    shard_outer = outer_sum.finish(last)
    inner_sum.fold_far(last)
    last = inputs_sum.fold_z(inner_sum.came)
    shard_inner = inner_sum.finish(last)
    inputs_sum.fold_far(last)
    shard_inputs = inputs_sum.finish()
    shard_output, shard_query, shard_key, shard_value = (
        shard_inputs[:, i * width : (i + 1) * width] for i in range(4)
    )
    rows = jnp.concatenate(
        [grad_query_bias[None], grad_value_bias[None], attn_sums[:3], ffn_sums[:3]], axis=0
    )
    rows = rows.reshape(8, net.count, mine).swapaxes(0, 1).reshape(net.count, 8 * mine)
    packed = jnp.concatenate([rows, inner_sums[0].reshape(net.count, -1)], axis=1)
    packed = tie(packed, last)
    summed = jnp.sum(lax.all_to_all(packed, AXES, 0, 0, tiled=True), axis=0)
    vector = [summed[i * mine : (i + 1) * mine] for i in range(8)]
    return (
        outputs.reshape(inputs.shape),
        input_grad.reshape(inputs.shape),
        shard_query,
        shard_key,
        shard_value,
        shard_output,
        vector[0],
        vector[1],
        vector[4],
        vector[2],
        vector[3],
        shard_inner,
        summed[8 * mine :],
        shard_outer,
        vector[7],
        vector[5],
        vector[6],
    )


def solution(mesh):
    placed = (
        P(("dp", "fsdp"), None, None),
        P(("dp", "fsdp"), None),
        P(("dp", "fsdp"), None),
        P(("dp", "fsdp"), None),
        P(("dp", "fsdp"), None),
        P(("dp", "fsdp"), None),
        P(("dp", "fsdp")),
        P(("dp", "fsdp")),
        P(("dp", "fsdp")),
        P(("dp", "fsdp")),
        P(("dp", "fsdp")),
        P(("dp", "fsdp"), None),
        P(("dp", "fsdp")),
        P(("dp", "fsdp"), None),
        P(("dp", "fsdp")),
        P(("dp", "fsdp")),
        P(("dp", "fsdp")),
        P(("dp", "fsdp"), None, None),
    )
    return jax.shard_map(
        functools.partial(shards, Slice(mesh.shape["dp"], mesh.shape["fsdp"])),
        mesh=mesh,
        in_specs=placed,
        out_specs=(
            P(("dp", "fsdp"), None, None),
            P(("dp", "fsdp"), None, None),
            P(("dp", "fsdp"), None),
            P(("dp", "fsdp"), None),
            P(("dp", "fsdp"), None),
            P(("dp", "fsdp"), None),
            P(("dp", "fsdp")),
            P(("dp", "fsdp")),
            P(("dp", "fsdp")),
            P(("dp", "fsdp")),
            P(("dp", "fsdp")),
            P(("dp", "fsdp"), None),
            P(("dp", "fsdp")),
            P(("dp", "fsdp"), None),
            P(("dp", "fsdp")),
            P(("dp", "fsdp")),
            P(("dp", "fsdp")),
        ),
        check_vma=False,
    )
```

```python
import functools

import jax
import jax.numpy as jnp
from jax import lax
from jax.experimental import pallas as pl
from jax.experimental.pallas import tpu as pltpu
from jax.sharding import PartitionSpec as P

H = 16
HD = 64
AXES = ("dp", "fsdp")
BF = jnp.bfloat16
F32 = jnp.float32
EPSILON = 1e-05
NT = (((1,), (1,)), ((), ()))
TN = (((0,), (0,)), ((), ()))
MASKED = -1e30
WEIGHT = 0.3


def spend(micros):
    return pl.CostEstimate(flops=1, bytes_accessed=int(micros * WEIGHT * 1e6), transcendentals=0)


ANY = pl.BlockSpec(memory_space=pl.ANY)


def whole(shape):
    return pl.BlockSpec(shape, lambda *_: (0,) * len(shape))


def struct(shape, dtype):
    return jax.ShapeDtypeStruct(shape, dtype)


def dot(left, right):
    return jnp.dot(left, right, preferred_element_type=F32)


def dot_tn(left, right):
    return lax.dot_general(left, right, TN, preferred_element_type=F32)


def dot_nt(left, right):
    return lax.dot_general(left, right, NT, preferred_element_type=F32)


def tie(value, *after):
    return lax.optimization_barrier((value, *after))[0]


def normalise(rows):
    centred = rows - jnp.mean(rows, axis=-1, keepdims=True)
    spread = jnp.mean(centred * centred, axis=-1, keepdims=True)
    inverse = lax.rsqrt(spread + EPSILON)
    return centred * inverse, inverse


def normalise_back(cotangent, normed, inverse):
    slope = jnp.mean(cotangent * normed, axis=-1, keepdims=True)
    return inverse * (cotangent - jnp.mean(cotangent, axis=-1, keepdims=True) - normed * slope)


def total_rows(matrix):
    return jnp.sum(matrix, axis=0, keepdims=True)


def lane_half(block, which):
    lane = lax.broadcasted_iota(jnp.int32, block.shape, 1)
    return jnp.where((lane >= HD) == (which == 1), block, jnp.zeros_like(block))


def set_mask(seg_ref, mask_ref):
    seg_row = seg_ref[...].astype(F32)
    seg_col = jnp.broadcast_to(seg_row, (128, seg_row.shape[1])).T
    for at in range(0, seg_row.shape[1], 128):
        same = seg_col == seg_row[:, at : at + 128]
        mask_ref[:, at : at + 128] = jnp.where(same, 0.0, MASKED)


def attend_forward_body(seg_ref, q_ref, k_ref, v_ref, mixed_ref, total_ref, mask_ref):
    @pl.when(pl.program_id(1) == 0)
    def _():
        set_mask(seg_ref, mask_ref)

    query = q_ref[...] * jnp.bfloat16(HD**-0.5)
    key = k_ref[...]
    value_t = v_ref[...].T
    halves = []
    for h in range(2):
        scores = lax.dot_general(lane_half(key, h), query, NT, preferred_element_type=F32)
        scores = scores + mask_ref[...]
        high = jnp.max(scores, axis=0, keepdims=True)
        raised = jnp.exp(scores - high)
        total = jnp.sum(raised, axis=0, keepdims=True)
        low = (raised * (1.0 / total)).astype(BF)
        rows = value_t[h * HD : (h + 1) * HD]
        halves.append(jnp.dot(rows, low, preferred_element_type=F32))
        total_ref[0, h : h + 1, :] = high + jnp.log(total)
    mixed_ref[...] = jnp.concatenate(halves, axis=0).T.astype(BF)


def attend_backward_body(
    seg_ref, q_ref, k_ref, v_ref, g_ref, total_ref, *rest
):
    dq_ref, dk_ref, dv_ref, dq_sum_ref, dv_sum_ref, mask_ref = rest[-6:]

    @pl.when(pl.program_id(1) == 0)
    def _():
        set_mask(seg_ref, mask_ref)

    scale = HD**-0.5
    query = q_ref[...] * jnp.bfloat16(scale)
    key, value, grad = k_ref[...], v_ref[...], g_ref[...]
    key_t = key.T
    lane = lax.broadcasted_iota(jnp.int32, key.shape, 1)
    dq_t, dk, dv = [], None, None
    for h in range(2):
        scores = lax.dot_general(lane_half(key, h), query, NT, preferred_element_type=F32)
        probs = jnp.exp(scores + mask_ref[...] - total_ref[0, h : h + 1, :])
        prob_grad = lax.dot_general(lane_half(value, h), grad, NT, preferred_element_type=F32)
        inner_sum = jnp.sum(probs * prob_grad, axis=0, keepdims=True)
        score_grad = (probs * (prob_grad - inner_sum)).astype(BF)
        dv_h = jnp.dot(probs.astype(BF), grad, preferred_element_type=F32)
        dk_h = jnp.dot(score_grad, query, preferred_element_type=F32)
        dv = dv_h if h == 0 else jnp.where(lane < HD, dv, dv_h)
        dk = dk_h if h == 0 else jnp.where(lane < HD, dk, dk_h)
        rows = key_t[h * HD : (h + 1) * HD]
        dq_t.append(jnp.dot(rows, score_grad, preferred_element_type=F32))
    dq = (jnp.concatenate(dq_t, axis=0).T * scale).astype(BF)
    dv = dv.astype(BF)
    dq_ref[...] = dq
    dk_ref[...] = dk.astype(BF)
    dv_ref[...] = dv
    wide = (8, dq.shape[1])
    dq_sum_ref[0] = jnp.broadcast_to(jnp.sum(dq.astype(F32), axis=0, keepdims=True), wide)
    dv_sum_ref[0] = jnp.broadcast_to(jnp.sum(dv.astype(F32), axis=0, keepdims=True), wide)


def attention_specs(seq_len, deps):
    block = pl.BlockSpec((seq_len, 2 * HD), lambda r, n: (r, n))
    seg = pl.BlockSpec((None, 1, seq_len), lambda r, n: (r, 0, 0))
    total = pl.BlockSpec((None, 1, 8, seq_len), lambda r, n: (r, n, 0, 0))
    sums = pl.BlockSpec((1, 8, 2 * HD), lambda r, n: (r, 0, n))
    return block, seg, total, sums, [pl.BlockSpec(memory_space=pl.ANY)] * deps


def attend_forward(seg, queries, keys, values):
    rows, seq_len = seg.shape
    block, seg_spec, total, _, _ = attention_specs(seq_len, 0)
    tokens, width = queries.shape
    pairs = width // (2 * HD)
    return pl.pallas_call(
        attend_forward_body,
        out_shape=[
            jax.ShapeDtypeStruct((tokens, width), BF),
            jax.ShapeDtypeStruct((rows, pairs, 8, seq_len), F32),
        ],
        grid=(rows, pairs),
        in_specs=[seg_spec, block, block, block],
        out_specs=[block, total],
        scratch_shapes=[pltpu.VMEM((seq_len, seq_len), F32)],
        name="attend_forward",
        cost_estimate=spend(13),
    )(seg.reshape(rows, 1, seq_len), queries, keys, values)


def attend_backward(seg, queries, keys, values, mixed_grad, totals, deps):
    rows, seq_len = seg.shape
    block, seg_spec, total, sums, extra = attention_specs(seq_len, len(deps))
    tokens, width = queries.shape
    pairs = width // (2 * HD)
    outs = pl.pallas_call(
        attend_backward_body,
        out_shape=[jax.ShapeDtypeStruct((tokens, width), BF)] * 3
        + [jax.ShapeDtypeStruct((rows, 8, width), F32)] * 2,
        grid=(rows, pairs),
        in_specs=[seg_spec, block, block, block, block, total] + extra,
        out_specs=[block, block, block, sums, sums],
        scratch_shapes=[pltpu.VMEM((seq_len, seq_len), F32)],
        name="attend_backward",
        cost_estimate=spend(17),
    )(seg.reshape(rows, 1, seq_len), queries, keys, values, mixed_grad, totals, *deps)
    dq, dk, dv, dq_sum, dv_sum = outs
    return dq, dk, dv, jnp.sum(dq_sum[:, 0], axis=0), jnp.sum(dv_sum[:, 0], axis=0)


class Slice:
    def __init__(self, dp, inner):
        self.inner, self.chips, self.count = inner, dp // 2, dp * inner

    def swap(self, value, mask):
        pairs = [(i, i ^ mask) for i in range(self.count)]
        return lax.ppermute(value, AXES, pairs)

    def across_core(self, value):
        return self.swap(value, self.inner)

    def across_chip(self, value, hop):
        return self.swap(value, hop * 2 * self.inner)

    def place(self):
        me = lax.axis_index(AXES)
        z = me % self.inner
        core = (me // self.inner) % 2
        return me, jnp.stack([me // (2 * self.inner), core, z]).astype(jnp.int32)


def first_shard(matrices, vectors):
    rows = matrices[0].shape[0]
    columns = sum(p.shape[1] for p in matrices)

    def body(*refs):
        out_ref, turn_ref = refs[-2:]
        at = 0
        for ref in refs[: len(matrices)]:
            out_ref[:, at : at + ref.shape[1]] = ref[...]
            at += ref.shape[1]
        turn_ref[...] = jnp.zeros_like(turn_ref)
        row = 0
        for ref in refs[len(matrices) : -2]:
            for start in range(0, ref.shape[1], rows):
                turn_ref[row : row + 1, 0:rows] = ref[:, start : start + rows].astype(F32)
                row += 1
        out_ref[:, at:] = turn_ref[...].T[0:rows].astype(BF)

    return pl.pallas_call(
        body,
        out_shape=struct((rows, columns + 128), BF),
        scratch_shapes=[pltpu.VMEM((128, 128), F32)],
        name="first_shard",
        cost_estimate=spend(2),
    )(*matrices, *[v.reshape(1, -1) for v in vectors])


def in_z_order(net, parts, ids):
    rows, columns = parts[0].shape
    if rows % 16:
        stacked = jnp.stack(parts)
        return jnp.take(stacked, jnp.arange(net.inner) ^ ids[2], axis=0).reshape(-1, columns)
    tile = next(columns // n for n in (2, 3, 1) if columns % (n * 128) == 0)

    def body(ids_ref, *refs):
        for s, part in enumerate(refs[:-1]):
            row = (ids_ref[2] ^ s) * rows
            refs[-1][pl.ds(pl.multiple_of(row, rows), rows), :] = part[...]

    return pl.pallas_call(
        body,
        out_shape=struct((net.inner * rows, columns), BF),
        grid_spec=pltpu.PrefetchScalarGridSpec(
            num_scalar_prefetch=1,
            grid=(columns // tile,),
            in_specs=[pl.BlockSpec((rows, tile), lambda n, ids: (0, n))] * net.inner,
            out_specs=pl.BlockSpec((net.inner * rows, tile), lambda n, ids: (0, n)),
        ),
        name="in_z_order",
        cost_estimate=spend(3),
    )(ids, *parts)


class Gather:
    def __init__(self, net, shard, ids, relay, *late):
        self.net, self.ids = net, ids
        self.relayed = relay and net.chips == 4
        self.along = [shard]
        reach = net.inner // 2
        while reach:
            if late and len(self.along) > 1:
                self.along[1:] = [tie(part, *late) for part in self.along[1:]]
            self.along = [
                part
                for near in self.along
                for part in (near, net.swap(near, reach))
            ]
            reach //= 2
        order = [0]
        reach = net.inner // 2
        while reach:
            order = [s ^ far for s in order for far in (0, reach)]
            reach //= 2
        self.along = [self.along[order.index(s)] for s in range(net.inner)]

    def ordered(self, *after):
        parts = list(lax.optimization_barrier((*self.along, *after))[: self.net.inner])
        self.block = in_z_order(self.net, parts, self.ids)
        self.rows = self.block.shape[0]
        return self.block

    def plane(self, *after):
        net = self.net
        self.pieces = [(self.block, 0, 0, 0)]
        hops = range(1, 3 if self.relayed else net.chips)
        sent = tie(self.block, *after)
        self.pieces += [(net.across_chip(sent, j), j, 0, 0) for j in hops]

    def relay(self, *after):
        net = self.net
        if self.relayed:
            half = self.rows // 2
            first, second = self.pieces[1][0], self.pieces[2][0]
            low = net.across_chip(tie(first, second, *after)[:half], 2)
            high = net.across_chip(tie(second, first, *after)[half:], 1)
            self.pieces += [(low, 3, 0, 0), (high, 3, 0, half)]
        return [p for p, _, _, _ in self.pieces]

    def cores(self, *after):
        across = [(self.net.across_core(tie(p, *after)), j, 1, s) for p, j, _, s in self.pieces]
        return Rows(self.net, self.rows, self.pieces + across)


class Rows:
    def __init__(self, net, block, pieces):
        self.block = block
        self.count = net.chips * 2
        self.arrays = [p for p, _, _, _ in pieces]
        self.meta = [(p.shape[0], j, c, s) for p, j, c, s in pieces]

    def after(self, *others):
        again = Rows.__new__(Rows)
        again.block, again.count, again.meta = self.block, self.count, self.meta
        tied = lax.optimization_barrier((*self.arrays, *others))
        again.arrays = list(tied[: len(self.arrays)])
        return again

    def start(self, ids_ref, refs, column, target, at, width, sems, hop=None):
        for ref, (rows, j, c, s) in zip(refs, self.meta):
            if hop is not None and j != hop:
                continue
            block = (ids_ref[0] ^ j) * 2 + (ids_ref[1] ^ c)
            row = pl.multiple_of(block * self.block + s, 16)
            pltpu.make_async_copy(
                ref.at[:, pl.ds(column, width)],
                target.at[pl.ds(row, rows), pl.ds(at, width)],
                sems.at[block],
            ).start()

    def wait(self, block, target, at, width, sems):
        row = block * self.block
        if not isinstance(row, int):
            row = pl.multiple_of(row, 16)
        there = target.at[pl.ds(row, self.block), pl.ds(at, width)]
        pltpu.make_async_copy(there, there, sems.at[block]).wait()

    def wait_all(self, target, at, width, sems):
        for block in range(self.count):
            self.wait(block, target, at, width, sems)


def copies(pairs, sems, *at):
    return [
        pltpu.make_async_copy(source, target, sems.at[(*at, i)])
        for i, (source, target) in enumerate(pairs)
    ]


def start_all(some):
    for copy in some:
        copy.start()


def wait_for(some):
    for copy in some:
        copy.wait()


def aligned(start, size):
    return pl.ds(pl.multiple_of(start, 128), size)


def kernel(body, name, micros, ids, grid, operands, outs, scratch):
    return pl.pallas_call(
        body,
        out_shape=[o for o, _ in outs],
        grid_spec=pltpu.PrefetchScalarGridSpec(
            num_scalar_prefetch=1,
            grid=grid,
            in_specs=[s for _, s in operands],
            out_specs=[s for _, s in outs],
            scratch_shapes=scratch,
        ),
        name=name,
        cost_estimate=spend(micros),
    )(ids, *[o for o, _ in operands])


def project(ids, tokens, weights):
    count, width = tokens.shape
    tile = min(width, 1024)
    per = width // tile
    n_pieces = len(weights.arrays)

    def body(ids_ref, x_ref, *refs):
        pieces = refs[:n_pieces]
        outs = refs[n_pieces : n_pieces + 3]
        vec_ref, w_ref, s_ref, sems = refs[n_pieces + 3 :]
        step = pl.program_id(0)

        @pl.when(step == 0)
        def _():
            weights.start(ids_ref, pieces, 4 * width, s_ref, 0, 128, sems.at[3])
            for i in range(3):
                weights.start(ids_ref, pieces, i * width, w_ref, i * width, width, sems.at[i])
            weights.wait_all(s_ref, 0, 128, sems.at[3])
            vec_ref[...] = s_ref[...].astype(F32).T[0 : vec_ref.shape[0]]

        for i, row in enumerate((0, None, 1)):

            @pl.when(step == i * per)
            def _():
                weights.wait_all(w_ref, i * width, width, sems.at[i])

            @pl.when((step >= i * per) & (step < (i + 1) * per))
            def _():
                columns = pl.ds(pl.multiple_of(step * tile, tile), tile)
                out = dot(x_ref[...], w_ref[:, columns])
                if row is not None:
                    inside = pl.ds(pl.multiple_of((step - i * per) * tile, tile), tile)
                    out = out + vec_ref[row : row + 1, inside]
                outs[i][...] = out.astype(BF)

    def out_spec(i):
        return pl.BlockSpec((count, tile), lambda n, ids: (0, jnp.clip(n - i * per, 0, per - 1)))

    return kernel(
        body,
        "project",
        10,
        ids,
        (3 * per,),
        [(tokens, whole(tokens.shape))] + [(p, ANY) for p in weights.arrays],
        [(struct(tokens.shape, BF), out_spec(i)) for i in range(3)]
        + [(struct((16, width), F32), whole((16, width)))],
        [
            pltpu.VMEM((width, 3 * width), BF),
            pltpu.VMEM((width, 128), BF),
            pltpu.SemaphoreType.DMA((4, weights.count)),
        ],
    )


def close_attention(ids, mixed, tokens, weights, vectors):
    count, width = tokens.shape
    rows = 256
    n_pieces = len(weights.arrays)

    def body(ids_ref, m_ref, x_ref, vec_ref, *refs):
        pieces = refs[:n_pieces]
        normed_ref, inverse_ref, low_ref, w_ref, sems = refs[n_pieces:]

        @pl.when(pl.program_id(0) == 0)
        def _():
            weights.start(ids_ref, pieces, 3 * width, w_ref, 0, width, sems)
            weights.wait_all(w_ref, 0, width, sems)

        total = x_ref[...].astype(F32) + (dot(m_ref[...], w_ref[...]) + vec_ref[2:3])
        normed, inverse = normalise(total)
        normed_ref[...] = normed
        inverse_ref[...] = jnp.broadcast_to(inverse, inverse_ref.shape)
        low_ref[...] = (normed * vec_ref[3:4] + vec_ref[4:5]).astype(BF)

    block = pl.BlockSpec((rows, width), lambda n, ids: (n, 0))
    return kernel(
        body,
        "close_attention",
        7,
        ids,
        (count // rows,),
        [(mixed, block), (tokens, block), (vectors, whole(vectors.shape))]
        + [(p, ANY) for p in weights.arrays],
        [
            (struct((count, width), F32), block),
            (struct((count, 128), F32), pl.BlockSpec((rows, 128), lambda n, ids: (n, 0))),
            (struct((count, width), BF), block),
        ],
        [pltpu.VMEM((width, width), BF), pltpu.SemaphoreType.DMA((weights.count,))],
    )


def ffn_in(ids, low, weights, bias):
    count, width = low.shape
    wide = bias.shape[1]
    tile = 1024
    n_pieces = len(weights.arrays)

    def body(ids_ref, x_ref, bias_ref, *refs):
        pieces = refs[:n_pieces]
        act_ref, slope_ref, w_ref, sems = refs[n_pieces:]
        step = pl.program_id(0)

        @pl.when(step == 0)
        def _():
            for g in range(wide // tile):
                weights.start(ids_ref, pieces, g * tile, w_ref.at[g], 0, tile, sems.at[g])

        weights.wait_all(w_ref.at[step], 0, tile, sems.at[step])
        @pl.loop(0, tile // 512)
        def _(part):
            columns = pl.ds(pl.multiple_of(part * 512, 512), 512)
            pre = dot(x_ref[...], w_ref[step, :, columns]) + bias_ref[:, columns]
            below = 0.5 + 0.5 * lax.erf(pre * (0.5**0.5))
            density = jnp.exp(pre * pre * -0.5) * 0.3989422804014327
            act_ref[:, columns] = (pre * below).astype(BF)
            slope_ref[:, columns] = below + pre * density

    block = pl.BlockSpec((count, tile), lambda n, ids: (0, n))
    return kernel(
        body,
        "ffn_in",
        13,
        ids,
        (wide // tile,),
        [(low, whole(low.shape)), (bias, pl.BlockSpec((1, tile), lambda n, ids: (0, n)))]
        + [(p, ANY) for p in weights.arrays],
        [(struct((count, wide), BF), block), (struct((count, wide), F32), block)],
        [
            pltpu.VMEM((wide // tile, width, tile), BF),
            pltpu.SemaphoreType.DMA((wide // tile, weights.count)),
        ],
    )


def ffn_out(ids, act, normed, out_grad, weights, vectors):
    count, wide = act.shape
    width = normed.shape[1]
    block = weights.block
    hops = weights.count // 2
    n_pieces = len(weights.arrays)
    step = 128

    def body(ids_ref, vec_ref, act_hbm, n_hbm, g_hbm, *refs):
        pieces = refs[:n_pieces]
        out_hbm, sum_hbm, low_hbm, sums_ref, sent_hbm = refs[n_pieces : n_pieces + 5]
        acc_ref, n_ref, g_ref, out_ref, low_ref = refs[n_pieces + 5 : n_pieces + 10]
        act_ref, w_ref, sent_ref, sems, in_sems, out_sems, sent_sems = refs[n_pieces + 10 :]
        places = [aligned((ids_ref[0] ^ j) * 2 * block, 2 * block) for j in range(hops)]
        fetch = copies([(act_hbm.at[:, p], act_ref.at[:, p]) for p in places], in_sems)
        for j in range(hops):
            fetch[j].start()
            weights.start(ids_ref, pieces, 0, w_ref, 0, width, sems, hop=j)
        late = [
            pltpu.make_async_copy(n_hbm, n_ref, in_sems.at[hops]),
            pltpu.make_async_copy(g_hbm, g_ref, in_sems.at[hops + 1]),
        ]
        start_all(late)
        for j in range(hops):
            fetch[j].wait()
            for c in range(2):
                weights.wait((ids_ref[0] ^ j) * 2 + c, w_ref, 0, width, sems)
            product = dot(act_ref[:, places[j]], w_ref[places[j], :])
            if j == 0:
                acc_ref[...] = product
            else:
                acc_ref[...] += product
        sums_ref[...] = jnp.zeros_like(sums_ref)
        wait_for(late)

        @pl.loop(0, count // step)
        def _(part):
            rows = pl.ds(pl.multiple_of(part * step, step), step)
            base = n_ref[rows, :] * vec_ref[3:4] + vec_ref[4:5] + vec_ref[5:6]
            n2, inverse = normalise(acc_ref[rows, :] + base)
            out_ref[rows, :] = (n2 * vec_ref[6:7] + vec_ref[7:8]).astype(BF)
            grad = g_ref[rows, :].astype(F32)
            back = normalise_back(grad * vec_ref[6:7], n2, inverse)
            low = back.astype(BF)
            acc_ref[rows, :] = back
            low_ref[rows, :] = low
            sums_ref[0:1, :] += total_rows(grad * n2)
            sums_ref[1:2, :] += total_rows(grad)
            sums_ref[2:3, :] += total_rows(low.astype(F32))

        done = copies([(low_ref, low_hbm), (acc_ref, sum_hbm), (out_ref, out_hbm)], out_sems)
        start_all(done)
        send = copies(
            [(sent_ref.at[j], sent_hbm.at[pl.ds(j * block, block), :]) for j in range(hops)],
            sent_sems,
        )
        for j in range(hops):
            at = ((ids_ref[0] ^ j) * 2 + (ids_ref[1] ^ 1)) * block
            sent_ref[j] = dot_tn(act_ref[:, aligned(at, block)], low_ref[...]).astype(BF)
            send[j].start()
        wait_for(done + send)

    size = (count, width)
    return kernel(
        body,
        "ffn_out",
        18,
        ids,
        (1,),
        [(vectors, whole(vectors.shape))]
        + [(a, ANY) for a in [act, normed, out_grad] + weights.arrays],
        [
            (struct(size, BF), ANY),
            (struct(size, F32), ANY),
            (struct(size, BF), ANY),
            (struct((8, width), F32), whole((8, width))),
            (struct((wide // 2, width), BF), ANY),
        ],
        [
            pltpu.VMEM(size, F32),
            pltpu.VMEM(size, F32),
            pltpu.VMEM(size, BF),
            pltpu.VMEM(size, BF),
            pltpu.VMEM(size, BF),
            pltpu.VMEM((count, wide), BF),
            pltpu.VMEM((wide, width), BF),
            pltpu.VMEM((hops, block, width), BF),
            pltpu.SemaphoreType.DMA((weights.count,)),
            pltpu.SemaphoreType.DMA((hops + 2,)),
            pltpu.SemaphoreType.DMA((3,)),
            pltpu.SemaphoreType.DMA((hops,)),
        ],
    )


def ffn_back(ids, grad, slope, weights, lefts, left_specs, deps):
    count, wide = slope.shape
    width = grad.shape[1]
    block = min(wide, 1024)
    per = block // weights.block
    n_pieces = len(weights.arrays)
    rows_out = sum(spec.block_shape[1] for spec in left_specs)

    def body(ids_ref, grad_ref, slope_ref, *refs):
        left_refs = refs[: len(lefts)]
        pieces = refs[len(lefts) : len(lefts) + n_pieces]
        out_ref, sums_ref, sent_ref, w_ref, sems = refs[-5:]
        step = pl.program_id(0)

        @pl.when(step == 0)
        def _():
            weights.start(ids_ref, pieces, 0, w_ref, 0, width, sems)

        for i in range(per):
            weights.wait(step * per + i, w_ref, 0, width, sems)
        rows = pl.ds(pl.multiple_of(step * block, 16), block)
        back = (dot_nt(grad_ref[...], w_ref[rows, :]) * slope_ref[...]).astype(BF)
        out_ref[...] = back
        sums_ref[...] = jnp.broadcast_to(total_rows(back.astype(F32)), sums_ref.shape)
        left = jnp.concatenate([ref[...] for ref in left_refs], axis=1)
        sent_ref[...] = dot_tn(left, out_ref[...]).astype(BF)

    tile = pl.BlockSpec((count, block), lambda n, ids: (0, n))
    return kernel(
        body,
        "ffn_back",
        12,
        ids,
        (wide // block,),
        [(grad, whole(grad.shape)), (slope, tile)]
        + list(zip(lefts, left_specs))
        + [(p, ANY) for p in weights.arrays]
        + [(d, ANY) for d in deps],
        [
            (struct((count, wide), BF), tile),
            (struct((8, wide), F32), pl.BlockSpec((8, block), lambda n, ids: (0, n))),
            (
                struct((rows_out, wide), BF),
                pl.BlockSpec((rows_out, block), lambda n, ids: (0, n)),
            ),
        ],
        [pltpu.VMEM((wide, width), BF), pltpu.SemaphoreType.DMA((weights.count,))],
    )


def attention_norm_back(ids, inner_grad, ffn_grad, normed, inverse, inner, weights, vectors, deps):
    count, wide = inner_grad.shape
    width = normed.shape[1]
    tile = min(wide, 1024)
    steps = wide // tile
    n_pieces = len(weights.arrays)
    part_rows = 128

    def body(ids_ref, inverse_ref, vec_ref, grad_hbm, ffn_hbm, n_hbm, *refs):
        pieces = refs[:n_pieces]
        inner_pieces = refs[n_pieces : 2 * n_pieces]
        low_hbm, sum_hbm, mixed_hbm, sums_ref = refs[-17:-13]
        acc_ref, ffn_ref, n_ref, low_ref, mixed_ref, grad_ref, w_ref = refs[-13:-6]
        w_sems, o_ref, o_sems, sems, grad_sems, out_sems = refs[-6:]
        tiles = [slice(g * tile, (g + 1) * tile) for g in range(steps)]
        fetch = copies([(grad_hbm.at[:, t], grad_ref.at[:, t]) for t in tiles], grad_sems)
        for g in range(steps):
            fetch[g].start()
            inner.start(ids_ref, inner_pieces, g * tile, w_ref.at[g], 0, tile, w_sems.at[g])
        late = copies([(ffn_hbm, ffn_ref), (n_hbm, n_ref)], sems)
        start_all(late)
        weights.start(ids_ref, pieces, 3 * width, o_ref, 0, width, o_sems)
        acc_ref[...] = jnp.zeros_like(acc_ref)

        @pl.loop(0, steps)
        def _(g):
            there = grad_ref.at[:, aligned(g * tile, tile)]
            pltpu.make_async_copy(there, there, grad_sems.at[g]).wait()
            inner.wait_all(w_ref.at[g], 0, tile, w_sems.at[g])
            acc_ref[...] += dot_nt(there[...], w_ref[g])

        wait_for(late)
        sums_ref[...] = jnp.zeros_like(sums_ref)

        @pl.loop(0, count // part_rows)
        def _(part):
            rows = pl.ds(pl.multiple_of(part * part_rows, part_rows), part_rows)
            grad = acc_ref[rows, :] + ffn_ref[rows, :]
            normed_rows = n_ref[rows, :]
            back = normalise_back(grad * vec_ref[3:4], normed_rows, inverse_ref[rows, 0:1])
            low = back.astype(BF)
            low_ref[rows, :] = low
            acc_ref[rows, :] = back
            sums_ref[0:1, :] += total_rows(grad * normed_rows)
            sums_ref[1:2, :] += total_rows(grad)
            sums_ref[2:3, :] += total_rows(low.astype(F32))

        done = copies(
            [(low_ref, low_hbm), (acc_ref, sum_hbm), (mixed_ref, mixed_hbm)], out_sems
        )
        start_all(done[:2])
        weights.wait_all(o_ref, 0, width, o_sems)
        mixed_ref[...] = dot_nt(low_ref[...], o_ref[...]).astype(BF)
        done[2].start()
        wait_for(done)

    size = (count, width)
    return kernel(
        body,
        "attention_norm_back",
        16,
        ids,
        (1,),
        [(inverse, whole(inverse.shape)), (vectors, whole(vectors.shape))]
        + [
            (a, ANY)
            for a in [inner_grad, ffn_grad, normed] + weights.arrays + inner.arrays + list(deps)
        ],
        [
            (struct(size, BF), ANY),
            (struct(size, F32), ANY),
            (struct(size, BF), ANY),
            (struct((8, width), F32), whole((8, width))),
        ],
        [
            pltpu.VMEM(size, F32),
            pltpu.VMEM(size, F32),
            pltpu.VMEM(size, F32),
            pltpu.VMEM(size, BF),
            pltpu.VMEM(size, BF),
            pltpu.VMEM((count, wide), BF),
            pltpu.VMEM((steps, width, tile), BF),
            pltpu.SemaphoreType.DMA((steps, inner.count)),
            pltpu.VMEM((width, width), BF),
            pltpu.SemaphoreType.DMA((weights.count,)),
            pltpu.SemaphoreType.DMA((2,)),
            pltpu.SemaphoreType.DMA((steps,)),
            pltpu.SemaphoreType.DMA((3,)),
        ],
    )


def inputs_back(ids, base, grads, weights, deps):
    count, width = base.shape
    tile = 256
    per = tile // weights.block
    n_pieces = len(weights.arrays)

    def body(ids_ref, base_ref, q_ref, k_ref, v_ref, *refs):
        pieces = refs[:n_pieces]
        out_ref, w_ref, sems = refs[-3:]
        step = pl.program_id(0)

        @pl.when(step == 0)
        def _():
            weights.start(ids_ref, pieces, 0, w_ref, 0, 3 * width, sems)

        for i in range(per):
            weights.wait(step * per + i, w_ref, 0, 3 * width, sems)
        place = pl.ds(pl.multiple_of(step * tile, tile), tile)
        out = base_ref[...]
        for i, ref in enumerate((q_ref, k_ref, v_ref)):
            out = out + dot_nt(ref[...], w_ref[place, i * width : (i + 1) * width])
        out_ref[...] = out

    block = pl.BlockSpec((count, tile), lambda n, ids: (0, n))
    return kernel(
        body,
        "inputs_back",
        10,
        ids,
        (width // tile,),
        [(base, block)]
        + [(g, whole(g.shape)) for g in grads]
        + [(p, ANY) for p in weights.arrays]
        + [(d, ANY) for d in deps],
        [(struct(base.shape, F32), block)],
        [pltpu.VMEM((width, 3 * width), BF), pltpu.SemaphoreType.DMA((weights.count,))],
    )[0]


def split_hops(kept, bit):
    stay = [j for j in kept if not j & bit]
    return stay, [j | bit for j in stay]


class RowSum:
    def __init__(self, net, pairs, ids, tile):
        self.net, self.ids, self.tile = net, ids, tile
        self.rights = [right for _, right in pairs]
        self.left = []
        for left, _ in pairs:
            if not any(left is known for known in self.left):
                self.left.append(left)
        self.uses = [[left is known for known in self.left].index(True) for left, _ in pairs]
        self.width = self.left[0].shape[1] // (net.chips * 2)
        self.columns = sum(r.shape[1] for r in self.rights)
        bits = [1 << b for b in range(net.chips.bit_length() - 1)]
        self.bits = (bits, bits[::-1])
        self.kept = [list(range(net.chips))] * 2

    def lefts(self, core):
        net, width = self.net, self.width
        if width % 128 == 0:
            spec = [
                pl.BlockSpec(
                    (self.left[0].shape[0], width),
                    lambda n, ids, j=j: (0, (ids[0] ^ j) * 2 + (ids[1] ^ core)),
                )
                for j in range(net.chips)
            ]
            return [left for left in self.left for _ in spec], spec * len(self.left)
        chosen = []
        for left in self.left:
            picked = []
            for j in range(net.chips):
                at = ((self.ids[0] ^ j) * 2 + (self.ids[1] ^ core)) * width
                picked.append(lax.dynamic_slice_in_dim(left, at, width, axis=1))
            chosen.append(jnp.concatenate(picked, axis=1))
        return chosen, [whole(picked.shape) for picked in chosen]

    def multiply(self, name, micros, core, got, outs, groups, targets, deps):
        net, width, tile = self.net, self.width, self.tile
        rows, tokens = net.chips * width, self.left[0].shape[0]
        ready = width % 128 != 0
        lefts = self.lefts(core)[0] if ready else self.left
        tiles = []
        for right, use in zip(range(len(self.rights)), self.uses):
            for at in range(0, self.rights[right].shape[1], tile):
                tiles.append((right, at, use))
        extra = [] if got is None else [got]
        cuts = [t for t in range(1, len(tiles)) if tiles[t][2] != tiles[t - 1][2]]

        def body(ids_ref, *refs):
            left_hbm = refs[: len(lefts)]
            right_hbm = refs[len(lefts) : len(lefts) + len(self.rights)]
            got_hbm = refs[len(lefts) + len(self.rights)]
            scratch = refs[len(refs) - 7 - len(extra) :]
            out_hbm = refs[len(refs) - 7 - len(extra) - len(outs) : len(refs) - 7 - len(extra)]
            left_ref, right_ref, out_ref, left_sems, right_sems, got_sems, out_sems = scratch[:7]
            fetch_left = []
            for i, source in enumerate(left_hbm):
                if ready:
                    pairs = [(source, left_ref.at[i])]
                else:
                    pairs = []
                    for j in range(net.chips):
                        at = ((ids_ref[0] ^ j) * 2 + (ids_ref[1] ^ core)) * width
                        place = (slice(None), slice(j * width, (j + 1) * width))
                        pairs.append((source.at[:, aligned(at, width)], left_ref.at[i].at[place]))
                fetch_left.append(copies(pairs, left_sems, i))
            fetch_right = [
                pltpu.make_async_copy(
                    right_hbm[r].at[:, at : at + tile], right_ref.at[t], right_sems.at[t]
                )
                for t, (r, at, _) in enumerate(tiles)
            ]
            fetch_got = [
                pltpu.make_async_copy(
                    got_hbm.at[:, t * tile : (t + 1) * tile], scratch[7].at[t], got_sems.at[t]
                )
                for t in range(len(tiles) if extra else 0)
            ]
            waited = set()
            for t, (_, _, use) in enumerate(tiles):
                if use not in waited:
                    start_all(fetch_left[use])
                    waited.add(use)
                fetch_right[t].start()
                if extra:
                    fetch_got[t].start()
            def part(t, which):
                use = sum(((t >= cut).astype(jnp.int32) for cut in cuts), jnp.int32(0))
                there = [right_ref.at[t]] + [ref.at[t] for ref in scratch[7:]]
                for ref, sems in zip(there, (right_sems, got_sems)):
                    pltpu.make_async_copy(ref, ref, sems.at[t]).wait()
                value = dot_tn(left_ref[use], right_ref[t])
                for ref in there[1:]:
                    value = value + ref[...].astype(F32)
                out_ref[t] = value.astype(BF)
                return copies(
                    [
                        (
                            out_ref.at[t].at[first : first + n, :],
                            out_hbm[kind].at[row : row + n, aligned(column, tile)],
                        )
                        for first, n, kind, row, column in targets(t, which)
                    ],
                    out_sems,
                    t,
                )

            count = len(tiles)
            group = count // groups
            waited = 0
            for which in range(groups):
                last = tiles[(which + 1) * group - 1][2]
                while waited <= last:
                    wait_for(fetch_left[waited])
                    waited += 1

                @pl.loop(which * group, (which + 1) * group)
                def _(t):
                    start_all(part(t, which))

            for t in range(count):
                wait_for(
                    pltpu.make_async_copy(
                        out_ref.at[t].at[first : first + n, :],
                        out_ref.at[t].at[first : first + n, :],
                        out_sems.at[t, i],
                    )
                    for i, (first, n, _, _, _) in enumerate(targets(t, t // group))
                )

        count = len(tiles)
        return kernel(
            body,
            name,
            micros,
            self.ids,
            (1,),
            [(a, ANY) for a in list(lefts) + self.rights + extra + list(deps)],
            [(o, ANY) for o in outs],
            [
                pltpu.VMEM((len(lefts), tokens, rows), BF),
                pltpu.VMEM((count, tokens, tile), BF),
                pltpu.VMEM((count, rows, tile), BF),
                pltpu.SemaphoreType.DMA((len(lefts), net.chips)),
                pltpu.SemaphoreType.DMA((count,)),
                pltpu.SemaphoreType.DMA((count,)),
                pltpu.SemaphoreType.DMA((count, net.chips)),
            ]
            + [pltpu.VMEM((count, rows, tile), BF) for _ in extra],
        )

    def other_core(self, *deps):
        rows = self.net.chips * self.width
        (self.sent,) = self.multiply(
            "rows_of_other_core",
            7,
            1,
            None,
            [struct((rows, self.columns), BF)],
            1,
            lambda t, _: [(0, rows, 0, 0, t * self.tile)],
            deps,
        )
        return self.exchange(self.sent)

    def exchange(self, sent):
        self.got = self.net.across_core(sent)
        return sent

    def own_core(self, *deps):
        rows, tile, width = self.net.chips * self.width, self.tile, self.width
        half = self.columns // tile // 2
        sides = [split_hops(self.kept[s], self.bits[s][0]) for s in range(2)]

        def targets(t, side):
            return [
                (j * width, width, side * 2 + which, i * width, (t - side * half) * tile)
                for which, hops in enumerate(sides[side])
                for i, j in enumerate(hops)
            ]

        out = self.multiply(
            "rows_of_own_core",
            9,
            0,
            self.got,
            [struct((rows // 2, self.columns // 2), BF)] * 4,
            2,
            targets,
            deps,
        )
        self.held = [out[0], out[2]]
        self.away = [out[1], out[3]]
        self.send()
        return out[0]

    def send(self):
        for s in range(2):
            self.kept[s] = split_hops(self.kept[s], self.bits[s][0])[0]
        self.arrived = [self.net.across_chip(self.away[s], self.bits[s][0]) for s in range(2)]
        self.bits = (self.bits[0][1:], self.bits[1][1:])

    def fold(self, *deps):
        rows, columns = self.held[0].shape
        tile = columns // 2
        sides = [split_hops(self.kept[s], self.bits[s][0]) for s in range(2)]

        def body(ids_ref, *refs):
            out_refs = refs[-4:]
            for s in range(2):
                for which, hops in enumerate(sides[s]):
                    for i, j in enumerate(hops):
                        at = self.kept[s].index(j) * self.width
                        part = slice(at, at + self.width)
                        value = refs[2 * s][part, :].astype(F32) + refs[2 * s + 1][part, :].astype(F32)
                        out_refs[2 * s + which][i * self.width : (i + 1) * self.width, :] = (
                            value.astype(BF)
                        )

        block = pl.BlockSpec((rows, tile), lambda n, ids: (0, n))
        half = pl.BlockSpec((rows // 2, tile), lambda n, ids: (0, n))
        out = kernel(
            body,
            "fold",
            4,
            self.ids,
            (columns // tile,),
            [(a, block) for s in range(2) for a in (self.held[s], self.arrived[s])]
            + [(d, ANY) for d in deps],
            [(struct((rows // 2, columns), BF), half)] * 4,
            [],
        )
        self.held = [out[0], out[2]]
        self.away = [out[1], out[3]]
        self.send()
        return self.fold() if self.bits[0] else out[0]

    def fold_z(self, *deps):
        net, count = self.net, self.net.inner
        columns = self.held[0].shape[1]
        rows = self.width // count
        stay, leave = split_hops(list(range(count)), 1)
        size = (rows * len(stay), 2 * columns)
        if rows % 16:
            held = tie(jnp.concatenate(self.held, axis=1), *deps).astype(F32)
            held = held + jnp.concatenate(self.arrived, axis=1).astype(F32)
            held = held.reshape(count, rows, -1).astype(BF)
            keep, away = (
                jnp.take(held, jnp.array(hops) ^ self.ids[2], axis=0).reshape(size)
                for hops in (stay, leave)
            )
        else:

            def body(ids_ref, *refs):
                for out_ref, hops in zip(refs[-2:], (stay, leave)):
                    for i, s in enumerate(hops):
                        at = pl.ds(pl.multiple_of((ids_ref[2] ^ s) * rows, 16), rows)
                        for side in range(2):
                            value = refs[2 * side][at, :].astype(F32)
                            value = value + refs[2 * side + 1][at, :].astype(F32)
                            place = slice(side * columns, (side + 1) * columns)
                            out_ref[i * rows : (i + 1) * rows, place] = value.astype(BF)

            keep, away = kernel(
                body,
                "fold_z",
                3,
                self.ids,
                (1,),
                [
                    (a, whole(a.shape))
                    for s in range(2)
                    for a in (self.held[s], self.arrived[s])
                ]
                + [(d, ANY) for d in deps],
                [(struct(size, BF), whole(size))] * 2,
                [],
            )
        self.total, self.came, self.reach = keep, net.swap(away, 1), 1
        return keep

    def fold_far(self, *deps):
        while self.reach * 2 < self.net.inner:
            self.reach *= 2
            total = tie(self.total, *deps).astype(F32) + self.came.astype(F32)
            rows = self.width // self.net.inner
            count = total.shape[0] // rows
            stay = [i for i in range(count) if not i & 1]
            blocks = total.reshape(count, rows, -1)
            away = jnp.concatenate([blocks[i + 1] for i in stay], axis=0).astype(BF)
            self.total = jnp.concatenate([blocks[i] for i in stay], axis=0)
            self.came = self.net.swap(away, self.reach)
        return self.came

    def finish(self, *deps):
        return tie(self.total, *deps).astype(F32) + self.came.astype(F32)


class ZFirst:
    def __init__(self, rows_sum):
        self.sum, self.net = rows_sum, rows_sum.net
        self.low = rows_sum.width // self.net.inner
        self.usual = self.net.inner != 4 or len(rows_sum.bits[0]) != 1 or self.low % 16 != 0

    def cross_near(self, *deps):
        source, low = self.sum, self.low
        if self.usual:
            source.fold(*deps)
            return source.fold_z()
        columns = source.held[0].shape[1]
        split = split_hops(list(range(4)), 1)
        sides = [split_hops(source.kept[s], source.bits[s][0]) for s in range(2)]
        size = (4 * low, 2 * columns)

        def body(ids_ref, *refs):
            for out_ref, zs in zip(refs[-2:], split):
                for i, z in enumerate(zs):
                    for s in range(2):
                        for h in range(2):
                            at = source.kept[s].index(sides[s][h][0]) * source.width
                            at = pl.multiple_of(at + (ids_ref[2] ^ z) * low, 16)
                            value = refs[2 * s][pl.ds(at, low), :].astype(F32)
                            value = value + refs[2 * s + 1][pl.ds(at, low), :].astype(F32)
                            row = (2 * i + h) * low
                            out_ref[row : row + low, s * columns : (s + 1) * columns] = (
                                value.astype(BF)
                            )

        self.keep, away = kernel(
            body,
            "cross_near",
            6,
            source.ids,
            (1,),
            [
                (a, whole(a.shape))
                for s in range(2)
                for a in (source.held[s], source.arrived[s])
            ]
            + [(d, ANY) for d in deps],
            [(struct(size, BF), whole(size))] * 2,
            [],
        )
        self.came = self.net.swap(away, 1)
        return self.keep

    def halve(self, *deps):
        total = tie(self.keep, *deps).astype(F32) + self.came.astype(F32)
        half = total.shape[0] // 2
        self.keep = total[:half].astype(BF)
        return total[half:].astype(BF)

    def cross_far(self, *deps):
        if self.usual:
            return self.sum.fold_far(*deps)
        self.came = self.net.swap(self.halve(*deps), 2)
        return self.came

    def cross_chip(self, *deps):
        if self.usual:
            return None
        away = self.halve(*deps)
        half = away.shape[1] // 2
        parts = [
            self.net.across_chip(away[:, s * half : (s + 1) * half], self.sum.bits[s][0])
            for s in range(2)
        ]
        self.came = jnp.concatenate(parts, axis=1)
        return None

    def finish(self, *deps):
        if self.usual:
            return self.sum.finish(*deps)
        return tie(self.keep, *deps).astype(F32) + self.came.astype(F32)


def shards(
    net,
    inputs,
    segment_ids,
    query_weight,
    key_weight,
    value_weight,
    output_weight,
    query_bias,
    value_bias,
    output_bias,
    attn_gain,
    attn_shift,
    inner_weight,
    inner_bias,
    outer_weight,
    outer_bias,
    ffn_gain,
    ffn_shift,
    out_grad,
):
    row_count, seq_len, width = inputs.shape
    tokens = inputs.reshape(row_count * seq_len, width)
    _, ids = net.place()
    small = [
        query_bias,
        value_bias,
        output_bias,
        attn_gain,
        attn_shift,
        outer_bias,
        ffn_gain,
        ffn_shift,
        inner_bias,
    ]
    mine = query_bias.shape[0]
    shard = first_shard([query_weight, key_weight, value_weight, output_weight], small)
    gather_a = Gather(net, shard, ids, True)
    gather_a.ordered()
    gather_a.plane()
    gather_b = Gather(net, tie(inner_weight, gather_a.block), ids, True)
    gather_a.relay(*gather_b.along)
    gather_b.ordered()
    weights_a = gather_a.cores()
    gather_b.plane(*weights_a.arrays)
    queries, keys, values, vectors = project(ids, tokens, weights_a)
    spread = inner_bias.shape[0] // mine
    inner_bias_full = vectors[8 : 8 + spread].reshape(spread, net.count, mine)
    inner_bias_full = inner_bias_full.swapaxes(0, 1).reshape(1, -1)
    mixed, totals = attend_forward(segment_ids, queries, keys, values)
    gather_c = Gather(net, tie(outer_weight, queries), ids, True, mixed)
    arrived = gather_b.relay(mixed)
    normed, inverse, normed_low = close_attention(ids, mixed, tokens, weights_a, vectors)
    gather_c.ordered(normed_low)
    gather_c.plane(*arrived)
    weights_b = gather_b.cores()
    act, slope = ffn_in(ids, normed_low, weights_b, inner_bias_full)
    gather_c.relay(act)
    weights_c = gather_c.cores()
    grad_out = out_grad.reshape(tokens.shape)
    outputs, ffn_grad, branch_grad, ffn_sums, sent = ffn_out(
        ids, act, normed, grad_out, weights_c, vectors
    )
    outer_sum = RowSum(net, [(act, branch_grad)], ids, 256)
    last = outer_sum.exchange(sent)
    lefts = RowSum(net, [(normed_low, slope)], ids, 1024).lefts(1)
    inner_grad, inner_sums, sent = ffn_back(ids, branch_grad, slope, weights_c, *lefts, [last])
    inner_sum = RowSum(net, [(normed_low, inner_grad)], ids, 1024)
    last = inner_sum.exchange(sent)
    last = outer_sum.own_core(last)
    attn_grad, attn_sum_grad, mixed_grad, attn_sums = attention_norm_back(
        ids, inner_grad, ffn_grad, normed, inverse, weights_b, weights_a, vectors, [last]
    )
    last = inner_sum.own_core(attn_grad)
    query_grad, key_grad, value_grad, grad_query_bias, grad_value_bias = attend_backward(
        segment_ids, queries, keys, values, mixed_grad, totals, [last, *outer_sum.arrived]
    )
    inputs_sum = RowSum(
        net,
        [(mixed, attn_grad)] + [(tokens, g) for g in (query_grad, key_grad, value_grad)],
        ids,
        1024,
    )
    outer = ZFirst(outer_sum)
    last = outer.cross_near(query_grad)
    last = inputs_sum.other_core(last, *inner_sum.arrived)
    last = inner_sum.fold(last)
    last = inputs_sum.own_core(last)
    last = inner_sum.fold_z(last)
    outer.cross_far(last)
    last = inputs_sum.fold(last)
    inner_sum.fold_far(last)
    input_grad = inputs_back(
        ids, attn_sum_grad, (query_grad, key_grad, value_grad), weights_a, [last]
    )
    last = inputs_sum.fold_z(input_grad)
    outer.cross_chip(last)
    shard_inner = inner_sum.finish(last)
    shard_outer = outer.finish(last)
    inputs_sum.fold_far(last)
    shard_inputs = inputs_sum.finish()
    shard_output, shard_query, shard_key, shard_value = (
        shard_inputs[:, i * width : (i + 1) * width] for i in range(4)
    )
    rows = jnp.concatenate(
        [grad_query_bias[None], grad_value_bias[None], attn_sums[:3], ffn_sums[:3]], axis=0
    )
    rows = rows.reshape(8, net.count, mine).swapaxes(0, 1).reshape(net.count, 8 * mine)
    packed = jnp.concatenate([rows, inner_sums[0].reshape(net.count, -1)], axis=1)
    packed = tie(packed, last)
    summed = jnp.sum(lax.all_to_all(packed, AXES, 0, 0, tiled=True), axis=0)
    vector = [summed[i * mine : (i + 1) * mine] for i in range(8)]
    return (
        outputs.reshape(inputs.shape),
        input_grad.reshape(inputs.shape),
        shard_query,
        shard_key,
        shard_value,
        shard_output,
        vector[0],
        vector[1],
        vector[4],
        vector[2],
        vector[3],
        shard_inner,
        summed[8 * mine :],
        shard_outer,
        vector[7],
        vector[5],
        vector[6],
    )


def solution(mesh):
    placed = (
        P(("dp", "fsdp"), None, None),
        P(("dp", "fsdp"), None),
        P(("dp", "fsdp"), None),
        P(("dp", "fsdp"), None),
        P(("dp", "fsdp"), None),
        P(("dp", "fsdp"), None),
        P(("dp", "fsdp")),
        P(("dp", "fsdp")),
        P(("dp", "fsdp")),
        P(("dp", "fsdp")),
        P(("dp", "fsdp")),
        P(("dp", "fsdp"), None),
        P(("dp", "fsdp")),
        P(("dp", "fsdp"), None),
        P(("dp", "fsdp")),
        P(("dp", "fsdp")),
        P(("dp", "fsdp")),
        P(("dp", "fsdp"), None, None),
    )
    return jax.shard_map(
        functools.partial(shards, Slice(mesh.shape["dp"], mesh.shape["fsdp"])),
        mesh=mesh,
        in_specs=placed,
        out_specs=(
            P(("dp", "fsdp"), None, None),
            P(("dp", "fsdp"), None, None),
            P(("dp", "fsdp"), None),
            P(("dp", "fsdp"), None),
            P(("dp", "fsdp"), None),
            P(("dp", "fsdp"), None),
            P(("dp", "fsdp")),
            P(("dp", "fsdp")),
            P(("dp", "fsdp")),
            P(("dp", "fsdp")),
            P(("dp", "fsdp")),
            P(("dp", "fsdp"), None),
            P(("dp", "fsdp")),
            P(("dp", "fsdp"), None),
            P(("dp", "fsdp")),
            P(("dp", "fsdp")),
            P(("dp", "fsdp")),
        ),
        check_vma=False,
    )
```

```python
import functools

import jax
import jax.numpy as jnp
from jax import lax
from jax.experimental import pallas as pl
from jax.experimental.pallas import tpu as pltpu
from jax.sharding import PartitionSpec as P

H = 16
HD = 64
AXES = ("dp", "fsdp")
BF = jnp.bfloat16
F32 = jnp.float32
EPSILON = 1e-05
NT = (((1,), (1,)), ((), ()))
TN = (((0,), (0,)), ((), ()))
MASKED = -1e30
WEIGHT = 0.3


def spend(micros):
    return pl.CostEstimate(flops=1, bytes_accessed=int(micros * WEIGHT * 1e6), transcendentals=0)


ANY = pl.BlockSpec(memory_space=pl.ANY)


def whole(shape):
    return pl.BlockSpec(shape, lambda *_: (0,) * len(shape))


def struct(shape, dtype):
    return jax.ShapeDtypeStruct(shape, dtype)


def dot(left, right):
    return jnp.dot(left, right, preferred_element_type=F32)


def dot_tn(left, right):
    return lax.dot_general(left, right, TN, preferred_element_type=F32)


def dot_nt(left, right):
    return lax.dot_general(left, right, NT, preferred_element_type=F32)


def tie(value, *after):
    return lax.optimization_barrier((value, *after))[0]


def normalise(rows):
    centred = rows - jnp.mean(rows, axis=-1, keepdims=True)
    spread = jnp.mean(centred * centred, axis=-1, keepdims=True)
    inverse = lax.rsqrt(spread + EPSILON)
    return centred * inverse, inverse


def normalise_back(cotangent, normed, inverse):
    slope = jnp.mean(cotangent * normed, axis=-1, keepdims=True)
    return inverse * (cotangent - jnp.mean(cotangent, axis=-1, keepdims=True) - normed * slope)


def total_rows(matrix):
    return jnp.sum(matrix, axis=0, keepdims=True)


def lane_half(block, which):
    lane = lax.broadcasted_iota(jnp.int32, block.shape, 1)
    return jnp.where((lane >= HD) == (which == 1), block, jnp.zeros_like(block))


def set_mask(seg_ref, mask_ref):
    seg_row = seg_ref[...].astype(F32)
    seg_col = jnp.broadcast_to(seg_row, (128, seg_row.shape[1])).T
    for at in range(0, seg_row.shape[1], 128):
        same = seg_col == seg_row[:, at : at + 128]
        mask_ref[:, at : at + 128] = jnp.where(same, 0.0, MASKED)


def attend_forward_body(seg_ref, q_ref, k_ref, v_ref, mixed_ref, total_ref, mask_ref):
    @pl.when(pl.program_id(1) == 0)
    def _():
        set_mask(seg_ref, mask_ref)

    query = q_ref[...] * jnp.bfloat16(HD**-0.5)
    key = k_ref[...]
    value_t = v_ref[...].T
    halves = []
    for h in range(2):
        scores = lax.dot_general(lane_half(key, h), query, NT, preferred_element_type=F32)
        scores = scores + mask_ref[...]
        high = jnp.max(scores, axis=0, keepdims=True)
        raised = jnp.exp(scores - high)
        total = jnp.sum(raised, axis=0, keepdims=True)
        low = (raised * (1.0 / total)).astype(BF)
        rows = value_t[h * HD : (h + 1) * HD]
        halves.append(jnp.dot(rows, low, preferred_element_type=F32))
        total_ref[0, h : h + 1, :] = high + jnp.log(total)
    mixed_ref[...] = jnp.concatenate(halves, axis=0).T.astype(BF)


def attend_backward_body(
    seg_ref, q_ref, k_ref, v_ref, g_ref, total_ref, *rest
):
    dq_ref, dk_ref, dv_ref, dq_sum_ref, dv_sum_ref, mask_ref = rest[-6:]

    @pl.when(pl.program_id(1) == 0)
    def _():
        set_mask(seg_ref, mask_ref)

    scale = HD**-0.5
    query = q_ref[...] * jnp.bfloat16(scale)
    key, value, grad = k_ref[...], v_ref[...], g_ref[...]
    key_t = key.T
    lane = lax.broadcasted_iota(jnp.int32, key.shape, 1)
    dq_t, dk, dv = [], None, None
    for h in range(2):
        scores = lax.dot_general(lane_half(key, h), query, NT, preferred_element_type=F32)
        probs = jnp.exp(scores + mask_ref[...] - total_ref[0, h : h + 1, :])
        prob_grad = lax.dot_general(lane_half(value, h), grad, NT, preferred_element_type=F32)
        inner_sum = jnp.sum(probs * prob_grad, axis=0, keepdims=True)
        score_grad = (probs * (prob_grad - inner_sum)).astype(BF)
        dv_h = jnp.dot(probs.astype(BF), grad, preferred_element_type=F32)
        dk_h = jnp.dot(score_grad, query, preferred_element_type=F32)
        dv = dv_h if h == 0 else jnp.where(lane < HD, dv, dv_h)
        dk = dk_h if h == 0 else jnp.where(lane < HD, dk, dk_h)
        rows = key_t[h * HD : (h + 1) * HD]
        dq_t.append(jnp.dot(rows, score_grad, preferred_element_type=F32))
    dq = (jnp.concatenate(dq_t, axis=0).T * scale).astype(BF)
    dv = dv.astype(BF)
    dq_ref[...] = dq
    dk_ref[...] = dk.astype(BF)
    dv_ref[...] = dv
    wide = (8, dq.shape[1])
    dq_sum_ref[0] = jnp.broadcast_to(jnp.sum(dq.astype(F32), axis=0, keepdims=True), wide)
    dv_sum_ref[0] = jnp.broadcast_to(jnp.sum(dv.astype(F32), axis=0, keepdims=True), wide)


def attention_specs(seq_len, deps):
    block = pl.BlockSpec((seq_len, 2 * HD), lambda r, n: (r, n))
    seg = pl.BlockSpec((None, 1, seq_len), lambda r, n: (r, 0, 0))
    total = pl.BlockSpec((None, 1, 8, seq_len), lambda r, n: (r, n, 0, 0))
    sums = pl.BlockSpec((1, 8, 2 * HD), lambda r, n: (r, 0, n))
    return block, seg, total, sums, [pl.BlockSpec(memory_space=pl.ANY)] * deps


def attend_forward(seg, queries, keys, values):
    rows, seq_len = seg.shape
    block, seg_spec, total, _, _ = attention_specs(seq_len, 0)
    tokens, width = queries.shape
    pairs = width // (2 * HD)
    return pl.pallas_call(
        attend_forward_body,
        out_shape=[
            jax.ShapeDtypeStruct((tokens, width), BF),
            jax.ShapeDtypeStruct((rows, pairs, 8, seq_len), F32),
        ],
        grid=(rows, pairs),
        in_specs=[seg_spec, block, block, block],
        out_specs=[block, total],
        scratch_shapes=[pltpu.VMEM((seq_len, seq_len), F32)],
        name="attend_forward",
        cost_estimate=spend(13),
    )(seg.reshape(rows, 1, seq_len), queries, keys, values)


def attend_backward(seg, queries, keys, values, mixed_grad, totals, deps):
    rows, seq_len = seg.shape
    block, seg_spec, total, sums, extra = attention_specs(seq_len, len(deps))
    tokens, width = queries.shape
    pairs = width // (2 * HD)
    outs = pl.pallas_call(
        attend_backward_body,
        out_shape=[jax.ShapeDtypeStruct((tokens, width), BF)] * 3
        + [jax.ShapeDtypeStruct((rows, 8, width), F32)] * 2,
        grid=(rows, pairs),
        in_specs=[seg_spec, block, block, block, block, total] + extra,
        out_specs=[block, block, block, sums, sums],
        scratch_shapes=[pltpu.VMEM((seq_len, seq_len), F32)],
        name="attend_backward",
        cost_estimate=spend(17),
    )(seg.reshape(rows, 1, seq_len), queries, keys, values, mixed_grad, totals, *deps)
    dq, dk, dv, dq_sum, dv_sum = outs
    return dq, dk, dv, jnp.sum(dq_sum[:, 0], axis=0), jnp.sum(dv_sum[:, 0], axis=0)


class Slice:
    def __init__(self, dp, inner):
        self.inner, self.chips, self.count = inner, dp // 2, dp * inner

    def swap(self, value, mask):
        pairs = [(i, i ^ mask) for i in range(self.count)]
        return lax.ppermute(value, AXES, pairs)

    def across_core(self, value):
        return self.swap(value, self.inner)

    def across_chip(self, value, hop):
        return self.swap(value, hop * 2 * self.inner)

    def place(self):
        me = lax.axis_index(AXES)
        z = me % self.inner
        core = (me // self.inner) % 2
        return me, jnp.stack([me // (2 * self.inner), core, z]).astype(jnp.int32)


def first_shard(matrices, vectors):
    rows = matrices[0].shape[0]
    columns = sum(p.shape[1] for p in matrices)

    def body(*refs):
        out_ref, turn_ref = refs[-2:]
        at = 0
        for ref in refs[: len(matrices)]:
            out_ref[:, at : at + ref.shape[1]] = ref[...]
            at += ref.shape[1]
        turn_ref[...] = jnp.zeros_like(turn_ref)
        row = 0
        for ref in refs[len(matrices) : -2]:
            for start in range(0, ref.shape[1], rows):
                turn_ref[row : row + 1, 0:rows] = ref[:, start : start + rows].astype(F32)
                row += 1
        out_ref[:, at:] = turn_ref[...].T[0:rows].astype(BF)

    return pl.pallas_call(
        body,
        out_shape=struct((rows, columns + 128), BF),
        scratch_shapes=[pltpu.VMEM((128, 128), F32)],
        name="first_shard",
        cost_estimate=spend(2),
    )(*matrices, *[v.reshape(1, -1) for v in vectors])


def in_z_order(net, parts, ids):
    rows, columns = parts[0].shape
    if rows % 16:
        stacked = jnp.stack(parts)
        return jnp.take(stacked, jnp.arange(net.inner) ^ ids[2], axis=0).reshape(-1, columns)
    tile = next(columns // n for n in (2, 3, 1) if columns % (n * 128) == 0)

    def body(ids_ref, *refs):
        for s, part in enumerate(refs[:-1]):
            row = (ids_ref[2] ^ s) * rows
            refs[-1][pl.ds(pl.multiple_of(row, rows), rows), :] = part[...]

    return pl.pallas_call(
        body,
        out_shape=struct((net.inner * rows, columns), BF),
        grid_spec=pltpu.PrefetchScalarGridSpec(
            num_scalar_prefetch=1,
            grid=(columns // tile,),
            in_specs=[pl.BlockSpec((rows, tile), lambda n, ids: (0, n))] * net.inner,
            out_specs=pl.BlockSpec((net.inner * rows, tile), lambda n, ids: (0, n)),
        ),
        name="in_z_order",
        cost_estimate=spend(3),
    )(ids, *parts)


class Gather:
    def __init__(self, net, shard, ids, relay, *late):
        self.net, self.ids = net, ids
        self.relayed = relay and net.chips == 4
        self.along = [shard]
        reach = net.inner // 2
        while reach:
            if late and len(self.along) > 1:
                self.along[1:] = [tie(part, *late) for part in self.along[1:]]
            self.along = [
                part
                for near in self.along
                for part in (near, net.swap(near, reach))
            ]
            reach //= 2
        order = [0]
        reach = net.inner // 2
        while reach:
            order = [s ^ far for s in order for far in (0, reach)]
            reach //= 2
        self.along = [self.along[order.index(s)] for s in range(net.inner)]

    def ordered(self, *after):
        parts = list(lax.optimization_barrier((*self.along, *after))[: self.net.inner])
        self.block = in_z_order(self.net, parts, self.ids)
        self.rows = self.block.shape[0]
        return self.block

    def plane(self, *after):
        net = self.net
        self.pieces = [(self.block, 0, 0, 0)]
        hops = range(1, 3 if self.relayed else net.chips)
        sent = tie(self.block, *after)
        self.pieces += [(net.across_chip(sent, j), j, 0, 0) for j in hops]

    def relay(self, *after):
        net = self.net
        if self.relayed:
            half = self.rows // 2
            first, second = self.pieces[1][0], self.pieces[2][0]
            low = net.across_chip(tie(first, second, *after)[:half], 2)
            high = net.across_chip(tie(second, first, *after)[half:], 1)
            self.pieces += [(low, 3, 0, 0), (high, 3, 0, half)]
        return [p for p, _, _, _ in self.pieces]

    def cores(self, *after):
        across = [(self.net.across_core(tie(p, *after)), j, 1, s) for p, j, _, s in self.pieces]
        return Rows(self.net, self.rows, self.pieces + across)


class Rows:
    def __init__(self, net, block, pieces):
        self.block = block
        self.count = net.chips * 2
        self.arrays = [p for p, _, _, _ in pieces]
        self.meta = [(p.shape[0], j, c, s) for p, j, c, s in pieces]

    def after(self, *others):
        again = Rows.__new__(Rows)
        again.block, again.count, again.meta = self.block, self.count, self.meta
        tied = lax.optimization_barrier((*self.arrays, *others))
        again.arrays = list(tied[: len(self.arrays)])
        return again

    def start(self, ids_ref, refs, column, target, at, width, sems, hop=None):
        for ref, (rows, j, c, s) in zip(refs, self.meta):
            if hop is not None and j != hop:
                continue
            block = (ids_ref[0] ^ j) * 2 + (ids_ref[1] ^ c)
            row = pl.multiple_of(block * self.block + s, 16)
            pltpu.make_async_copy(
                ref.at[:, pl.ds(column, width)],
                target.at[pl.ds(row, rows), pl.ds(at, width)],
                sems.at[block],
            ).start()

    def wait(self, block, target, at, width, sems):
        row = block * self.block
        if not isinstance(row, int):
            row = pl.multiple_of(row, 16)
        there = target.at[pl.ds(row, self.block), pl.ds(at, width)]
        pltpu.make_async_copy(there, there, sems.at[block]).wait()

    def wait_all(self, target, at, width, sems):
        for block in range(self.count):
            self.wait(block, target, at, width, sems)


def copies(pairs, sems, *at):
    return [
        pltpu.make_async_copy(source, target, sems.at[(*at, i)])
        for i, (source, target) in enumerate(pairs)
    ]


def start_all(some):
    for copy in some:
        copy.start()


def wait_for(some):
    for copy in some:
        copy.wait()


def aligned(start, size):
    return pl.ds(pl.multiple_of(start, 128), size)


def kernel(body, name, micros, ids, grid, operands, outs, scratch):
    return pl.pallas_call(
        body,
        out_shape=[o for o, _ in outs],
        grid_spec=pltpu.PrefetchScalarGridSpec(
            num_scalar_prefetch=1,
            grid=grid,
            in_specs=[s for _, s in operands],
            out_specs=[s for _, s in outs],
            scratch_shapes=scratch,
        ),
        name=name,
        cost_estimate=spend(micros),
    )(ids, *[o for o, _ in operands])


def project(ids, tokens, weights):
    count, width = tokens.shape
    tile = min(width, 1024)
    per = width // tile
    n_pieces = len(weights.arrays)

    def body(ids_ref, x_ref, *refs):
        pieces = refs[:n_pieces]
        outs = refs[n_pieces : n_pieces + 3]
        vec_ref, w_ref, s_ref, sems = refs[n_pieces + 3 :]
        step = pl.program_id(0)

        @pl.when(step == 0)
        def _():
            weights.start(ids_ref, pieces, 4 * width, s_ref, 0, 128, sems.at[3])
            for i in range(3):
                weights.start(ids_ref, pieces, i * width, w_ref, i * width, width, sems.at[i])
            weights.wait_all(s_ref, 0, 128, sems.at[3])
            vec_ref[...] = s_ref[...].astype(F32).T[0 : vec_ref.shape[0]]

        for i, row in enumerate((0, None, 1)):

            @pl.when(step == i * per)
            def _():
                weights.wait_all(w_ref, i * width, width, sems.at[i])

            @pl.when((step >= i * per) & (step < (i + 1) * per))
            def _():
                columns = pl.ds(pl.multiple_of(step * tile, tile), tile)
                out = dot(x_ref[...], w_ref[:, columns])
                if row is not None:
                    inside = pl.ds(pl.multiple_of((step - i * per) * tile, tile), tile)
                    out = out + vec_ref[row : row + 1, inside]
                outs[i][...] = out.astype(BF)

    def out_spec(i):
        return pl.BlockSpec((count, tile), lambda n, ids: (0, jnp.clip(n - i * per, 0, per - 1)))

    return kernel(
        body,
        "project",
        10,
        ids,
        (3 * per,),
        [(tokens, whole(tokens.shape))] + [(p, ANY) for p in weights.arrays],
        [(struct(tokens.shape, BF), out_spec(i)) for i in range(3)]
        + [(struct((16, width), F32), whole((16, width)))],
        [
            pltpu.VMEM((width, 3 * width), BF),
            pltpu.VMEM((width, 128), BF),
            pltpu.SemaphoreType.DMA((4, weights.count)),
        ],
    )


def close_attention(ids, mixed, tokens, weights, vectors):
    count, width = tokens.shape
    rows = 256
    n_pieces = len(weights.arrays)

    def body(ids_ref, m_ref, x_ref, vec_ref, *refs):
        pieces = refs[:n_pieces]
        normed_ref, inverse_ref, low_ref, w_ref, sems = refs[n_pieces:]

        @pl.when(pl.program_id(0) == 0)
        def _():
            weights.start(ids_ref, pieces, 3 * width, w_ref, 0, width, sems)
            weights.wait_all(w_ref, 0, width, sems)

        total = x_ref[...].astype(F32) + (dot(m_ref[...], w_ref[...]) + vec_ref[2:3])
        normed, inverse = normalise(total)
        normed_ref[...] = normed
        inverse_ref[...] = jnp.broadcast_to(inverse, inverse_ref.shape)
        low_ref[...] = (normed * vec_ref[3:4] + vec_ref[4:5]).astype(BF)

    block = pl.BlockSpec((rows, width), lambda n, ids: (n, 0))
    return kernel(
        body,
        "close_attention",
        7,
        ids,
        (count // rows,),
        [(mixed, block), (tokens, block), (vectors, whole(vectors.shape))]
        + [(p, ANY) for p in weights.arrays],
        [
            (struct((count, width), F32), block),
            (struct((count, 128), F32), pl.BlockSpec((rows, 128), lambda n, ids: (n, 0))),
            (struct((count, width), BF), block),
        ],
        [pltpu.VMEM((width, width), BF), pltpu.SemaphoreType.DMA((weights.count,))],
    )


def ffn_in(ids, low, weights, bias):
    count, width = low.shape
    wide = bias.shape[1]
    tile = 1024
    n_pieces = len(weights.arrays)

    def body(ids_ref, x_ref, bias_ref, *refs):
        pieces = refs[:n_pieces]
        act_ref, slope_ref, w_ref, sems = refs[n_pieces:]
        step = pl.program_id(0)

        @pl.when(step == 0)
        def _():
            for g in range(wide // tile):
                weights.start(ids_ref, pieces, g * tile, w_ref.at[g], 0, tile, sems.at[g])

        weights.wait_all(w_ref.at[step], 0, tile, sems.at[step])
        @pl.loop(0, tile // 512)
        def _(part):
            columns = pl.ds(pl.multiple_of(part * 512, 512), 512)
            pre = dot(x_ref[...], w_ref[step, :, columns]) + bias_ref[:, columns]
            below = 0.5 + 0.5 * lax.erf(pre * (0.5**0.5))
            density = jnp.exp(pre * pre * -0.5) * 0.3989422804014327
            act_ref[:, columns] = (pre * below).astype(BF)
            slope_ref[:, columns] = below + pre * density

    block = pl.BlockSpec((count, tile), lambda n, ids: (0, n))
    return kernel(
        body,
        "ffn_in",
        13,
        ids,
        (wide // tile,),
        [(low, whole(low.shape)), (bias, pl.BlockSpec((1, tile), lambda n, ids: (0, n)))]
        + [(p, ANY) for p in weights.arrays],
        [(struct((count, wide), BF), block), (struct((count, wide), F32), block)],
        [
            pltpu.VMEM((wide // tile, width, tile), BF),
            pltpu.SemaphoreType.DMA((wide // tile, weights.count)),
        ],
    )


def ffn_out(ids, act, normed, out_grad, weights, vectors):
    count, wide = act.shape
    width = normed.shape[1]
    block = weights.block
    hops = weights.count // 2
    n_pieces = len(weights.arrays)
    step = 128

    def body(ids_ref, vec_ref, act_hbm, n_hbm, g_hbm, *refs):
        pieces = refs[:n_pieces]
        out_hbm, sum_hbm, low_hbm, sums_ref, sent_hbm = refs[n_pieces : n_pieces + 5]
        acc_ref, n_ref, g_ref, out_ref, low_ref = refs[n_pieces + 5 : n_pieces + 10]
        act_ref, w_ref, sent_ref, sems, in_sems, out_sems, sent_sems = refs[n_pieces + 10 :]
        places = [aligned((ids_ref[0] ^ j) * 2 * block, 2 * block) for j in range(hops)]
        fetch = copies([(act_hbm.at[:, p], act_ref.at[:, p]) for p in places], in_sems)
        for j in range(hops):
            fetch[j].start()
            weights.start(ids_ref, pieces, 0, w_ref, 0, width, sems, hop=j)
        late = [
            pltpu.make_async_copy(n_hbm, n_ref, in_sems.at[hops]),
            pltpu.make_async_copy(g_hbm, g_ref, in_sems.at[hops + 1]),
        ]
        start_all(late)
        for j in range(hops):
            fetch[j].wait()
            for c in range(2):
                weights.wait((ids_ref[0] ^ j) * 2 + c, w_ref, 0, width, sems)
            product = dot(act_ref[:, places[j]], w_ref[places[j], :])
            if j == 0:
                acc_ref[...] = product
            else:
                acc_ref[...] += product
        sums_ref[...] = jnp.zeros_like(sums_ref)
        wait_for(late)

        @pl.loop(0, count // step)
        def _(part):
            rows = pl.ds(pl.multiple_of(part * step, step), step)
            base = n_ref[rows, :] * vec_ref[3:4] + vec_ref[4:5] + vec_ref[5:6]
            n2, inverse = normalise(acc_ref[rows, :] + base)
            out_ref[rows, :] = (n2 * vec_ref[6:7] + vec_ref[7:8]).astype(BF)
            grad = g_ref[rows, :].astype(F32)
            back = normalise_back(grad * vec_ref[6:7], n2, inverse)
            low = back.astype(BF)
            acc_ref[rows, :] = back
            low_ref[rows, :] = low
            sums_ref[0:1, :] += total_rows(grad * n2)
            sums_ref[1:2, :] += total_rows(grad)
            sums_ref[2:3, :] += total_rows(low.astype(F32))

        done = copies([(low_ref, low_hbm), (acc_ref, sum_hbm), (out_ref, out_hbm)], out_sems)
        start_all(done)
        send = copies(
            [(sent_ref.at[j], sent_hbm.at[pl.ds(j * block, block), :]) for j in range(hops)],
            sent_sems,
        )
        for j in range(hops):
            at = ((ids_ref[0] ^ j) * 2 + (ids_ref[1] ^ 1)) * block
            sent_ref[j] = dot_tn(act_ref[:, aligned(at, block)], low_ref[...]).astype(BF)
            send[j].start()
        wait_for(done + send)

    size = (count, width)
    return kernel(
        body,
        "ffn_out",
        18,
        ids,
        (1,),
        [(vectors, whole(vectors.shape))]
        + [(a, ANY) for a in [act, normed, out_grad] + weights.arrays],
        [
            (struct(size, BF), ANY),
            (struct(size, F32), ANY),
            (struct(size, BF), ANY),
            (struct((8, width), F32), whole((8, width))),
            (struct((wide // 2, width), BF), ANY),
        ],
        [
            pltpu.VMEM(size, F32),
            pltpu.VMEM(size, F32),
            pltpu.VMEM(size, BF),
            pltpu.VMEM(size, BF),
            pltpu.VMEM(size, BF),
            pltpu.VMEM((count, wide), BF),
            pltpu.VMEM((wide, width), BF),
            pltpu.VMEM((hops, block, width), BF),
            pltpu.SemaphoreType.DMA((weights.count,)),
            pltpu.SemaphoreType.DMA((hops + 2,)),
            pltpu.SemaphoreType.DMA((3,)),
            pltpu.SemaphoreType.DMA((hops,)),
        ],
    )


def ffn_back(ids, grad, slope, weights, lefts, left_specs, deps):
    count, wide = slope.shape
    width = grad.shape[1]
    block = min(wide, 1024)
    per = block // weights.block
    n_pieces = len(weights.arrays)
    rows_out = sum(spec.block_shape[1] for spec in left_specs)

    def body(ids_ref, grad_ref, slope_ref, *refs):
        left_refs = refs[: len(lefts)]
        pieces = refs[len(lefts) : len(lefts) + n_pieces]
        out_ref, sums_ref, sent_ref, w_ref, sems = refs[-5:]
        step = pl.program_id(0)

        @pl.when(step == 0)
        def _():
            weights.start(ids_ref, pieces, 0, w_ref, 0, width, sems)

        for i in range(per):
            weights.wait(step * per + i, w_ref, 0, width, sems)
        rows = pl.ds(pl.multiple_of(step * block, 16), block)
        back = (dot_nt(grad_ref[...], w_ref[rows, :]) * slope_ref[...]).astype(BF)
        out_ref[...] = back
        sums_ref[...] = jnp.broadcast_to(total_rows(back.astype(F32)), sums_ref.shape)
        left = jnp.concatenate([ref[...] for ref in left_refs], axis=1)
        sent_ref[...] = dot_tn(left, out_ref[...]).astype(BF)

    tile = pl.BlockSpec((count, block), lambda n, ids: (0, n))
    return kernel(
        body,
        "ffn_back",
        12,
        ids,
        (wide // block,),
        [(grad, whole(grad.shape)), (slope, tile)]
        + list(zip(lefts, left_specs))
        + [(p, ANY) for p in weights.arrays]
        + [(d, ANY) for d in deps],
        [
            (struct((count, wide), BF), tile),
            (struct((8, wide), F32), pl.BlockSpec((8, block), lambda n, ids: (0, n))),
            (
                struct((rows_out, wide), BF),
                pl.BlockSpec((rows_out, block), lambda n, ids: (0, n)),
            ),
        ],
        [pltpu.VMEM((wide, width), BF), pltpu.SemaphoreType.DMA((weights.count,))],
    )


def attention_norm_back(ids, inner_grad, ffn_grad, normed, inverse, inner, weights, vectors, deps):
    count, wide = inner_grad.shape
    width = normed.shape[1]
    tile = min(wide, 1024)
    steps = wide // tile
    n_pieces = len(weights.arrays)
    part_rows = 128

    def body(ids_ref, inverse_ref, vec_ref, grad_hbm, ffn_hbm, n_hbm, *refs):
        pieces = refs[:n_pieces]
        inner_pieces = refs[n_pieces : 2 * n_pieces]
        low_hbm, sum_hbm, mixed_hbm, sums_ref = refs[-17:-13]
        acc_ref, ffn_ref, n_ref, low_ref, mixed_ref, grad_ref, w_ref = refs[-13:-6]
        w_sems, o_ref, o_sems, sems, grad_sems, out_sems = refs[-6:]
        tiles = [slice(g * tile, (g + 1) * tile) for g in range(steps)]
        fetch = copies([(grad_hbm.at[:, t], grad_ref.at[:, t]) for t in tiles], grad_sems)
        for g in range(steps):
            fetch[g].start()
            inner.start(ids_ref, inner_pieces, g * tile, w_ref.at[g], 0, tile, w_sems.at[g])
        late = copies([(ffn_hbm, ffn_ref), (n_hbm, n_ref)], sems)
        start_all(late)
        weights.start(ids_ref, pieces, 3 * width, o_ref, 0, width, o_sems)
        acc_ref[...] = jnp.zeros_like(acc_ref)

        @pl.loop(0, steps)
        def _(g):
            there = grad_ref.at[:, aligned(g * tile, tile)]
            pltpu.make_async_copy(there, there, grad_sems.at[g]).wait()
            inner.wait_all(w_ref.at[g], 0, tile, w_sems.at[g])
            acc_ref[...] += dot_nt(there[...], w_ref[g])

        wait_for(late)
        sums_ref[...] = jnp.zeros_like(sums_ref)

        @pl.loop(0, count // part_rows)
        def _(part):
            rows = pl.ds(pl.multiple_of(part * part_rows, part_rows), part_rows)
            grad = acc_ref[rows, :] + ffn_ref[rows, :]
            normed_rows = n_ref[rows, :]
            back = normalise_back(grad * vec_ref[3:4], normed_rows, inverse_ref[rows, 0:1])
            low = back.astype(BF)
            low_ref[rows, :] = low
            acc_ref[rows, :] = back
            sums_ref[0:1, :] += total_rows(grad * normed_rows)
            sums_ref[1:2, :] += total_rows(grad)
            sums_ref[2:3, :] += total_rows(low.astype(F32))

        done = copies(
            [(low_ref, low_hbm), (acc_ref, sum_hbm), (mixed_ref, mixed_hbm)], out_sems
        )
        start_all(done[:2])
        weights.wait_all(o_ref, 0, width, o_sems)
        mixed_ref[...] = dot_nt(low_ref[...], o_ref[...]).astype(BF)
        done[2].start()
        wait_for(done)

    size = (count, width)
    return kernel(
        body,
        "attention_norm_back",
        16,
        ids,
        (1,),
        [(inverse, whole(inverse.shape)), (vectors, whole(vectors.shape))]
        + [
            (a, ANY)
            for a in [inner_grad, ffn_grad, normed] + weights.arrays + inner.arrays + list(deps)
        ],
        [
            (struct(size, BF), ANY),
            (struct(size, F32), ANY),
            (struct(size, BF), ANY),
            (struct((8, width), F32), whole((8, width))),
        ],
        [
            pltpu.VMEM(size, F32),
            pltpu.VMEM(size, F32),
            pltpu.VMEM(size, F32),
            pltpu.VMEM(size, BF),
            pltpu.VMEM(size, BF),
            pltpu.VMEM((count, wide), BF),
            pltpu.VMEM((steps, width, tile), BF),
            pltpu.SemaphoreType.DMA((steps, inner.count)),
            pltpu.VMEM((width, width), BF),
            pltpu.SemaphoreType.DMA((weights.count,)),
            pltpu.SemaphoreType.DMA((2,)),
            pltpu.SemaphoreType.DMA((steps,)),
            pltpu.SemaphoreType.DMA((3,)),
        ],
    )


def inputs_back(ids, base, grads, weights, deps):
    count, width = base.shape
    tile = 256
    per = tile // weights.block
    n_pieces = len(weights.arrays)

    def body(ids_ref, base_ref, q_ref, k_ref, v_ref, *refs):
        pieces = refs[:n_pieces]
        out_ref, w_ref, sems = refs[-3:]
        step = pl.program_id(0)

        @pl.when(step == 0)
        def _():
            weights.start(ids_ref, pieces, 0, w_ref, 0, 3 * width, sems)

        for i in range(per):
            weights.wait(step * per + i, w_ref, 0, 3 * width, sems)
        place = pl.ds(pl.multiple_of(step * tile, tile), tile)
        out = base_ref[...]
        for i, ref in enumerate((q_ref, k_ref, v_ref)):
            out = out + dot_nt(ref[...], w_ref[place, i * width : (i + 1) * width])
        out_ref[...] = out

    block = pl.BlockSpec((count, tile), lambda n, ids: (0, n))
    return kernel(
        body,
        "inputs_back",
        10,
        ids,
        (width // tile,),
        [(base, block)]
        + [(g, whole(g.shape)) for g in grads]
        + [(p, ANY) for p in weights.arrays]
        + [(d, ANY) for d in deps],
        [(struct(base.shape, F32), block)],
        [pltpu.VMEM((width, 3 * width), BF), pltpu.SemaphoreType.DMA((weights.count,))],
    )[0]


def split_hops(kept, bit):
    stay = [j for j in kept if not j & bit]
    return stay, [j | bit for j in stay]


class RowSum:
    def __init__(self, net, pairs, ids, tile):
        self.net, self.ids, self.tile = net, ids, tile
        self.rights = [right for _, right in pairs]
        self.left = []
        for left, _ in pairs:
            if not any(left is known for known in self.left):
                self.left.append(left)
        self.uses = [[left is known for known in self.left].index(True) for left, _ in pairs]
        self.width = self.left[0].shape[1] // (net.chips * 2)
        self.columns = sum(r.shape[1] for r in self.rights)
        bits = [1 << b for b in range(net.chips.bit_length() - 1)]
        self.bits = (bits, bits[::-1])
        self.kept = [list(range(net.chips))] * 2

    def lefts(self, core):
        net, width = self.net, self.width
        if width % 128 == 0:
            spec = [
                pl.BlockSpec(
                    (self.left[0].shape[0], width),
                    lambda n, ids, j=j: (0, (ids[0] ^ j) * 2 + (ids[1] ^ core)),
                )
                for j in range(net.chips)
            ]
            return [left for left in self.left for _ in spec], spec * len(self.left)
        chosen = []
        for left in self.left:
            picked = []
            for j in range(net.chips):
                at = ((self.ids[0] ^ j) * 2 + (self.ids[1] ^ core)) * width
                picked.append(lax.dynamic_slice_in_dim(left, at, width, axis=1))
            chosen.append(jnp.concatenate(picked, axis=1))
        return chosen, [whole(picked.shape) for picked in chosen]

    def multiply(self, name, micros, core, got, outs, groups, targets, deps):
        net, width, tile = self.net, self.width, self.tile
        rows, tokens = net.chips * width, self.left[0].shape[0]
        ready = width % 128 != 0
        lefts = self.lefts(core)[0] if ready else self.left
        tiles = []
        for right, use in zip(range(len(self.rights)), self.uses):
            for at in range(0, self.rights[right].shape[1], tile):
                tiles.append((right, at, use))
        extra = [] if got is None else [got]
        cuts = [t for t in range(1, len(tiles)) if tiles[t][2] != tiles[t - 1][2]]

        def body(ids_ref, *refs):
            left_hbm = refs[: len(lefts)]
            right_hbm = refs[len(lefts) : len(lefts) + len(self.rights)]
            got_hbm = refs[len(lefts) + len(self.rights)]
            scratch = refs[len(refs) - 7 - len(extra) :]
            out_hbm = refs[len(refs) - 7 - len(extra) - len(outs) : len(refs) - 7 - len(extra)]
            left_ref, right_ref, out_ref, left_sems, right_sems, got_sems, out_sems = scratch[:7]
            fetch_left = []
            for i, source in enumerate(left_hbm):
                if ready:
                    pairs = [(source, left_ref.at[i])]
                else:
                    pairs = []
                    for j in range(net.chips):
                        at = ((ids_ref[0] ^ j) * 2 + (ids_ref[1] ^ core)) * width
                        place = (slice(None), slice(j * width, (j + 1) * width))
                        pairs.append((source.at[:, aligned(at, width)], left_ref.at[i].at[place]))
                fetch_left.append(copies(pairs, left_sems, i))
            fetch_right = [
                pltpu.make_async_copy(
                    right_hbm[r].at[:, at : at + tile], right_ref.at[t], right_sems.at[t]
                )
                for t, (r, at, _) in enumerate(tiles)
            ]
            fetch_got = [
                pltpu.make_async_copy(
                    got_hbm.at[:, t * tile : (t + 1) * tile], scratch[7].at[t], got_sems.at[t]
                )
                for t in range(len(tiles) if extra else 0)
            ]
            waited = set()
            for t, (_, _, use) in enumerate(tiles):
                if use not in waited:
                    start_all(fetch_left[use])
                    waited.add(use)
                fetch_right[t].start()
                if extra:
                    fetch_got[t].start()
            def part(t, which):
                use = sum(((t >= cut).astype(jnp.int32) for cut in cuts), jnp.int32(0))
                there = [right_ref.at[t]] + [ref.at[t] for ref in scratch[7:]]
                for ref, sems in zip(there, (right_sems, got_sems)):
                    pltpu.make_async_copy(ref, ref, sems.at[t]).wait()
                value = dot_tn(left_ref[use], right_ref[t])
                for ref in there[1:]:
                    value = value + ref[...].astype(F32)
                out_ref[t] = value.astype(BF)
                return copies(
                    [
                        (
                            out_ref.at[t].at[first : first + n, :],
                            out_hbm[kind].at[row : row + n, aligned(column, tile)],
                        )
                        for first, n, kind, row, column in targets(t, which)
                    ],
                    out_sems,
                    t,
                )

            count = len(tiles)
            group = count // groups
            waited = 0
            for which in range(groups):
                last = tiles[(which + 1) * group - 1][2]
                while waited <= last:
                    wait_for(fetch_left[waited])
                    waited += 1

                @pl.loop(which * group, (which + 1) * group)
                def _(t):
                    start_all(part(t, which))

            for t in range(count):
                wait_for(
                    pltpu.make_async_copy(
                        out_ref.at[t].at[first : first + n, :],
                        out_ref.at[t].at[first : first + n, :],
                        out_sems.at[t, i],
                    )
                    for i, (first, n, _, _, _) in enumerate(targets(t, t // group))
                )

        count = len(tiles)
        return kernel(
            body,
            name,
            micros,
            self.ids,
            (1,),
            [(a, ANY) for a in list(lefts) + self.rights + extra + list(deps)],
            [(o, ANY) for o in outs],
            [
                pltpu.VMEM((len(lefts), tokens, rows), BF),
                pltpu.VMEM((count, tokens, tile), BF),
                pltpu.VMEM((count, rows, tile), BF),
                pltpu.SemaphoreType.DMA((len(lefts), net.chips)),
                pltpu.SemaphoreType.DMA((count,)),
                pltpu.SemaphoreType.DMA((count,)),
                pltpu.SemaphoreType.DMA((count, net.chips)),
            ]
            + [pltpu.VMEM((count, rows, tile), BF) for _ in extra],
        )

    def other_core(self, *deps):
        rows = self.net.chips * self.width
        (self.sent,) = self.multiply(
            "rows_of_other_core",
            7,
            1,
            None,
            [struct((rows, self.columns), BF)],
            1,
            lambda t, _: [(0, rows, 0, 0, t * self.tile)],
            deps,
        )
        return self.exchange(self.sent)

    def exchange(self, sent):
        self.got = self.net.across_core(sent)
        return sent

    def own_core(self, *deps):
        rows, tile, width = self.net.chips * self.width, self.tile, self.width
        half = self.columns // tile // 2
        sides = [split_hops(self.kept[s], self.bits[s][0]) for s in range(2)]

        def targets(t, side):
            return [
                (j * width, width, side * 2 + which, i * width, (t - side * half) * tile)
                for which, hops in enumerate(sides[side])
                for i, j in enumerate(hops)
            ]

        out = self.multiply(
            "rows_of_own_core",
            9,
            0,
            self.got,
            [struct((rows // 2, self.columns // 2), BF)] * 4,
            2,
            targets,
            deps,
        )
        self.held = [out[0], out[2]]
        self.away = [out[1], out[3]]
        self.send()
        return out[0]

    def send(self):
        for s in range(2):
            self.kept[s] = split_hops(self.kept[s], self.bits[s][0])[0]
        self.arrived = [self.net.across_chip(self.away[s], self.bits[s][0]) for s in range(2)]
        self.bits = (self.bits[0][1:], self.bits[1][1:])

    def fold(self, *deps):
        rows, columns = self.held[0].shape
        tile = columns // 2
        sides = [split_hops(self.kept[s], self.bits[s][0]) for s in range(2)]

        def body(ids_ref, *refs):
            out_refs = refs[-4:]
            for s in range(2):
                for which, hops in enumerate(sides[s]):
                    for i, j in enumerate(hops):
                        at = self.kept[s].index(j) * self.width
                        part = slice(at, at + self.width)
                        value = refs[2 * s][part, :].astype(F32) + refs[2 * s + 1][part, :].astype(F32)
                        out_refs[2 * s + which][i * self.width : (i + 1) * self.width, :] = (
                            value.astype(BF)
                        )

        block = pl.BlockSpec((rows, tile), lambda n, ids: (0, n))
        half = pl.BlockSpec((rows // 2, tile), lambda n, ids: (0, n))
        out = kernel(
            body,
            "fold",
            4,
            self.ids,
            (columns // tile,),
            [(a, block) for s in range(2) for a in (self.held[s], self.arrived[s])]
            + [(d, ANY) for d in deps],
            [(struct((rows // 2, columns), BF), half)] * 4,
            [],
        )
        self.held = [out[0], out[2]]
        self.away = [out[1], out[3]]
        self.send()
        return self.fold() if self.bits[0] else out[0]

    def fold_z(self, *deps):
        net, count = self.net, self.net.inner
        columns = self.held[0].shape[1]
        rows = self.width // count
        stay, leave = split_hops(list(range(count)), 1)
        size = (rows * len(stay), 2 * columns)
        if rows % 16:
            held = tie(jnp.concatenate(self.held, axis=1), *deps).astype(F32)
            held = held + jnp.concatenate(self.arrived, axis=1).astype(F32)
            held = held.reshape(count, rows, -1).astype(BF)
            keep, away = (
                jnp.take(held, jnp.array(hops) ^ self.ids[2], axis=0).reshape(size)
                for hops in (stay, leave)
            )
        else:

            def body(ids_ref, *refs):
                for out_ref, hops in zip(refs[-2:], (stay, leave)):
                    for i, s in enumerate(hops):
                        at = pl.ds(pl.multiple_of((ids_ref[2] ^ s) * rows, 16), rows)
                        for side in range(2):
                            value = refs[2 * side][at, :].astype(F32)
                            value = value + refs[2 * side + 1][at, :].astype(F32)
                            place = slice(side * columns, (side + 1) * columns)
                            out_ref[i * rows : (i + 1) * rows, place] = value.astype(BF)

            keep, away = kernel(
                body,
                "fold_z",
                3,
                self.ids,
                (1,),
                [
                    (a, whole(a.shape))
                    for s in range(2)
                    for a in (self.held[s], self.arrived[s])
                ]
                + [(d, ANY) for d in deps],
                [(struct(size, BF), whole(size))] * 2,
                [],
            )
        self.total, self.came, self.reach = keep, net.swap(away, 1), 1
        return keep

    def fold_direct(self, *deps):
        net, count = self.net, self.net.inner
        columns = self.held[0].shape[1]
        rows = self.width // count
        self.parts = None
        if rows % 16 or count > 4:
            self.fold_z(*deps)
            return self.fold_far()

        def body(ids_ref, *refs):
            for s in range(count):
                at = pl.ds(pl.multiple_of((ids_ref[2] ^ s) * rows, 16), rows)
                out_ref = refs[s - count]
                for side in range(2):
                    value = refs[2 * side][at, :].astype(F32)
                    value = value + refs[2 * side + 1][at, :].astype(F32)
                    place = slice(side * columns, (side + 1) * columns)
                    out_ref[:, place] = value.astype(out_ref.dtype)

        size = (rows, 2 * columns)
        parts = kernel(
            body,
            "fold_direct",
            3,
            self.ids,
            (1,),
            [(a, whole(a.shape)) for s in range(2) for a in (self.held[s], self.arrived[s])]
            + [(d, ANY) for d in deps],
            [(struct(size, F32), whole(size))] + [(struct(size, BF), whole(size))] * (count - 1),
            [],
        )
        self.parts = [parts[0]] + [net.swap(parts[s], s) for s in range(1, count)]
        return parts[0]

    def finish_direct(self):
        if self.parts is None:
            return self.finish()
        total = self.parts[0]
        for part in self.parts[1:]:
            total = total + part.astype(F32)
        return total

    def fold_far(self, *deps):
        while self.reach * 2 < self.net.inner:
            self.reach *= 2
            total = tie(self.total, *deps).astype(F32) + self.came.astype(F32)
            rows = self.width // self.net.inner
            count = total.shape[0] // rows
            stay = [i for i in range(count) if not i & 1]
            blocks = total.reshape(count, rows, -1)
            away = jnp.concatenate([blocks[i + 1] for i in stay], axis=0).astype(BF)
            self.total = jnp.concatenate([blocks[i] for i in stay], axis=0)
            self.came = self.net.swap(away, self.reach)
        return self.came

    def finish(self, *deps):
        return tie(self.total, *deps).astype(F32) + self.came.astype(F32)


class ZFirst:
    def __init__(self, rows_sum):
        self.sum, self.net = rows_sum, rows_sum.net
        self.low = rows_sum.width // self.net.inner
        self.usual = self.net.inner != 4 or len(rows_sum.bits[0]) != 1 or self.low % 16 != 0

    def cross_near(self, *deps):
        source, low = self.sum, self.low
        if self.usual:
            source.fold(*deps)
            return source.fold_z()
        columns = source.held[0].shape[1]
        split = split_hops(list(range(4)), 1)
        sides = [split_hops(source.kept[s], source.bits[s][0]) for s in range(2)]
        size = (4 * low, 2 * columns)

        def body(ids_ref, *refs):
            for out_ref, zs in zip(refs[-2:], split):
                for i, z in enumerate(zs):
                    for s in range(2):
                        for h in range(2):
                            at = source.kept[s].index(sides[s][h][0]) * source.width
                            at = pl.multiple_of(at + (ids_ref[2] ^ z) * low, 16)
                            value = refs[2 * s][pl.ds(at, low), :].astype(F32)
                            value = value + refs[2 * s + 1][pl.ds(at, low), :].astype(F32)
                            row = (2 * i + h) * low
                            out_ref[row : row + low, s * columns : (s + 1) * columns] = (
                                value.astype(BF)
                            )

        self.keep, away = kernel(
            body,
            "cross_near",
            6,
            source.ids,
            (1,),
            [
                (a, whole(a.shape))
                for s in range(2)
                for a in (source.held[s], source.arrived[s])
            ]
            + [(d, ANY) for d in deps],
            [(struct(size, BF), whole(size))] * 2,
            [],
        )
        self.came = self.net.swap(away, 1)
        return self.keep

    def halve(self, *deps):
        total = tie(self.keep, *deps).astype(F32) + self.came.astype(F32)
        half = total.shape[0] // 2
        self.keep = total[:half].astype(BF)
        return total[half:].astype(BF)

    def cross_far(self, *deps):
        if self.usual:
            return self.sum.fold_far(*deps)
        self.came = self.net.swap(self.halve(*deps), 2)
        return self.came

    def cross_chip(self, *deps):
        if self.usual:
            return None
        away = self.halve(*deps)
        half = away.shape[1] // 2
        parts = [
            self.net.across_chip(away[:, s * half : (s + 1) * half], self.sum.bits[s][0])
            for s in range(2)
        ]
        self.came = jnp.concatenate(parts, axis=1)
        return None

    def finish(self, *deps):
        if self.usual:
            return self.sum.finish(*deps)
        return tie(self.keep, *deps).astype(F32) + self.came.astype(F32)


def shards(
    net,
    inputs,
    segment_ids,
    query_weight,
    key_weight,
    value_weight,
    output_weight,
    query_bias,
    value_bias,
    output_bias,
    attn_gain,
    attn_shift,
    inner_weight,
    inner_bias,
    outer_weight,
    outer_bias,
    ffn_gain,
    ffn_shift,
    out_grad,
):
    row_count, seq_len, width = inputs.shape
    tokens = inputs.reshape(row_count * seq_len, width)
    _, ids = net.place()
    small = [
        query_bias,
        value_bias,
        output_bias,
        attn_gain,
        attn_shift,
        outer_bias,
        ffn_gain,
        ffn_shift,
        inner_bias,
    ]
    mine = query_bias.shape[0]
    shard = first_shard([query_weight, key_weight, value_weight, output_weight], small)
    gather_a = Gather(net, shard, ids, True)
    gather_a.ordered()
    gather_a.plane()
    gather_b = Gather(net, tie(inner_weight, gather_a.block), ids, True)
    gather_a.relay(*gather_b.along)
    gather_b.ordered()
    weights_a = gather_a.cores()
    gather_b.plane(*weights_a.arrays)
    queries, keys, values, vectors = project(ids, tokens, weights_a)
    spread = inner_bias.shape[0] // mine
    inner_bias_full = vectors[8 : 8 + spread].reshape(spread, net.count, mine)
    inner_bias_full = inner_bias_full.swapaxes(0, 1).reshape(1, -1)
    mixed, totals = attend_forward(segment_ids, queries, keys, values)
    gather_c = Gather(net, tie(outer_weight, queries), ids, True, mixed)
    arrived = gather_b.relay(mixed)
    normed, inverse, normed_low = close_attention(ids, mixed, tokens, weights_a, vectors)
    gather_c.ordered(normed_low)
    gather_c.plane(*arrived)
    weights_b = gather_b.cores()
    act, slope = ffn_in(ids, normed_low, weights_b, inner_bias_full)
    gather_c.relay(act)
    weights_c = gather_c.cores()
    grad_out = out_grad.reshape(tokens.shape)
    outputs, ffn_grad, branch_grad, ffn_sums, sent = ffn_out(
        ids, act, normed, grad_out, weights_c, vectors
    )
    outer_sum = RowSum(net, [(act, branch_grad)], ids, 256)
    last = outer_sum.exchange(sent)
    lefts = RowSum(net, [(normed_low, slope)], ids, 1024).lefts(1)
    inner_grad, inner_sums, sent = ffn_back(ids, branch_grad, slope, weights_c, *lefts, [last])
    inner_sum = RowSum(net, [(normed_low, inner_grad)], ids, 1024)
    last = inner_sum.exchange(sent)
    last = outer_sum.own_core(last)
    attn_grad, attn_sum_grad, mixed_grad, attn_sums = attention_norm_back(
        ids, inner_grad, ffn_grad, normed, inverse, weights_b, weights_a, vectors, [last]
    )
    last = inner_sum.own_core(attn_grad)
    query_grad, key_grad, value_grad, grad_query_bias, grad_value_bias = attend_backward(
        segment_ids, queries, keys, values, mixed_grad, totals, [last, *outer_sum.arrived]
    )
    inputs_sum = RowSum(
        net,
        [(mixed, attn_grad)] + [(tokens, g) for g in (query_grad, key_grad, value_grad)],
        ids,
        1024,
    )
    outer = ZFirst(outer_sum)
    last = outer.cross_near(query_grad)
    last = inputs_sum.other_core(last, *inner_sum.arrived)
    last = inner_sum.fold(last)
    last = inputs_sum.own_core(last)
    last = inner_sum.fold_z(last)
    outer.cross_far(last)
    last = inputs_sum.fold(last)
    inner_sum.fold_far(last)
    input_grad = inputs_back(
        ids, attn_sum_grad, (query_grad, key_grad, value_grad), weights_a, [last]
    )
    last = inputs_sum.fold_direct(input_grad)
    outer.cross_chip(last)
    shard_inner = inner_sum.finish(last)
    shard_outer = outer.finish(last)
    shard_inputs = inputs_sum.finish_direct()
    shard_output, shard_query, shard_key, shard_value = (
        shard_inputs[:, i * width : (i + 1) * width] for i in range(4)
    )
    rows = jnp.concatenate(
        [grad_query_bias[None], grad_value_bias[None], attn_sums[:3], ffn_sums[:3]], axis=0
    )
    rows = rows.reshape(8, net.count, mine).swapaxes(0, 1).reshape(net.count, 8 * mine)
    packed = jnp.concatenate([rows, inner_sums[0].reshape(net.count, -1)], axis=1)
    packed = tie(packed, inputs_sum.parts[1] if inputs_sum.parts else last)
    summed = jnp.sum(lax.all_to_all(packed, AXES, 0, 0, tiled=True), axis=0)
    vector = [summed[i * mine : (i + 1) * mine] for i in range(8)]
    return (
        outputs.reshape(inputs.shape),
        input_grad.reshape(inputs.shape),
        shard_query,
        shard_key,
        shard_value,
        shard_output,
        vector[0],
        vector[1],
        vector[4],
        vector[2],
        vector[3],
        shard_inner,
        summed[8 * mine :],
        shard_outer,
        vector[7],
        vector[5],
        vector[6],
    )


def solution(mesh):
    placed = (
        P(("dp", "fsdp"), None, None),
        P(("dp", "fsdp"), None),
        P(("dp", "fsdp"), None),
        P(("dp", "fsdp"), None),
        P(("dp", "fsdp"), None),
        P(("dp", "fsdp"), None),
        P(("dp", "fsdp")),
        P(("dp", "fsdp")),
        P(("dp", "fsdp")),
        P(("dp", "fsdp")),
        P(("dp", "fsdp")),
        P(("dp", "fsdp"), None),
        P(("dp", "fsdp")),
        P(("dp", "fsdp"), None),
        P(("dp", "fsdp")),
        P(("dp", "fsdp")),
        P(("dp", "fsdp")),
        P(("dp", "fsdp"), None, None),
    )
    return jax.shard_map(
        functools.partial(shards, Slice(mesh.shape["dp"], mesh.shape["fsdp"])),
        mesh=mesh,
        in_specs=placed,
        out_specs=(
            P(("dp", "fsdp"), None, None),
            P(("dp", "fsdp"), None, None),
            P(("dp", "fsdp"), None),
            P(("dp", "fsdp"), None),
            P(("dp", "fsdp"), None),
            P(("dp", "fsdp"), None),
            P(("dp", "fsdp")),
            P(("dp", "fsdp")),
            P(("dp", "fsdp")),
            P(("dp", "fsdp")),
            P(("dp", "fsdp")),
            P(("dp", "fsdp"), None),
            P(("dp", "fsdp")),
            P(("dp", "fsdp"), None),
            P(("dp", "fsdp")),
            P(("dp", "fsdp")),
            P(("dp", "fsdp")),
        ),
        check_vma=False,
    )
```

```python
import functools

import jax
import jax.numpy as jnp
from jax import lax
from jax.experimental import pallas as pl
from jax.experimental.pallas import tpu as pltpu
from jax.sharding import PartitionSpec as P

H = 16
HD = 64
AXES = ("dp", "fsdp")
BF = jnp.bfloat16
F32 = jnp.float32
EPSILON = 1e-05
NT = (((1,), (1,)), ((), ()))
TN = (((0,), (0,)), ((), ()))
MASKED = -1e30
WEIGHT = 0.3


def spend(micros):
    return pl.CostEstimate(flops=1, bytes_accessed=int(micros * WEIGHT * 1e6), transcendentals=0)


ANY = pl.BlockSpec(memory_space=pl.ANY)


def whole(shape):
    return pl.BlockSpec(shape, lambda *_: (0,) * len(shape))


def struct(shape, dtype):
    return jax.ShapeDtypeStruct(shape, dtype)


def dot(left, right):
    return jnp.dot(left, right, preferred_element_type=F32)


def dot_tn(left, right):
    return lax.dot_general(left, right, TN, preferred_element_type=F32)


def dot_nt(left, right):
    return lax.dot_general(left, right, NT, preferred_element_type=F32)


def tie(value, *after):
    return lax.optimization_barrier((value, *after))[0]


def normalise(rows):
    centred = rows - jnp.mean(rows, axis=-1, keepdims=True)
    spread = jnp.mean(centred * centred, axis=-1, keepdims=True)
    inverse = lax.rsqrt(spread + EPSILON)
    return centred * inverse, inverse


def normalise_back(cotangent, normed, inverse):
    slope = jnp.mean(cotangent * normed, axis=-1, keepdims=True)
    return inverse * (cotangent - jnp.mean(cotangent, axis=-1, keepdims=True) - normed * slope)


def total_rows(matrix):
    return jnp.sum(matrix, axis=0, keepdims=True)


def lane_half(block, which):
    lane = lax.broadcasted_iota(jnp.int32, block.shape, 1)
    return jnp.where((lane >= HD) == (which == 1), block, jnp.zeros_like(block))


def set_mask(seg_ref, mask_ref):
    seg_row = seg_ref[...].astype(F32)
    seg_col = jnp.broadcast_to(seg_row, (128, seg_row.shape[1])).T
    for at in range(0, seg_row.shape[1], 128):
        same = seg_col == seg_row[:, at : at + 128]
        mask_ref[:, at : at + 128] = jnp.where(same, 0.0, MASKED)


def attend_forward_body(seg_ref, q_ref, k_ref, v_ref, mixed_ref, total_ref, mask_ref):
    @pl.when(pl.program_id(1) == 0)
    def _():
        set_mask(seg_ref, mask_ref)

    query = q_ref[...] * jnp.bfloat16(HD**-0.5)
    key = k_ref[...]
    value_t = v_ref[...].T
    halves = []
    for h in range(2):
        scores = lax.dot_general(lane_half(key, h), query, NT, preferred_element_type=F32)
        scores = scores + mask_ref[...]
        high = jnp.max(scores, axis=0, keepdims=True)
        raised = jnp.exp(scores - high)
        total = jnp.sum(raised, axis=0, keepdims=True)
        low = (raised * (1.0 / total)).astype(BF)
        rows = value_t[h * HD : (h + 1) * HD]
        halves.append(jnp.dot(rows, low, preferred_element_type=F32))
        total_ref[0, h : h + 1, :] = high + jnp.log(total)
    mixed_ref[...] = jnp.concatenate(halves, axis=0).T.astype(BF)


def attend_backward_body(
    seg_ref, q_ref, k_ref, v_ref, g_ref, total_ref, *rest
):
    dq_ref, dk_ref, dv_ref, dq_sum_ref, dv_sum_ref, mask_ref = rest[-6:]

    @pl.when(pl.program_id(1) == 0)
    def _():
        set_mask(seg_ref, mask_ref)

    scale = HD**-0.5
    query = q_ref[...] * jnp.bfloat16(scale)
    key, value, grad = k_ref[...], v_ref[...], g_ref[...]
    key_t = key.T
    lane = lax.broadcasted_iota(jnp.int32, key.shape, 1)
    dq_t, dk, dv = [], None, None
    for h in range(2):
        scores = lax.dot_general(lane_half(key, h), query, NT, preferred_element_type=F32)
        probs = jnp.exp(scores + mask_ref[...] - total_ref[0, h : h + 1, :])
        prob_grad = lax.dot_general(lane_half(value, h), grad, NT, preferred_element_type=F32)
        inner_sum = jnp.sum(probs * prob_grad, axis=0, keepdims=True)
        score_grad = (probs * (prob_grad - inner_sum)).astype(BF)
        dv_h = jnp.dot(probs.astype(BF), grad, preferred_element_type=F32)
        dk_h = jnp.dot(score_grad, query, preferred_element_type=F32)
        dv = dv_h if h == 0 else jnp.where(lane < HD, dv, dv_h)
        dk = dk_h if h == 0 else jnp.where(lane < HD, dk, dk_h)
        rows = key_t[h * HD : (h + 1) * HD]
        dq_t.append(jnp.dot(rows, score_grad, preferred_element_type=F32))
    dq = (jnp.concatenate(dq_t, axis=0).T * scale).astype(BF)
    dv = dv.astype(BF)
    dq_ref[...] = dq
    dk_ref[...] = dk.astype(BF)
    dv_ref[...] = dv
    wide = (8, dq.shape[1])
    dq_sum_ref[0] = jnp.broadcast_to(jnp.sum(dq.astype(F32), axis=0, keepdims=True), wide)
    dv_sum_ref[0] = jnp.broadcast_to(jnp.sum(dv.astype(F32), axis=0, keepdims=True), wide)


def attention_specs(seq_len, deps):
    block = pl.BlockSpec((seq_len, 2 * HD), lambda r, n: (r, n))
    seg = pl.BlockSpec((None, 1, seq_len), lambda r, n: (r, 0, 0))
    total = pl.BlockSpec((None, 1, 8, seq_len), lambda r, n: (r, n, 0, 0))
    sums = pl.BlockSpec((1, 8, 2 * HD), lambda r, n: (r, 0, n))
    return block, seg, total, sums, [pl.BlockSpec(memory_space=pl.ANY)] * deps


def attend_forward(seg, queries, keys, values):
    rows, seq_len = seg.shape
    block, seg_spec, total, _, _ = attention_specs(seq_len, 0)
    tokens, width = queries.shape
    pairs = width // (2 * HD)
    return pl.pallas_call(
        attend_forward_body,
        out_shape=[
            jax.ShapeDtypeStruct((tokens, width), BF),
            jax.ShapeDtypeStruct((rows, pairs, 8, seq_len), F32),
        ],
        grid=(rows, pairs),
        in_specs=[seg_spec, block, block, block],
        out_specs=[block, total],
        scratch_shapes=[pltpu.VMEM((seq_len, seq_len), F32)],
        name="attend_forward",
        cost_estimate=spend(13),
    )(seg.reshape(rows, 1, seq_len), queries, keys, values)


def attend_backward(seg, queries, keys, values, mixed_grad, totals, deps):
    rows, seq_len = seg.shape
    block, seg_spec, total, sums, extra = attention_specs(seq_len, len(deps))
    tokens, width = queries.shape
    pairs = width // (2 * HD)
    outs = pl.pallas_call(
        attend_backward_body,
        out_shape=[jax.ShapeDtypeStruct((tokens, width), BF)] * 3
        + [jax.ShapeDtypeStruct((rows, 8, width), F32)] * 2,
        grid=(rows, pairs),
        in_specs=[seg_spec, block, block, block, block, total] + extra,
        out_specs=[block, block, block, sums, sums],
        scratch_shapes=[pltpu.VMEM((seq_len, seq_len), F32)],
        name="attend_backward",
        cost_estimate=spend(17),
    )(seg.reshape(rows, 1, seq_len), queries, keys, values, mixed_grad, totals, *deps)
    dq, dk, dv, dq_sum, dv_sum = outs
    return dq, dk, dv, jnp.sum(dq_sum[:, 0], axis=0), jnp.sum(dv_sum[:, 0], axis=0)


class Slice:
    def __init__(self, dp, inner):
        self.inner, self.chips, self.count = inner, dp // 2, dp * inner

    def swap(self, value, mask):
        pairs = [(i, i ^ mask) for i in range(self.count)]
        return lax.ppermute(value, AXES, pairs)

    def across_core(self, value):
        return self.swap(value, self.inner)

    def across_chip(self, value, hop):
        return self.swap(value, hop * 2 * self.inner)

    def place(self):
        me = lax.axis_index(AXES)
        z = me % self.inner
        core = (me // self.inner) % 2
        return me, jnp.stack([me // (2 * self.inner), core, z]).astype(jnp.int32)


def first_shard(matrices, vectors):
    rows = matrices[0].shape[0]
    columns = sum(p.shape[1] for p in matrices)

    def body(*refs):
        out_ref, turn_ref = refs[-2:]
        at = 0
        for ref in refs[: len(matrices)]:
            out_ref[:, at : at + ref.shape[1]] = ref[...]
            at += ref.shape[1]
        turn_ref[...] = jnp.zeros_like(turn_ref)
        row = 0
        for ref in refs[len(matrices) : -2]:
            for start in range(0, ref.shape[1], rows):
                turn_ref[row : row + 1, 0:rows] = ref[:, start : start + rows].astype(F32)
                row += 1
        out_ref[:, at:] = turn_ref[...].T[0:rows].astype(BF)

    return pl.pallas_call(
        body,
        out_shape=struct((rows, columns + 128), BF),
        scratch_shapes=[pltpu.VMEM((128, 128), F32)],
        name="first_shard",
        cost_estimate=spend(2),
    )(*matrices, *[v.reshape(1, -1) for v in vectors])


def in_z_order(net, parts, ids):
    rows, columns = parts[0].shape
    if rows % 16:
        stacked = jnp.stack(parts)
        return jnp.take(stacked, jnp.arange(net.inner) ^ ids[2], axis=0).reshape(-1, columns)
    tile = columns

    def body(ids_ref, *refs):
        for s, part in enumerate(refs[:-1]):
            row = (ids_ref[2] ^ s) * rows
            refs[-1][pl.ds(pl.multiple_of(row, rows), rows), :] = part[...]

    return pl.pallas_call(
        body,
        out_shape=struct((net.inner * rows, columns), BF),
        grid_spec=pltpu.PrefetchScalarGridSpec(
            num_scalar_prefetch=1,
            grid=(columns // tile,),
            in_specs=[pl.BlockSpec((rows, tile), lambda n, ids: (0, n))] * net.inner,
            out_specs=pl.BlockSpec((net.inner * rows, tile), lambda n, ids: (0, n)),
        ),
        name="in_z_order",
        cost_estimate=spend(3),
    )(ids, *parts)


class Gather:
    def __init__(self, net, shard, ids, relay, *late):
        self.net, self.ids = net, ids
        self.relayed = relay and net.chips == 4
        self.along = [shard]
        reach = net.inner // 2
        while reach:
            if late and len(self.along) > 1:
                self.along[1:] = [tie(part, *late) for part in self.along[1:]]
            self.along = [
                part
                for near in self.along
                for part in (near, net.swap(near, reach))
            ]
            reach //= 2
        order = [0]
        reach = net.inner // 2
        while reach:
            order = [s ^ far for s in order for far in (0, reach)]
            reach //= 2
        self.along = [self.along[order.index(s)] for s in range(net.inner)]

    def ordered(self, *after):
        parts = list(lax.optimization_barrier((*self.along, *after))[: self.net.inner])
        self.block = in_z_order(self.net, parts, self.ids)
        self.rows = self.block.shape[0]
        return self.block

    def plane(self, *after):
        net = self.net
        self.pieces = [(self.block, 0, 0, 0)]
        hops = range(1, 3 if self.relayed else net.chips)
        sent = tie(self.block, *after)
        self.pieces += [(net.across_chip(sent, j), j, 0, 0) for j in hops]

    def relay(self, *after):
        net = self.net
        if self.relayed:
            half = self.rows // 2
            first, second = self.pieces[1][0], self.pieces[2][0]
            low = net.across_chip(tie(first, second, *after)[:half], 2)
            high = net.across_chip(tie(second, first, *after)[half:], 1)
            self.pieces += [(low, 3, 0, 0), (high, 3, 0, half)]
        return [p for p, _, _, _ in self.pieces]

    def cores(self, *after):
        across = [(self.net.across_core(tie(p, *after)), j, 1, s) for p, j, _, s in self.pieces]
        return Rows(self.net, self.rows, self.pieces + across)


class Rows:
    def __init__(self, net, block, pieces):
        self.block = block
        self.count = net.chips * 2
        self.arrays = [p for p, _, _, _ in pieces]
        self.meta = [(p.shape[0], j, c, s) for p, j, c, s in pieces]

    def after(self, *others):
        again = Rows.__new__(Rows)
        again.block, again.count, again.meta = self.block, self.count, self.meta
        tied = lax.optimization_barrier((*self.arrays, *others))
        again.arrays = list(tied[: len(self.arrays)])
        return again

    def start(self, ids_ref, refs, column, target, at, width, sems, hop=None):
        for ref, (rows, j, c, s) in zip(refs, self.meta):
            if hop is not None and j != hop:
                continue
            block = (ids_ref[0] ^ j) * 2 + (ids_ref[1] ^ c)
            row = pl.multiple_of(block * self.block + s, 16)
            pltpu.make_async_copy(
                ref.at[:, pl.ds(column, width)],
                target.at[pl.ds(row, rows), pl.ds(at, width)],
                sems.at[block],
            ).start()

    def wait(self, block, target, at, width, sems):
        row = block * self.block
        if not isinstance(row, int):
            row = pl.multiple_of(row, 16)
        there = target.at[pl.ds(row, self.block), pl.ds(at, width)]
        pltpu.make_async_copy(there, there, sems.at[block]).wait()

    def wait_all(self, target, at, width, sems):
        for block in range(self.count):
            self.wait(block, target, at, width, sems)


def copies(pairs, sems, *at):
    return [
        pltpu.make_async_copy(source, target, sems.at[(*at, i)])
        for i, (source, target) in enumerate(pairs)
    ]


def start_all(some):
    for copy in some:
        copy.start()


def wait_for(some):
    for copy in some:
        copy.wait()


def aligned(start, size):
    return pl.ds(pl.multiple_of(start, 128), size)


def kernel(body, name, micros, ids, grid, operands, outs, scratch):
    return pl.pallas_call(
        body,
        out_shape=[o for o, _ in outs],
        grid_spec=pltpu.PrefetchScalarGridSpec(
            num_scalar_prefetch=1,
            grid=grid,
            in_specs=[s for _, s in operands],
            out_specs=[s for _, s in outs],
            scratch_shapes=scratch,
        ),
        name=name,
        cost_estimate=spend(micros),
    )(ids, *[o for o, _ in operands])


def project(ids, tokens, weights):
    count, width = tokens.shape
    tile = min(width, 1024)
    per = width // tile
    n_pieces = len(weights.arrays)

    def body(ids_ref, x_ref, *refs):
        pieces = refs[:n_pieces]
        outs = refs[n_pieces : n_pieces + 3]
        vec_ref, w_ref, s_ref, sems = refs[n_pieces + 3 :]
        step = pl.program_id(0)

        @pl.when(step == 0)
        def _():
            weights.start(ids_ref, pieces, 4 * width, s_ref, 0, 128, sems.at[3])
            for i in range(3):
                weights.start(ids_ref, pieces, i * width, w_ref, i * width, width, sems.at[i])
            weights.wait_all(s_ref, 0, 128, sems.at[3])
            vec_ref[...] = s_ref[...].astype(F32).T[0 : vec_ref.shape[0]]

        for i, row in enumerate((0, None, 1)):

            @pl.when(step == i * per)
            def _():
                weights.wait_all(w_ref, i * width, width, sems.at[i])

            @pl.when((step >= i * per) & (step < (i + 1) * per))
            def _():
                columns = pl.ds(pl.multiple_of(step * tile, tile), tile)
                out = dot(x_ref[...], w_ref[:, columns])
                if row is not None:
                    inside = pl.ds(pl.multiple_of((step - i * per) * tile, tile), tile)
                    out = out + vec_ref[row : row + 1, inside]
                outs[i][...] = out.astype(BF)

    def out_spec(i):
        return pl.BlockSpec((count, tile), lambda n, ids: (0, jnp.clip(n - i * per, 0, per - 1)))

    return kernel(
        body,
        "project",
        10,
        ids,
        (3 * per,),
        [(tokens, whole(tokens.shape))] + [(p, ANY) for p in weights.arrays],
        [(struct(tokens.shape, BF), out_spec(i)) for i in range(3)]
        + [(struct((16, width), F32), whole((16, width)))],
        [
            pltpu.VMEM((width, 3 * width), BF),
            pltpu.VMEM((width, 128), BF),
            pltpu.SemaphoreType.DMA((4, weights.count)),
        ],
    )


def close_attention(ids, mixed, tokens, weights, vectors):
    count, width = tokens.shape
    rows = 256
    n_pieces = len(weights.arrays)

    def body(ids_ref, m_ref, x_ref, vec_ref, *refs):
        pieces = refs[:n_pieces]
        normed_ref, inverse_ref, low_ref, w_ref, sems = refs[n_pieces:]

        @pl.when(pl.program_id(0) == 0)
        def _():
            weights.start(ids_ref, pieces, 3 * width, w_ref, 0, width, sems)
            weights.wait_all(w_ref, 0, width, sems)

        total = x_ref[...].astype(F32) + (dot(m_ref[...], w_ref[...]) + vec_ref[2:3])
        normed, inverse = normalise(total)
        normed_ref[...] = normed
        inverse_ref[...] = jnp.broadcast_to(inverse, inverse_ref.shape)
        low_ref[...] = (normed * vec_ref[3:4] + vec_ref[4:5]).astype(BF)

    block = pl.BlockSpec((rows, width), lambda n, ids: (n, 0))
    return kernel(
        body,
        "close_attention",
        7,
        ids,
        (count // rows,),
        [(mixed, block), (tokens, block), (vectors, whole(vectors.shape))]
        + [(p, ANY) for p in weights.arrays],
        [
            (struct((count, width), F32), block),
            (struct((count, 128), F32), pl.BlockSpec((rows, 128), lambda n, ids: (n, 0))),
            (struct((count, width), BF), block),
        ],
        [pltpu.VMEM((width, width), BF), pltpu.SemaphoreType.DMA((weights.count,))],
    )


def ffn_in(ids, low, weights, bias):
    count, width = low.shape
    wide = bias.shape[1]
    tile = 1024
    n_pieces = len(weights.arrays)

    def body(ids_ref, x_ref, bias_ref, *refs):
        pieces = refs[:n_pieces]
        act_ref, slope_ref, w_ref, sems = refs[n_pieces:]
        step = pl.program_id(0)

        @pl.when(step == 0)
        def _():
            for g in range(wide // tile):
                weights.start(ids_ref, pieces, g * tile, w_ref.at[g], 0, tile, sems.at[g])

        weights.wait_all(w_ref.at[step], 0, tile, sems.at[step])
        @pl.loop(0, tile // 512)
        def _(part):
            columns = pl.ds(pl.multiple_of(part * 512, 512), 512)
            pre = dot(x_ref[...], w_ref[step, :, columns]) + bias_ref[:, columns]
            below = 0.5 + 0.5 * lax.erf(pre * (0.5**0.5))
            density = jnp.exp(pre * pre * -0.5) * 0.3989422804014327
            act_ref[:, columns] = (pre * below).astype(BF)
            slope_ref[:, columns] = below + pre * density

    block = pl.BlockSpec((count, tile), lambda n, ids: (0, n))
    return kernel(
        body,
        "ffn_in",
        13,
        ids,
        (wide // tile,),
        [(low, whole(low.shape)), (bias, pl.BlockSpec((1, tile), lambda n, ids: (0, n)))]
        + [(p, ANY) for p in weights.arrays],
        [(struct((count, wide), BF), block), (struct((count, wide), F32), block)],
        [
            pltpu.VMEM((wide // tile, width, tile), BF),
            pltpu.SemaphoreType.DMA((wide // tile, weights.count)),
        ],
    )


def ffn_out(ids, act, normed, out_grad, weights, vectors):
    count, wide = act.shape
    width = normed.shape[1]
    block = weights.block
    hops = weights.count // 2
    n_pieces = len(weights.arrays)
    step = 128

    def body(ids_ref, vec_ref, act_hbm, n_hbm, g_hbm, *refs):
        pieces = refs[:n_pieces]
        out_hbm, sum_hbm, low_hbm, sums_ref, sent_hbm = refs[n_pieces : n_pieces + 5]
        acc_ref, n_ref, g_ref, out_ref, low_ref = refs[n_pieces + 5 : n_pieces + 10]
        act_ref, w_ref, sent_ref, sems, in_sems, out_sems, sent_sems = refs[n_pieces + 10 :]
        places = [aligned((ids_ref[0] ^ j) * 2 * block, 2 * block) for j in range(hops)]
        fetch = copies([(act_hbm.at[:, p], act_ref.at[:, p]) for p in places], in_sems)
        for j in range(hops):
            fetch[j].start()
            weights.start(ids_ref, pieces, 0, w_ref, 0, width, sems, hop=j)
        late = [
            pltpu.make_async_copy(n_hbm, n_ref, in_sems.at[hops]),
            pltpu.make_async_copy(g_hbm, g_ref, in_sems.at[hops + 1]),
        ]
        start_all(late)
        for j in range(hops):
            fetch[j].wait()
            for c in range(2):
                weights.wait((ids_ref[0] ^ j) * 2 + c, w_ref, 0, width, sems)
            product = dot(act_ref[:, places[j]], w_ref[places[j], :])
            if j == 0:
                acc_ref[...] = product
            else:
                acc_ref[...] += product
        sums_ref[...] = jnp.zeros_like(sums_ref)
        wait_for(late)

        @pl.loop(0, count // step)
        def _(part):
            rows = pl.ds(pl.multiple_of(part * step, step), step)
            base = n_ref[rows, :] * vec_ref[3:4] + vec_ref[4:5] + vec_ref[5:6]
            n2, inverse = normalise(acc_ref[rows, :] + base)
            out_ref[rows, :] = (n2 * vec_ref[6:7] + vec_ref[7:8]).astype(BF)
            grad = g_ref[rows, :].astype(F32)
            back = normalise_back(grad * vec_ref[6:7], n2, inverse)
            low = back.astype(BF)
            acc_ref[rows, :] = back
            low_ref[rows, :] = low
            sums_ref[0:1, :] += total_rows(grad * n2)
            sums_ref[1:2, :] += total_rows(grad)
            sums_ref[2:3, :] += total_rows(low.astype(F32))

        done = copies([(low_ref, low_hbm), (acc_ref, sum_hbm), (out_ref, out_hbm)], out_sems)
        start_all(done)
        send = copies(
            [(sent_ref.at[j], sent_hbm.at[pl.ds(j * block, block), :]) for j in range(hops)],
            sent_sems,
        )
        for j in range(hops):
            at = ((ids_ref[0] ^ j) * 2 + (ids_ref[1] ^ 1)) * block
            sent_ref[j] = dot_tn(act_ref[:, aligned(at, block)], low_ref[...]).astype(BF)
            send[j].start()
        wait_for(done + send)

    size = (count, width)
    return kernel(
        body,
        "ffn_out",
        18,
        ids,
        (1,),
        [(vectors, whole(vectors.shape))]
        + [(a, ANY) for a in [act, normed, out_grad] + weights.arrays],
        [
            (struct(size, BF), ANY),
            (struct(size, F32), ANY),
            (struct(size, BF), ANY),
            (struct((8, width), F32), whole((8, width))),
            (struct((wide // 2, width), BF), ANY),
        ],
        [
            pltpu.VMEM(size, F32),
            pltpu.VMEM(size, F32),
            pltpu.VMEM(size, BF),
            pltpu.VMEM(size, BF),
            pltpu.VMEM(size, BF),
            pltpu.VMEM((count, wide), BF),
            pltpu.VMEM((wide, width), BF),
            pltpu.VMEM((hops, block, width), BF),
            pltpu.SemaphoreType.DMA((weights.count,)),
            pltpu.SemaphoreType.DMA((hops + 2,)),
            pltpu.SemaphoreType.DMA((3,)),
            pltpu.SemaphoreType.DMA((hops,)),
        ],
    )


def ffn_back(ids, grad, slope, weights, lefts, left_specs, deps):
    count, wide = slope.shape
    width = grad.shape[1]
    block = min(wide, 1024)
    per = block // weights.block
    n_pieces = len(weights.arrays)
    rows_out = sum(spec.block_shape[1] for spec in left_specs)

    def body(ids_ref, grad_ref, slope_ref, *refs):
        left_refs = refs[: len(lefts)]
        pieces = refs[len(lefts) : len(lefts) + n_pieces]
        out_ref, sums_ref, sent_ref, w_ref, sems = refs[-5:]
        step = pl.program_id(0)

        @pl.when(step == 0)
        def _():
            weights.start(ids_ref, pieces, 0, w_ref, 0, width, sems)

        for i in range(per):
            weights.wait(step * per + i, w_ref, 0, width, sems)
        rows = pl.ds(pl.multiple_of(step * block, 16), block)
        back = (dot_nt(grad_ref[...], w_ref[rows, :]) * slope_ref[...]).astype(BF)
        out_ref[...] = back
        sums_ref[...] = jnp.broadcast_to(total_rows(back.astype(F32)), sums_ref.shape)
        left = jnp.concatenate([ref[...] for ref in left_refs], axis=1)
        sent_ref[...] = dot_tn(left, out_ref[...]).astype(BF)

    tile = pl.BlockSpec((count, block), lambda n, ids: (0, n))
    return kernel(
        body,
        "ffn_back",
        12,
        ids,
        (wide // block,),
        [(grad, whole(grad.shape)), (slope, tile)]
        + list(zip(lefts, left_specs))
        + [(p, ANY) for p in weights.arrays]
        + [(d, ANY) for d in deps],
        [
            (struct((count, wide), BF), tile),
            (struct((8, wide), F32), pl.BlockSpec((8, block), lambda n, ids: (0, n))),
            (
                struct((rows_out, wide), BF),
                pl.BlockSpec((rows_out, block), lambda n, ids: (0, n)),
            ),
        ],
        [pltpu.VMEM((wide, width), BF), pltpu.SemaphoreType.DMA((weights.count,))],
    )


def attention_norm_back(ids, inner_grad, ffn_grad, normed, inverse, inner, weights, vectors, deps):
    count, wide = inner_grad.shape
    width = normed.shape[1]
    tile = min(wide, 1024)
    steps = wide // tile
    n_pieces = len(weights.arrays)
    part_rows = 128

    def body(ids_ref, inverse_ref, vec_ref, grad_hbm, ffn_hbm, n_hbm, *refs):
        pieces = refs[:n_pieces]
        inner_pieces = refs[n_pieces : 2 * n_pieces]
        low_hbm, sum_hbm, mixed_hbm, sums_ref = refs[-17:-13]
        acc_ref, ffn_ref, n_ref, low_ref, mixed_ref, grad_ref, w_ref = refs[-13:-6]
        w_sems, o_ref, o_sems, sems, grad_sems, out_sems = refs[-6:]
        tiles = [slice(g * tile, (g + 1) * tile) for g in range(steps)]
        fetch = copies([(grad_hbm.at[:, t], grad_ref.at[:, t]) for t in tiles], grad_sems)
        for g in range(steps):
            fetch[g].start()
            inner.start(ids_ref, inner_pieces, g * tile, w_ref.at[g], 0, tile, w_sems.at[g])
        late = copies([(ffn_hbm, ffn_ref), (n_hbm, n_ref)], sems)
        start_all(late)
        weights.start(ids_ref, pieces, 3 * width, o_ref, 0, width, o_sems)
        acc_ref[...] = jnp.zeros_like(acc_ref)

        @pl.loop(0, steps)
        def _(g):
            there = grad_ref.at[:, aligned(g * tile, tile)]
            pltpu.make_async_copy(there, there, grad_sems.at[g]).wait()
            inner.wait_all(w_ref.at[g], 0, tile, w_sems.at[g])
            acc_ref[...] += dot_nt(there[...], w_ref[g])

        wait_for(late)
        sums_ref[...] = jnp.zeros_like(sums_ref)

        @pl.loop(0, count // part_rows)
        def _(part):
            rows = pl.ds(pl.multiple_of(part * part_rows, part_rows), part_rows)
            grad = acc_ref[rows, :] + ffn_ref[rows, :]
            normed_rows = n_ref[rows, :]
            back = normalise_back(grad * vec_ref[3:4], normed_rows, inverse_ref[rows, 0:1])
            low = back.astype(BF)
            low_ref[rows, :] = low
            acc_ref[rows, :] = back
            sums_ref[0:1, :] += total_rows(grad * normed_rows)
            sums_ref[1:2, :] += total_rows(grad)
            sums_ref[2:3, :] += total_rows(low.astype(F32))

        done = copies(
            [(low_ref, low_hbm), (acc_ref, sum_hbm), (mixed_ref, mixed_hbm)], out_sems
        )
        start_all(done[:2])
        weights.wait_all(o_ref, 0, width, o_sems)
        mixed_ref[...] = dot_nt(low_ref[...], o_ref[...]).astype(BF)
        done[2].start()
        wait_for(done)

    size = (count, width)
    return kernel(
        body,
        "attention_norm_back",
        16,
        ids,
        (1,),
        [(inverse, whole(inverse.shape)), (vectors, whole(vectors.shape))]
        + [
            (a, ANY)
            for a in [inner_grad, ffn_grad, normed] + weights.arrays + inner.arrays + list(deps)
        ],
        [
            (struct(size, BF), ANY),
            (struct(size, F32), ANY),
            (struct(size, BF), ANY),
            (struct((8, width), F32), whole((8, width))),
        ],
        [
            pltpu.VMEM(size, F32),
            pltpu.VMEM(size, F32),
            pltpu.VMEM(size, F32),
            pltpu.VMEM(size, BF),
            pltpu.VMEM(size, BF),
            pltpu.VMEM((count, wide), BF),
            pltpu.VMEM((steps, width, tile), BF),
            pltpu.SemaphoreType.DMA((steps, inner.count)),
            pltpu.VMEM((width, width), BF),
            pltpu.SemaphoreType.DMA((weights.count,)),
            pltpu.SemaphoreType.DMA((2,)),
            pltpu.SemaphoreType.DMA((steps,)),
            pltpu.SemaphoreType.DMA((3,)),
        ],
    )


def inputs_back(ids, base, grads, weights, deps):
    count, width = base.shape
    tile = 256
    per = tile // weights.block
    n_pieces = len(weights.arrays)

    def body(ids_ref, base_ref, q_ref, k_ref, v_ref, *refs):
        pieces = refs[:n_pieces]
        out_ref, w_ref, sems = refs[-3:]
        step = pl.program_id(0)

        @pl.when(step == 0)
        def _():
            weights.start(ids_ref, pieces, 0, w_ref, 0, 3 * width, sems)

        for i in range(per):
            weights.wait(step * per + i, w_ref, 0, 3 * width, sems)
        place = pl.ds(pl.multiple_of(step * tile, tile), tile)
        out = base_ref[...]
        for i, ref in enumerate((q_ref, k_ref, v_ref)):
            out = out + dot_nt(ref[...], w_ref[place, i * width : (i + 1) * width])
        out_ref[...] = out

    block = pl.BlockSpec((count, tile), lambda n, ids: (0, n))
    return kernel(
        body,
        "inputs_back",
        10,
        ids,
        (width // tile,),
        [(base, block)]
        + [(g, whole(g.shape)) for g in grads]
        + [(p, ANY) for p in weights.arrays]
        + [(d, ANY) for d in deps],
        [(struct(base.shape, F32), block)],
        [pltpu.VMEM((width, 3 * width), BF), pltpu.SemaphoreType.DMA((weights.count,))],
    )[0]


def split_hops(kept, bit):
    stay = [j for j in kept if not j & bit]
    return stay, [j | bit for j in stay]


class RowSum:
    def __init__(self, net, pairs, ids, tile):
        self.net, self.ids, self.tile = net, ids, tile
        self.rights = [right for _, right in pairs]
        self.left = []
        for left, _ in pairs:
            if not any(left is known for known in self.left):
                self.left.append(left)
        self.uses = [[left is known for known in self.left].index(True) for left, _ in pairs]
        self.width = self.left[0].shape[1] // (net.chips * 2)
        self.columns = sum(r.shape[1] for r in self.rights)
        bits = [1 << b for b in range(net.chips.bit_length() - 1)]
        self.bits = (bits, bits[::-1])
        self.kept = [list(range(net.chips))] * 2

    def lefts(self, core):
        net, width = self.net, self.width
        if width % 128 == 0:
            spec = [
                pl.BlockSpec(
                    (self.left[0].shape[0], width),
                    lambda n, ids, j=j: (0, (ids[0] ^ j) * 2 + (ids[1] ^ core)),
                )
                for j in range(net.chips)
            ]
            return [left for left in self.left for _ in spec], spec * len(self.left)
        chosen = []
        for left in self.left:
            picked = []
            for j in range(net.chips):
                at = ((self.ids[0] ^ j) * 2 + (self.ids[1] ^ core)) * width
                picked.append(lax.dynamic_slice_in_dim(left, at, width, axis=1))
            chosen.append(jnp.concatenate(picked, axis=1))
        return chosen, [whole(picked.shape) for picked in chosen]

    def multiply(self, name, micros, core, got, outs, groups, targets, deps):
        net, width, tile = self.net, self.width, self.tile
        rows, tokens = net.chips * width, self.left[0].shape[0]
        ready = width % 128 != 0
        lefts = self.lefts(core)[0] if ready else self.left
        tiles = []
        for right, use in zip(range(len(self.rights)), self.uses):
            for at in range(0, self.rights[right].shape[1], tile):
                tiles.append((right, at, use))
        extra = [] if got is None else [got]
        cuts = [t for t in range(1, len(tiles)) if tiles[t][2] != tiles[t - 1][2]]

        def body(ids_ref, *refs):
            left_hbm = refs[: len(lefts)]
            right_hbm = refs[len(lefts) : len(lefts) + len(self.rights)]
            got_hbm = refs[len(lefts) + len(self.rights)]
            scratch = refs[len(refs) - 7 - len(extra) :]
            out_hbm = refs[len(refs) - 7 - len(extra) - len(outs) : len(refs) - 7 - len(extra)]
            left_ref, right_ref, out_ref, left_sems, right_sems, got_sems, out_sems = scratch[:7]
            fetch_left = []
            for i, source in enumerate(left_hbm):
                if ready:
                    pairs = [(source, left_ref.at[i])]
                else:
                    pairs = []
                    for j in range(net.chips):
                        at = ((ids_ref[0] ^ j) * 2 + (ids_ref[1] ^ core)) * width
                        place = (slice(None), slice(j * width, (j + 1) * width))
                        pairs.append((source.at[:, aligned(at, width)], left_ref.at[i].at[place]))
                fetch_left.append(copies(pairs, left_sems, i))
            fetch_right = [
                pltpu.make_async_copy(
                    right_hbm[r].at[:, at : at + tile], right_ref.at[t], right_sems.at[t]
                )
                for t, (r, at, _) in enumerate(tiles)
            ]
            fetch_got = [
                pltpu.make_async_copy(
                    got_hbm.at[:, t * tile : (t + 1) * tile], scratch[7].at[t], got_sems.at[t]
                )
                for t in range(len(tiles) if extra else 0)
            ]
            waited = set()
            for t, (_, _, use) in enumerate(tiles):
                if use not in waited:
                    start_all(fetch_left[use])
                    waited.add(use)
                fetch_right[t].start()
                if extra:
                    fetch_got[t].start()
            def part(t, which):
                use = sum(((t >= cut).astype(jnp.int32) for cut in cuts), jnp.int32(0))
                there = [right_ref.at[t]] + [ref.at[t] for ref in scratch[7:]]
                for ref, sems in zip(there, (right_sems, got_sems)):
                    pltpu.make_async_copy(ref, ref, sems.at[t]).wait()
                value = dot_tn(left_ref[use], right_ref[t])
                for ref in there[1:]:
                    value = value + ref[...].astype(F32)
                out_ref[t] = value.astype(BF)
                return copies(
                    [
                        (
                            out_ref.at[t].at[first : first + n, :],
                            out_hbm[kind].at[row : row + n, aligned(column, tile)],
                        )
                        for first, n, kind, row, column in targets(t, which)
                    ],
                    out_sems,
                    t,
                )

            count = len(tiles)
            group = count // groups
            waited = 0
            for which in range(groups):
                last = tiles[(which + 1) * group - 1][2]
                while waited <= last:
                    wait_for(fetch_left[waited])
                    waited += 1

                @pl.loop(which * group, (which + 1) * group)
                def _(t):
                    start_all(part(t, which))

            for t in range(count):
                wait_for(
                    pltpu.make_async_copy(
                        out_ref.at[t].at[first : first + n, :],
                        out_ref.at[t].at[first : first + n, :],
                        out_sems.at[t, i],
                    )
                    for i, (first, n, _, _, _) in enumerate(targets(t, t // group))
                )

        count = len(tiles)
        return kernel(
            body,
            name,
            micros,
            self.ids,
            (1,),
            [(a, ANY) for a in list(lefts) + self.rights + extra + list(deps)],
            [(o, ANY) for o in outs],
            [
                pltpu.VMEM((len(lefts), tokens, rows), BF),
                pltpu.VMEM((count, tokens, tile), BF),
                pltpu.VMEM((count, rows, tile), BF),
                pltpu.SemaphoreType.DMA((len(lefts), net.chips)),
                pltpu.SemaphoreType.DMA((count,)),
                pltpu.SemaphoreType.DMA((count,)),
                pltpu.SemaphoreType.DMA((count, net.chips)),
            ]
            + [pltpu.VMEM((count, rows, tile), BF) for _ in extra],
        )

    def other_core(self, *deps):
        rows = self.net.chips * self.width
        (self.sent,) = self.multiply(
            "rows_of_other_core",
            7,
            1,
            None,
            [struct((rows, self.columns), BF)],
            1,
            lambda t, _: [(0, rows, 0, 0, t * self.tile)],
            deps,
        )
        return self.exchange(self.sent)

    def exchange(self, sent):
        self.got = self.net.across_core(sent)
        return sent

    def own_core(self, *deps):
        rows, tile, width = self.net.chips * self.width, self.tile, self.width
        half = self.columns // tile // 2
        sides = [split_hops(self.kept[s], self.bits[s][0]) for s in range(2)]

        def targets(t, side):
            return [
                (j * width, width, side * 2 + which, i * width, (t - side * half) * tile)
                for which, hops in enumerate(sides[side])
                for i, j in enumerate(hops)
            ]

        out = self.multiply(
            "rows_of_own_core",
            9,
            0,
            self.got,
            [struct((rows // 2, self.columns // 2), BF)] * 4,
            2,
            targets,
            deps,
        )
        self.held = [out[0], out[2]]
        self.away = [out[1], out[3]]
        self.send()
        return out[0]

    def send(self):
        for s in range(2):
            self.kept[s] = split_hops(self.kept[s], self.bits[s][0])[0]
        self.arrived = [self.net.across_chip(self.away[s], self.bits[s][0]) for s in range(2)]
        self.bits = (self.bits[0][1:], self.bits[1][1:])

    def fold(self, *deps):
        rows, columns = self.held[0].shape
        tile = columns // 2
        sides = [split_hops(self.kept[s], self.bits[s][0]) for s in range(2)]

        def body(ids_ref, *refs):
            out_refs = refs[-4:]
            for s in range(2):
                for which, hops in enumerate(sides[s]):
                    for i, j in enumerate(hops):
                        at = self.kept[s].index(j) * self.width
                        part = slice(at, at + self.width)
                        value = refs[2 * s][part, :].astype(F32) + refs[2 * s + 1][part, :].astype(F32)
                        out_refs[2 * s + which][i * self.width : (i + 1) * self.width, :] = (
                            value.astype(BF)
                        )

        block = pl.BlockSpec((rows, tile), lambda n, ids: (0, n))
        half = pl.BlockSpec((rows // 2, tile), lambda n, ids: (0, n))
        out = kernel(
            body,
            "fold",
            4,
            self.ids,
            (columns // tile,),
            [(a, block) for s in range(2) for a in (self.held[s], self.arrived[s])]
            + [(d, ANY) for d in deps],
            [(struct((rows // 2, columns), BF), half)] * 4,
            [],
        )
        self.held = [out[0], out[2]]
        self.away = [out[1], out[3]]
        self.send()
        return self.fold() if self.bits[0] else out[0]

    def fold_z(self, *deps):
        net, count = self.net, self.net.inner
        columns = self.held[0].shape[1]
        rows = self.width // count
        stay, leave = split_hops(list(range(count)), 1)
        size = (rows * len(stay), 2 * columns)
        if rows % 16:
            held = tie(jnp.concatenate(self.held, axis=1), *deps).astype(F32)
            held = held + jnp.concatenate(self.arrived, axis=1).astype(F32)
            held = held.reshape(count, rows, -1).astype(BF)
            keep, away = (
                jnp.take(held, jnp.array(hops) ^ self.ids[2], axis=0).reshape(size)
                for hops in (stay, leave)
            )
        else:

            def body(ids_ref, *refs):
                for out_ref, hops in zip(refs[-2:], (stay, leave)):
                    for i, s in enumerate(hops):
                        at = pl.ds(pl.multiple_of((ids_ref[2] ^ s) * rows, 16), rows)
                        for side in range(2):
                            value = refs[2 * side][at, :].astype(F32)
                            value = value + refs[2 * side + 1][at, :].astype(F32)
                            place = slice(side * columns, (side + 1) * columns)
                            out_ref[i * rows : (i + 1) * rows, place] = value.astype(BF)

            keep, away = kernel(
                body,
                "fold_z",
                3,
                self.ids,
                (1,),
                [
                    (a, whole(a.shape))
                    for s in range(2)
                    for a in (self.held[s], self.arrived[s])
                ]
                + [(d, ANY) for d in deps],
                [(struct(size, BF), whole(size))] * 2,
                [],
            )
        self.total, self.came, self.reach = keep, net.swap(away, 1), 1
        return keep

    def fold_direct(self, *deps):
        net, count = self.net, self.net.inner
        columns = self.held[0].shape[1]
        rows = self.width // count
        self.parts = None
        if rows % 16 or count > 4:
            self.fold_z(*deps)
            return self.fold_far()

        def body(ids_ref, *refs):
            for s in range(count):
                at = pl.ds(pl.multiple_of((ids_ref[2] ^ s) * rows, 16), rows)
                out_ref = refs[s - count]
                for side in range(2):
                    value = refs[2 * side][at, :].astype(F32)
                    value = value + refs[2 * side + 1][at, :].astype(F32)
                    place = slice(side * columns, (side + 1) * columns)
                    out_ref[:, place] = value.astype(out_ref.dtype)

        size = (rows, 2 * columns)
        parts = kernel(
            body,
            "fold_direct",
            3,
            self.ids,
            (1,),
            [(a, whole(a.shape)) for s in range(2) for a in (self.held[s], self.arrived[s])]
            + [(d, ANY) for d in deps],
            [(struct(size, F32), whole(size))] + [(struct(size, BF), whole(size))] * (count - 1),
            [],
        )
        self.parts = [parts[0]] + [net.swap(parts[s], s) for s in range(1, count)]
        return parts[0]

    def finish_direct(self):
        if self.parts is None:
            return self.finish()
        total = self.parts[0]
        for part in self.parts[1:]:
            total = total + part.astype(F32)
        return total

    def fold_far(self, *deps):
        while self.reach * 2 < self.net.inner:
            self.reach *= 2
            total = tie(self.total, *deps).astype(F32) + self.came.astype(F32)
            rows = self.width // self.net.inner
            count = total.shape[0] // rows
            stay = [i for i in range(count) if not i & 1]
            blocks = total.reshape(count, rows, -1)
            away = jnp.concatenate([blocks[i + 1] for i in stay], axis=0).astype(BF)
            self.total = jnp.concatenate([blocks[i] for i in stay], axis=0)
            self.came = self.net.swap(away, self.reach)
        return self.came

    def finish(self, *deps):
        return tie(self.total, *deps).astype(F32) + self.came.astype(F32)


class ZFirst:
    def __init__(self, rows_sum):
        self.sum, self.net = rows_sum, rows_sum.net
        self.low = rows_sum.width // self.net.inner
        self.usual = self.net.inner != 4 or len(rows_sum.bits[0]) != 1 or self.low % 16 != 0

    def cross_near(self, *deps):
        source, low = self.sum, self.low
        if self.usual:
            source.fold(*deps)
            return source.fold_z()
        columns = source.held[0].shape[1]
        split = split_hops(list(range(4)), 1)
        sides = [split_hops(source.kept[s], source.bits[s][0]) for s in range(2)]
        size = (4 * low, 2 * columns)

        def body(ids_ref, *refs):
            for out_ref, zs in zip(refs[-2:], split):
                for i, z in enumerate(zs):
                    for s in range(2):
                        for h in range(2):
                            at = source.kept[s].index(sides[s][h][0]) * source.width
                            at = pl.multiple_of(at + (ids_ref[2] ^ z) * low, 16)
                            value = refs[2 * s][pl.ds(at, low), :].astype(F32)
                            value = value + refs[2 * s + 1][pl.ds(at, low), :].astype(F32)
                            row = (2 * i + h) * low
                            out_ref[row : row + low, s * columns : (s + 1) * columns] = (
                                value.astype(BF)
                            )

        self.keep, away = kernel(
            body,
            "cross_near",
            6,
            source.ids,
            (1,),
            [
                (a, whole(a.shape))
                for s in range(2)
                for a in (source.held[s], source.arrived[s])
            ]
            + [(d, ANY) for d in deps],
            [(struct(size, BF), whole(size))] * 2,
            [],
        )
        self.came = self.net.swap(away, 1)
        return self.keep

    def halve(self, *deps):
        total = tie(self.keep, *deps).astype(F32) + self.came.astype(F32)
        half = total.shape[0] // 2
        self.keep = total[:half].astype(BF)
        return total[half:].astype(BF)

    def cross_far(self, *deps):
        if self.usual:
            return self.sum.fold_far(*deps)
        self.came = self.net.swap(self.halve(*deps), 2)
        return self.came

    def cross_chip(self, *deps):
        if self.usual:
            return None
        away = self.halve(*deps)
        half = away.shape[1] // 2
        parts = [
            self.net.across_chip(away[:, s * half : (s + 1) * half], self.sum.bits[s][0])
            for s in range(2)
        ]
        self.came = jnp.concatenate(parts, axis=1)
        return None

    def finish(self, *deps):
        if self.usual:
            return self.sum.finish(*deps)
        return tie(self.keep, *deps).astype(F32) + self.came.astype(F32)


def shards(
    net,
    inputs,
    segment_ids,
    query_weight,
    key_weight,
    value_weight,
    output_weight,
    query_bias,
    value_bias,
    output_bias,
    attn_gain,
    attn_shift,
    inner_weight,
    inner_bias,
    outer_weight,
    outer_bias,
    ffn_gain,
    ffn_shift,
    out_grad,
):
    row_count, seq_len, width = inputs.shape
    tokens = inputs.reshape(row_count * seq_len, width)
    _, ids = net.place()
    small = [
        query_bias,
        value_bias,
        output_bias,
        attn_gain,
        attn_shift,
        outer_bias,
        ffn_gain,
        ffn_shift,
        inner_bias,
    ]
    mine = query_bias.shape[0]
    shard = first_shard([query_weight, key_weight, value_weight, output_weight], small)
    gather_a = Gather(net, shard, ids, True)
    gather_a.ordered()
    gather_a.plane()
    gather_b = Gather(net, tie(inner_weight, gather_a.block), ids, True)
    gather_a.relay(*gather_b.along)
    gather_b.ordered()
    weights_a = gather_a.cores()
    gather_b.plane(*weights_a.arrays)
    queries, keys, values, vectors = project(ids, tokens, weights_a)
    spread = inner_bias.shape[0] // mine
    inner_bias_full = vectors[8 : 8 + spread].reshape(spread, net.count, mine)
    inner_bias_full = inner_bias_full.swapaxes(0, 1).reshape(1, -1)
    mixed, totals = attend_forward(segment_ids, queries, keys, values)
    gather_c = Gather(net, tie(outer_weight, queries), ids, True, mixed)
    arrived = gather_b.relay(mixed)
    normed, inverse, normed_low = close_attention(ids, mixed, tokens, weights_a, vectors)
    gather_c.ordered(normed_low)
    gather_c.plane(*arrived)
    weights_b = gather_b.cores()
    act, slope = ffn_in(ids, normed_low, weights_b, inner_bias_full)
    gather_c.relay(act)
    weights_c = gather_c.cores()
    grad_out = out_grad.reshape(tokens.shape)
    outputs, ffn_grad, branch_grad, ffn_sums, sent = ffn_out(
        ids, act, normed, grad_out, weights_c, vectors
    )
    outer_sum = RowSum(net, [(act, branch_grad)], ids, 256)
    last = outer_sum.exchange(sent)
    lefts = RowSum(net, [(normed_low, slope)], ids, 1024).lefts(1)
    inner_grad, inner_sums, sent = ffn_back(ids, branch_grad, slope, weights_c, *lefts, [last])
    inner_sum = RowSum(net, [(normed_low, inner_grad)], ids, 1024)
    last = inner_sum.exchange(sent)
    last = outer_sum.own_core(last)
    attn_grad, attn_sum_grad, mixed_grad, attn_sums = attention_norm_back(
        ids, inner_grad, ffn_grad, normed, inverse, weights_b, weights_a, vectors, [last]
    )
    last = inner_sum.own_core(attn_grad)
    query_grad, key_grad, value_grad, grad_query_bias, grad_value_bias = attend_backward(
        segment_ids, queries, keys, values, mixed_grad, totals, [last, *outer_sum.arrived]
    )
    inputs_sum = RowSum(
        net,
        [(mixed, attn_grad)] + [(tokens, g) for g in (query_grad, key_grad, value_grad)],
        ids,
        1024,
    )
    outer = ZFirst(outer_sum)
    last = outer.cross_near(query_grad)
    last = inputs_sum.other_core(last, *inner_sum.arrived)
    last = inner_sum.fold(last)
    last = inputs_sum.own_core(last)
    last = inner_sum.fold_z(last)
    outer.cross_far(last)
    last = inputs_sum.fold(last)
    inner_sum.fold_far(last)
    input_grad = inputs_back(
        ids, attn_sum_grad, (query_grad, key_grad, value_grad), weights_a, [last]
    )
    last = inputs_sum.fold_direct(input_grad)
    outer.cross_chip(last)
    shard_inner = inner_sum.finish(last)
    shard_outer = outer.finish(last)
    shard_inputs = inputs_sum.finish_direct()
    shard_output, shard_query, shard_key, shard_value = (
        shard_inputs[:, i * width : (i + 1) * width] for i in range(4)
    )
    rows = jnp.concatenate(
        [grad_query_bias[None], grad_value_bias[None], attn_sums[:3], ffn_sums[:3]], axis=0
    )
    rows = rows.reshape(8, net.count, mine).swapaxes(0, 1).reshape(net.count, 8 * mine)
    packed = jnp.concatenate([rows, inner_sums[0].reshape(net.count, -1)], axis=1)
    packed = tie(packed, inputs_sum.parts[1] if inputs_sum.parts else last)
    summed = jnp.sum(lax.all_to_all(packed, AXES, 0, 0, tiled=True), axis=0)
    vector = [summed[i * mine : (i + 1) * mine] for i in range(8)]
    return (
        outputs.reshape(inputs.shape),
        input_grad.reshape(inputs.shape),
        shard_query,
        shard_key,
        shard_value,
        shard_output,
        vector[0],
        vector[1],
        vector[4],
        vector[2],
        vector[3],
        shard_inner,
        summed[8 * mine :],
        shard_outer,
        vector[7],
        vector[5],
        vector[6],
    )


def solution(mesh):
    placed = (
        P(("dp", "fsdp"), None, None),
        P(("dp", "fsdp"), None),
        P(("dp", "fsdp"), None),
        P(("dp", "fsdp"), None),
        P(("dp", "fsdp"), None),
        P(("dp", "fsdp"), None),
        P(("dp", "fsdp")),
        P(("dp", "fsdp")),
        P(("dp", "fsdp")),
        P(("dp", "fsdp")),
        P(("dp", "fsdp")),
        P(("dp", "fsdp"), None),
        P(("dp", "fsdp")),
        P(("dp", "fsdp"), None),
        P(("dp", "fsdp")),
        P(("dp", "fsdp")),
        P(("dp", "fsdp")),
        P(("dp", "fsdp"), None, None),
    )
    return jax.shard_map(
        functools.partial(shards, Slice(mesh.shape["dp"], mesh.shape["fsdp"])),
        mesh=mesh,
        in_specs=placed,
        out_specs=(
            P(("dp", "fsdp"), None, None),
            P(("dp", "fsdp"), None, None),
            P(("dp", "fsdp"), None),
            P(("dp", "fsdp"), None),
            P(("dp", "fsdp"), None),
            P(("dp", "fsdp"), None),
            P(("dp", "fsdp")),
            P(("dp", "fsdp")),
            P(("dp", "fsdp")),
            P(("dp", "fsdp")),
            P(("dp", "fsdp")),
            P(("dp", "fsdp"), None),
            P(("dp", "fsdp")),
            P(("dp", "fsdp"), None),
            P(("dp", "fsdp")),
            P(("dp", "fsdp")),
            P(("dp", "fsdp")),
        ),
        check_vma=False,
    )
```
